32 devices in a mesh: cfg: 2 (over x), ctx: 8 (over z, y), tp: 2 (over core).
Axes of the slice: x: 2, y: 2, z: 4, core: 2. Of those that a mesh axis runs over, the one named last changes fastest.
Arguments:
- query_proj: bfloat16 [2, 2048, 3072], P('cfg', 'ctx', 'tp'), may hold values from -8 to 8
- key_proj: bfloat16 [2, 2048, 3072], P('cfg', 'ctx', 'tp'), may hold values from -8 to 8
- value_proj: bfloat16 [2, 2048, 3072], P('cfg', 'ctx', 'tp'), may hold values from -6 to 6
- query_gain: float32 [128], replicated, may hold values from 1 to 8
- key_gain: float32 [128], replicated, may hold values from 1 to 8
- block_input: bfloat16 [2, 2048, 3072], P('cfg', ('ctx', 'tp')), may hold values from -120 to 120
- cached_out: bfloat16 [2, 2048, 3072], P('cfg', ('ctx', 'tp')), may hold values from -120 to 120
- replay_mask: int32 [2, 2048], P('cfg', 'ctx'), may hold values from 0 to 1, as said below
- branch_gate: float32 [2, 3072], P('cfg'), may hold values from 1 to 4
- attn_weight: bfloat16 [3072, 3072], P('tp'), may hold values from -0.109375 to 0.109375
- final_shift: float32 [2, 3072], P('cfg'), may hold values from -4 to 4
- final_scale: float32 [2, 3072], P('cfg'), may hold values from -2 to 2
- patch_weight: bfloat16 [3072, 64], replicated, may hold values from -0.109375 to 0.109375
Outputs:
- block_out: bfloat16 [2, 2048, 3072], P('cfg', ('ctx', 'tp'))
- velocity: float32 [2048, 64], P(('ctx', 'tp'), 'cfg')
The draws below stay inside these ranges and needn't reach their ends.
Inputs may be any that keep to these rules, and one draw needn't show every extreme that they name: `replay_mask`: in each branch, at most 128 of the 256 rows of one index of ctx have a 0, and some index of ctx has exactly 128.
All inputs are finite; a program needn't handle non-finite values.
Results may differ from the reference program's by a relative error of at most 0.0097.
Values may be sent and summed in bfloat16 or wider, within the bound.
No kernel may reach another device: no remote copies, remote signals or barrier semaphores. Data moves between devices by JAX's collectives and lax.ppermute only.
A program may use at most 128 MiB of HBM per device.

```python
import math
import jax
import jax.numpy as jnp
from jax import lax

D = 3072
HEADS = 24
HD = 128
C = 64
TOK_DEV = 256
LIVE = 128
TOKENS = 2048


def activation_draw(key, salt):
    inner = jax.random.fold_in(key, salt)
    first, second = jax.random.split(inner, 2)
    base = jnp.clip(jax.random.normal(first, (2, TOKENS, D), jnp.float32), -6.0, 6.0)
    row_scale = jnp.exp(jax.random.uniform(second, (2, TOKENS, 1), jnp.float32, math.log(0.5), math.log(2.0)))
    return base * row_scale


def draw_block_input(key, part):
    return activation_draw(key, 101).astype(jnp.bfloat16)


def draw_cached_out(key, part):
    return activation_draw(key, 202).astype(jnp.bfloat16)


def pair_draw(key):
    inner = jax.random.fold_in(key, 303)
    parts = jax.random.split(inner, 2)
    width = HEADS * HD
    queries = jnp.clip(jax.random.normal(parts[0], (2, TOKENS, width), jnp.float32), -6.0, 6.0)
    keys_drawn = jnp.clip(jax.random.normal(parts[1], (2, TOKENS, width), jnp.float32), -6.0, 6.0)
    return (queries, keys_drawn)


def draw_query_proj(key, part):
    return pair_draw(key)[0].astype(jnp.bfloat16)


def draw_key_proj(key, part):
    return pair_draw(key)[1].astype(jnp.bfloat16)


def gain_draw(key, salt):
    inner = jax.random.fold_in(key, salt)
    return jnp.exp(jax.random.uniform(inner, (HD,), jnp.float32, 0.0, math.log(2.5)))


def draw_query_gain(key, part):
    return gain_draw(key, 404)


def draw_key_gain(key, part):
    return gain_draw(key, 505)


def draw_replay_mask(key, part):
    inner = jax.random.fold_in(key, 606)
    first, second, third = jax.random.split(inner, 3)
    blocks = TOKENS // TOK_DEV
    counts = jax.random.randint(first, (2, blocks), max(LIVE // 8, 1), LIVE // 2 + 1)
    fullest = jax.random.randint(second, (2,), 0, blocks)
    counts = jnp.where(jnp.arange(blocks)[None, :] == fullest[:, None], LIVE, counts)
    streams = jax.random.split(third, 2 * blocks)
    ranks = jax.vmap(lambda stream: jax.random.permutation(stream, TOK_DEV))(streams).reshape(2, blocks, TOK_DEV)
    marked = jnp.where(ranks < counts[:, :, None], 0, 1)
    return marked.reshape(2, TOKENS).astype(jnp.int32)


def shard_levels(stream_key, shape, shards, least, largest):
    factor_of = 1.0
    for position, blocks in shards:
        heights = jax.random.uniform(jax.random.fold_in(jax.random.fold_in(stream_key, 6), position), (blocks,), jnp.float32, least / len(shards), largest / len(shards))
        factor_of = factor_of * jnp.repeat(jnp.exp(heights), shape[position] // blocks).reshape((-1,) + (1,) * (len(shape) - 1 - position))
    return factor_of


def noise(rng, dims, deviation, reach, cuts=(), dtype=jnp.bfloat16):
    drawn = jax.random.normal(rng, dims, jnp.float32) * deviation
    if len(cuts) > 0:
        drawn = shard_levels(rng, dims, cuts, -0.22, 0.18) * drawn
    return jnp.clip(drawn, min=-reach, max=reach).astype(dtype)


def setup_inputs(seed: int = 0) -> dict:
    streams_of = jax.random.split(jax.random.key(seed), 14)
    query_proj = draw_query_proj(jax.random.fold_in(streams_of[13], 71), 0)
    key_proj = draw_key_proj(jax.random.fold_in(streams_of[13], 71), 0)
    value_proj = noise(streams_of[2], (2, TOKENS, HEADS * HD), 1.0, 6.0, ((0, 2), (1, 8), (2, 2)))
    query_gain = draw_query_gain(jax.random.fold_in(streams_of[13], 71), 0)
    key_gain = draw_key_gain(jax.random.fold_in(streams_of[13], 71), 0)
    block_input = draw_block_input(jax.random.fold_in(streams_of[13], 71), 0)
    cached_out = draw_cached_out(jax.random.fold_in(streams_of[13], 71), 0)
    replay_mask = draw_replay_mask(jax.random.fold_in(streams_of[13], 71), 0)
    branch_gate = jnp.clip(jnp.exp(math.log(4.0) - 1.3862944 * jax.random.uniform(streams_of[8], (2, D), jnp.float32) ** shard_levels(streams_of[8], (2, D), ((0, 2),), -0.2, 0.2)), 1.0, 4.0)
    attn_weight = noise(streams_of[9], (HEADS * HD, D), (HEADS * HD) ** -0.5, 0.109375, ((0, 2),))
    final_shift = noise(streams_of[10], (2, D), 1.0, 4.0, ((0, 2),), jnp.float32)
    final_scale = noise(streams_of[11], (2, D), 0.5, 2.0, ((0, 2),), jnp.float32)
    patch_weight = noise(streams_of[12], (D, C), D ** -0.5, 0.109375)
    return {"query_proj": query_proj, "key_proj": key_proj, "value_proj": value_proj, "query_gain": query_gain, "key_gain": key_gain, "block_input": block_input, "cached_out": cached_out, "replay_mask": replay_mask, "branch_gate": branch_gate, "attn_weight": attn_weight, "final_shift": final_shift, "final_scale": final_scale, "patch_weight": patch_weight}


def norm_heads(values, gain):
    lifted = values.astype(jnp.float32).reshape(values.shape[:-1] + (HEADS, HD))
    mean_square = lax.optimization_barrier(jnp.mean(lifted * lifted, axis=-1, keepdims=True))
    scaled = lifted * lax.rsqrt(mean_square + 1e-06) * gain
    return scaled.reshape(values.shape).astype(jnp.bfloat16)

def split_heads(values):
    return values.reshape(2, TOKENS, HEADS, HD).transpose(0, 2, 1, 3).reshape(2 * HEADS, TOKENS, HD)

def attend(queries, keys_normed, values_in):
    block = 1024 if TOKENS % 1024 == 0 else TOKENS
    scale = HD ** (-0.5)

    def one_head(triple):
        query_head, key_head, value_head = triple
        blocks = query_head.reshape(TOKENS // block, block, HD)

        def one_block(query_block):
            scores = jnp.dot(query_block, key_head.T, preferred_element_type=jnp.float32) * scale
            biggest = lax.optimization_barrier(jnp.max(scores, axis=-1, keepdims=True))
            weights = jnp.exp(scores - biggest)
            totals = lax.optimization_barrier(jnp.sum(weights, axis=-1, keepdims=True))
            summed = jnp.dot(weights.astype(jnp.bfloat16), value_head, preferred_element_type=jnp.float32)
            return (summed / totals).astype(jnp.bfloat16)
        return lax.map(one_block, blocks).reshape(TOKENS, HD)
    result = lax.map(one_head, (split_heads(queries), split_heads(keys_normed), split_heads(values_in)))
    return result.reshape(2, HEADS, TOKENS, HD).transpose(0, 2, 1, 3).reshape(2, TOKENS, HEADS * HD)

def reference(query_proj, key_proj, value_proj, query_gain, key_gain, block_input, cached_out, replay_mask, branch_gate, attn_weight, final_shift, final_scale, patch_weight):
    queries = norm_heads(query_proj, query_gain)
    keys_normed = norm_heads(key_proj, key_gain)
    attended = attend(queries, keys_normed, value_proj)
    outputs = []
    results = []
    for branch in range(2):
        projected = jnp.dot(attended[branch], attn_weight, preferred_element_type=jnp.float32)
        mixed = block_input[branch].astype(jnp.float32) + branch_gate[branch][None, :] * projected
        chosen = jnp.where(replay_mask[branch][:, None] == 1, cached_out[branch].astype(jnp.float32), mixed)
        block_out = chosen.astype(jnp.bfloat16)
        outputs.append(block_out)
        lifted = block_out.astype(jnp.float32)
        center = lax.optimization_barrier(jnp.mean(lifted, axis=-1, keepdims=True))
        spread = lax.optimization_barrier(jnp.mean((lifted - center) * (lifted - center), axis=-1, keepdims=True))
        normed = ((lifted - center) * lax.rsqrt(spread + 1e-06) * (1.0 + final_scale[branch][None, :]) + final_shift[branch][None, :]).astype(jnp.bfloat16)
        results.append(jnp.dot(normed, patch_weight, preferred_element_type=jnp.float32))
    velocity = results[1] + 3.0 * (results[0] - results[1])
    return (jnp.stack(outputs), velocity)
```

```python
import functools
import math

import jax
import jax.numpy as jnp
from jax import lax
from jax.experimental import pallas as pl
from jax.experimental.pallas import tpu as pltpu
from jax.sharding import PartitionSpec as P


guidance_scale = 3.0
VMEM = pl.BlockSpec(memory_space=pltpu.VMEM)
SMEM = pl.BlockSpec(memory_space=pltpu.SMEM)
NT = (((1,), (1,)), ((), ()))


def dot_f32(a, b):
    return jnp.dot(a, b, preferred_element_type=jnp.float32)


def dot_nt(a, b):
    return lax.dot_general(a, b, NT, preferred_element_type=jnp.float32)


def live_lanes(mask_ref):
    return jnp.where(mask_ref[...] == 1, 0.0, 1.0)


def pick_matrix(mask_ref, live_count):
    live = live_lanes(mask_ref)
    count = live.shape[1]
    rows = lax.broadcasted_iota(jnp.int32, (count, count), 0)
    cols = lax.broadcasted_iota(jnp.int32, (count, count), 1)
    upto = jnp.where(rows <= cols, 1.0, 0.0).astype(jnp.bfloat16)
    wide = jnp.broadcast_to(live, (8, count)).astype(jnp.bfloat16)
    rank = dot_f32(wide, upto)[0:1]
    slot = lax.broadcasted_iota(jnp.int32, (live_count, count), 0).astype(jnp.float32)
    hit = (jnp.broadcast_to(rank, slot.shape) == slot + 1.0) & (jnp.broadcast_to(live, slot.shape) > 0.5)
    return jnp.where(hit, 1.0, 0.0).astype(jnp.bfloat16)


def place_matrix(mask_ref, live_count, first, share):
    live = live_lanes(mask_ref)
    count = live.shape[1]
    wide = jnp.broadcast_to(live, (live_count, count)).astype(jnp.bfloat16)
    rows = lax.broadcasted_iota(jnp.int32, (share, count), 0) + first
    cols = lax.broadcasted_iota(jnp.int32, (share, count), 1)
    rank = dot_nt(jnp.where(cols <= rows, 1.0, 0.0).astype(jnp.bfloat16), wide)
    alive = dot_nt(jnp.where(cols == rows, 1.0, 0.0).astype(jnp.bfloat16), wide)
    slot = lax.broadcasted_iota(jnp.int32, (share, live_count), 1).astype(jnp.float32)
    hit = (rank == slot + 1.0) & (alive > 0.5)
    return jnp.where(hit, 1.0, 0.0).astype(jnp.bfloat16)


def prep_kernel(dims, place_ref, mask_ref, q_gain_ref, k_gain_ref, q_ref, k_ref, v_ref, *outs):
    members, own_heads, depth, live_count = dims
    packs, asks = outs[:members], outs[members:]
    count = q_ref.shape[0]
    width = own_heads * depth
    position = place_ref[0]
    picks = pick_matrix(mask_ref, live_count)

    def normed(ref, columns, gain_ref):
        lifted = ref[:, columns].astype(jnp.float32)
        mean_square = jnp.mean(lifted * lifted, axis=-1, keepdims=True)
        return (lifted * lax.rsqrt(mean_square + 1e-06) * gain_ref[...]).astype(jnp.bfloat16)

    for b in range(members):
        base = lax.rem(position + b, members) * width
        for h in range(own_heads):
            source = pl.ds(pl.multiple_of(base + h * depth, depth), depth)
            target = pl.ds(h * depth, depth)
            picked = dot_f32(picks, normed(q_ref, source, q_gain_ref)).astype(jnp.bfloat16)
            packs[b][pl.ds(0, live_count), target] = picked
            if asks:
                asks[b][:, target] = picked
            packs[b][pl.ds(live_count, count), target] = normed(k_ref, source, k_gain_ref)
        everything = pl.ds(pl.multiple_of(base, depth), width)
        packs[b][pl.ds(live_count + count, count), :] = v_ref[:, everything]


def attend_kernel(dims, *refs):
    members, groups, own_heads, depth, live_count, count, stat_rows = dims
    sources = members * groups
    packs = refs[:members]
    asks = refs[members:sources]
    outs = refs[sources : 2 * sources]
    stats = refs[2 * sources]
    factor = depth ** (-0.5)
    power = factor * math.log2(math.e)
    lanes = lax.broadcasted_iota(jnp.int32, (live_count, stats.shape[2]), 1)
    if groups > 1:
        stats[...] = jnp.zeros_like(stats)
    batch = 2 if sources % 2 == 0 else 1

    def one_head(h, carry):
        columns = pl.ds(pl.multiple_of(h * depth, depth), depth)
        keys = [ref[pl.ds(live_count, count), columns] for ref in packs]
        values = [ref[pl.ds(live_count + count, count), columns] for ref in packs]
        for first in range(0, sources, batch):
            chosen = range(first, first + batch)
            parts = [(packs[s] if s < members else asks[s - members])[pl.ds(0, live_count), columns] for s in chosen]
            queries = jnp.concatenate(parts, axis=0) if batch > 1 else parts[0]
            scores = [dot_nt(queries, k) for k in keys]
            biggest = functools.reduce(jnp.maximum, scores)
            biggest = jnp.max(biggest, axis=-1, keepdims=True)
            weights = [jnp.exp2((s - biggest) * power) for s in scores]
            totals = jnp.sum(functools.reduce(jnp.add, weights), axis=-1, keepdims=True)
            summed = functools.reduce(jnp.add, [dot_f32(w.astype(jnp.bfloat16), v) for w, v in zip(weights, values)])
            attended = (summed / totals).astype(jnp.bfloat16)
            logged = biggest * factor + jnp.log(totals)
            for n, s in enumerate(chosen):
                rows = slice(n * live_count, (n + 1) * live_count)
                outs[s][pl.ds(pl.multiple_of(h * live_count, live_count), live_count), :] = attended[rows]
                if groups > 1:
                    rest = logged[rows]
                    for piece in range(3):
                        rounded = rest.astype(jnp.bfloat16).astype(jnp.float32)
                        stats[s] = jnp.where(lanes == piece * own_heads + h, rounded, stats[s])
                        rest = rest - rounded
        return carry

    lax.fori_loop(0, own_heads, one_head, 0)
    if groups > 1:
        for s in range(sources):
            turned = jnp.transpose(stats[s])[:stat_rows]
            outs[s][pl.ds(own_heads * live_count, stat_rows), :] = turned.astype(jnp.bfloat16)


def merge_kernel(dims, place_ref, mask_ref, *refs):
    members, groups, own_heads, depth, live_count, stat_rows, parts = dims
    sources = members * groups
    parcels = refs[:sources]
    weight_ref = refs[sources]
    own_ref = refs[sources + 1]
    sends = refs[sources + 2 : sources + 1 + parts]
    attended_ref, spread_ref = refs[sources + 1 + parts :]
    share = own_ref.shape[0]
    width = own_heads * depth

    @pl.when(pl.program_id(0) == 0)
    def _():
        position, mine = place_ref[0], place_ref[1]
        for b in range(members):
            logged = []
            if groups > 1:
                for a in range(groups):
                    stat = parcels[a * members + b][pl.ds(own_heads * live_count, stat_rows), :].astype(jnp.float32)
                    full = jnp.concatenate([stat, jnp.zeros((depth - stat_rows, live_count), jnp.float32)], axis=0)
                    turned = jnp.transpose(full)
                    logged.append(
                        [
                            turned[:, h : h + 1]
                            + turned[:, own_heads + h : own_heads + h + 1]
                            + turned[:, 2 * own_heads + h : 2 * own_heads + h + 1]
                            for h in range(own_heads)
                        ]
                    )
            for h in range(own_heads):
                rows = pl.ds(h * live_count, live_count)
                held = [parcels[a * members + b][rows, :] for a in range(groups)]
                if groups > 1:
                    biggest = functools.reduce(jnp.maximum, [l[h] for l in logged])
                    shares = [jnp.exp(l[h] - biggest) for l in logged]
                    total = functools.reduce(jnp.add, shares)
                    mixed = functools.reduce(
                        jnp.add, [w * o.astype(jnp.float32) for w, o in zip(shares, held)]
                    )
                    value = (mixed / total).astype(jnp.bfloat16)
                else:
                    value = held[0]
                base = lax.rem(position + b, members) * width + h * depth
                attended_ref[:, pl.ds(pl.multiple_of(base, depth), depth)] = value
        attended = attended_ref[...]
        for s in range(parts):
            first = lax.rem(mine + s, parts) * share
            placed = dot_f32(place_matrix(mask_ref, live_count, first, share), attended)
            spread_ref[pl.ds(s * share, share), :] = placed.astype(jnp.bfloat16)

    product = dot_f32(spread_ref[...], weight_ref[...])
    own_ref[...] = product[:share]
    for s in range(1, parts):
        sends[s - 1][...] = product[s * share : (s + 1) * share].astype(jnp.bfloat16)


def tail_kernel(parts, mask_ref, own_ref, *refs):
    arrived = refs[: parts - 1]
    input_ref, cached_ref, gate_ref, shift_ref, scale_ref, patch_ref, block_ref, branch_ref = refs[parts - 1 :]
    projected = own_ref[...]
    for ref in arrived:
        projected = projected + ref[...].astype(jnp.float32)
    mixed = input_ref[...].astype(jnp.float32) + gate_ref[...] * projected
    block = jnp.where(mask_ref[...] == 1, cached_ref[...].astype(jnp.float32), mixed).astype(jnp.bfloat16)
    block_ref[...] = block
    lifted = block.astype(jnp.float32)
    centred = lifted - jnp.mean(lifted, axis=-1, keepdims=True)
    spread = jnp.mean(centred * centred, axis=-1, keepdims=True)
    normed = centred * lax.rsqrt(spread + 1e-06) * (1.0 + scale_ref[...]) + shift_ref[...]
    branch_ref[...] = dot_nt(patch_ref[...], normed.astype(jnp.bfloat16))


def shards(
    query_proj,
    key_proj,
    value_proj,
    query_gain,
    key_gain,
    block_input,
    cached_out,
    replay_mask,
    branch_gate,
    attn_weight,
    final_shift,
    final_scale,
    patch_weight,
):
    _, count, width = query_proj.shape
    depth = query_gain.shape[0]
    heads = width // depth
    features = attn_weight.shape[1]
    channels = patch_weight.shape[1]
    live_count = count // 2
    ring = lax.axis_size("ctx")
    parts = lax.axis_size("tp")
    share = count // parts
    members = math.gcd(heads, ring)
    groups = ring // members
    own_heads = heads // members
    own_width = own_heads * depth
    sources = ring
    stat_rows = -(-3 * own_heads // 16) * 16
    here = lax.axis_index("ctx")
    mine = lax.axis_index("tp")
    place = jnp.stack([lax.rem(here, members), mine]).astype(jnp.int32)

    def route(a, b, back):
        pairs = []
        for g in range(groups):
            for p in range(members):
                other = ((g + a) % groups) * members + (p + b) % members
                pairs.append((other, g * members + p) if back else (g * members + p, other))
        return pairs

    pack_shape = jax.ShapeDtypeStruct((live_count + 2 * count, own_width), jnp.bfloat16)
    ask_shape = jax.ShapeDtypeStruct((live_count, own_width), jnp.bfloat16)
    prep_outs = [pack_shape] * members + ([ask_shape] * members if groups > 1 else [])
    prepared = pl.pallas_call(
        functools.partial(prep_kernel, (members, own_heads, depth, live_count)),
        out_shape=prep_outs,
        in_specs=[SMEM] + [VMEM] * 6,
        out_specs=[VMEM] * len(prep_outs),
        compiler_params=pltpu.CompilerParams(vmem_limit_bytes=16 << 20),
        name="prep",
    )(
        place,
        replay_mask,
        query_gain[None],
        key_gain[None],
        query_proj[0],
        key_proj[0],
        value_proj[0],
    )
    packs, asks = list(prepared[:members]), list(prepared[members:])
    for b in range(1, members):
        packs[b] = lax.ppermute(packs[b], "ctx", route(0, b, False))
    gathered = [
        lax.ppermute(asks[b], "ctx", route(a, b, False)) for a in range(1, groups) for b in range(members)
    ]

    parcel_rows = own_heads * live_count + (stat_rows if groups > 1 else 0)
    parcel_shape = jax.ShapeDtypeStruct((parcel_rows, depth), jnp.bfloat16)
    parcels = pl.pallas_call(
        functools.partial(
            attend_kernel, (members, groups, own_heads, depth, live_count, count, stat_rows)
        ),
        out_shape=[parcel_shape] * sources,
        in_specs=[VMEM] * sources,
        out_specs=[VMEM] * sources,
        scratch_shapes=[pltpu.VMEM((sources, live_count, live_count), jnp.float32)],
        compiler_params=pltpu.CompilerParams(vmem_limit_bytes=24 << 20),
        name="attend",
    )(*packs, *gathered)
    parcels = [
        parcels[a * members + b]
        if a == 0 and b == 0
        else lax.ppermute(parcels[a * members + b], "ctx", route(a, b, True))
        for a in range(groups)
        for b in range(members)
    ]

    tile = 512 if features % 512 == 0 else features
    whole = lambda shape: pl.BlockSpec(shape, lambda i: (0,) * len(shape))
    projected = pl.pallas_call(
        functools.partial(
            merge_kernel, (members, groups, own_heads, depth, live_count, stat_rows, parts)
        ),
        out_shape=[jax.ShapeDtypeStruct((share, features), jnp.float32)]
        + [jax.ShapeDtypeStruct((share, features), jnp.bfloat16)] * (parts - 1),
        grid=(features // tile,),
        in_specs=[SMEM, whole((1, count))]
        + [whole((parcel_rows, depth))] * sources
        + [pl.BlockSpec((width, tile), lambda i: (0, i))],
        out_specs=[pl.BlockSpec((share, tile), lambda i: (0, i))] * parts,
        scratch_shapes=[
            pltpu.VMEM((live_count, width), jnp.bfloat16),
            pltpu.VMEM((count, width), jnp.bfloat16),
        ],
        compiler_params=pltpu.CompilerParams(vmem_limit_bytes=24 << 20),
        name="merge",
    )(place, replay_mask, *parcels, attn_weight)
    arrived = [
        lax.ppermute(projected[s], "tp", [(i, (i + s) % parts) for i in range(parts)]) for s in range(1, parts)
    ]

    mask_rows = lax.dynamic_slice_in_dim(replay_mask[0], mine * share, share, 0)[:, None]
    block_out, branch = pl.pallas_call(
        functools.partial(tail_kernel, parts),
        out_shape=[
            jax.ShapeDtypeStruct((share, features), jnp.bfloat16),
            jax.ShapeDtypeStruct((channels, share), jnp.float32),
        ],
        in_specs=[VMEM] * (7 + parts),
        out_specs=[VMEM] * 2,
        compiler_params=pltpu.CompilerParams(vmem_limit_bytes=24 << 20),
        name="tail",
    )(
        mask_rows,
        projected[0],
        *arrived,
        block_input[0],
        cached_out[0],
        branch_gate,
        final_shift,
        final_scale,
        patch_weight.T,
    )
    branches = lax.axis_size("cfg")
    part = channels // branches
    side = lax.axis_index("cfg")
    kept = lax.dynamic_slice_in_dim(branch, side * part, part, 0)
    given = lax.dynamic_slice_in_dim(branch, (1 - side) * part, part, 0)
    partner = lax.ppermute(given, "cfg", [(0, 1), (1, 0)])
    cond = jnp.where(side == 0, kept, partner)
    uncond = jnp.where(side == 0, partner, kept)
    velocity = uncond + guidance_scale * (cond - uncond)
    return (block_out[None], velocity.T)


def solution(mesh):
    in_specs = (
        P("cfg", "ctx", "tp"),
        P("cfg", "ctx", "tp"),
        P("cfg", "ctx", "tp"),
        P(),
        P(),
        P("cfg", ("ctx", "tp"), None),
        P("cfg", ("ctx", "tp"), None),
        P("cfg", "ctx"),
        P("cfg", None),
        P("tp", None),
        P("cfg", None),
        P("cfg", None),
        P(),
    )
    out_specs = (P("cfg", ("ctx", "tp"), None), P(("ctx", "tp"), "cfg"))
    return jax.shard_map(shards, mesh=mesh, in_specs=in_specs, out_specs=out_specs, check_vma=False)
```

```python
import functools
import math

import jax
import jax.numpy as jnp
from jax import lax
from jax.experimental import pallas as pl
from jax.experimental.pallas import tpu as pltpu
from jax.sharding import PartitionSpec as P


guidance_scale = 3.0
VMEM = pl.BlockSpec(memory_space=pltpu.VMEM)
HBM = pl.BlockSpec(memory_space=pltpu.HBM)
NT = (((1,), (1,)), ((), ()))


def in_hbm(value):
    return pltpu.with_memory_space_constraint(value, pltpu.HBM)


def dot_f32(a, b):
    return jnp.dot(a, b, preferred_element_type=jnp.float32)


def dot_nt(a, b):
    return lax.dot_general(a, b, NT, preferred_element_type=jnp.float32)


def live_lanes(mask_ref):
    return jnp.where(mask_ref[...] == 1, 0.0, 1.0)


def pick_matrix(mask_ref, live_count):
    live = live_lanes(mask_ref)
    count = live.shape[1]
    rows = lax.broadcasted_iota(jnp.int32, (count, count), 0)
    cols = lax.broadcasted_iota(jnp.int32, (count, count), 1)
    upto = jnp.where(rows <= cols, 1.0, 0.0).astype(jnp.bfloat16)
    wide = jnp.broadcast_to(live, (8, count)).astype(jnp.bfloat16)
    rank = dot_f32(wide, upto)[0:1]
    slot = lax.broadcasted_iota(jnp.int32, (live_count, count), 0).astype(jnp.float32)
    hit = (jnp.broadcast_to(rank, slot.shape) == slot + 1.0) & (jnp.broadcast_to(live, slot.shape) > 0.5)
    return jnp.where(hit, 1.0, 0.0).astype(jnp.bfloat16)


def place_matrix(mask_ref, live_count, first, share):
    live = live_lanes(mask_ref)
    count = live.shape[1]
    wide = jnp.broadcast_to(live, (live_count, count)).astype(jnp.bfloat16)
    rows = lax.broadcasted_iota(jnp.int32, (share, count), 0) + first
    cols = lax.broadcasted_iota(jnp.int32, (share, count), 1)
    rank = dot_nt(jnp.where(cols <= rows, 1.0, 0.0).astype(jnp.bfloat16), wide)
    alive = dot_nt(jnp.where(cols == rows, 1.0, 0.0).astype(jnp.bfloat16), wide)
    slot = lax.broadcasted_iota(jnp.int32, (share, live_count), 1).astype(jnp.float32)
    hit = (rank == slot + 1.0) & (alive > 0.5)
    return jnp.where(hit, 1.0, 0.0).astype(jnp.bfloat16)


def ring_place(members):
    return lax.rem(lax.axis_index("ctx"), members)


def prep_kernel(dims, mask_hbm, q_gain_hbm, k_gain_hbm, q_hbm, k_hbm, v_hbm, *refs):
    members, own_heads, depth, live_count, n_outs = dims
    outs = refs[:n_outs]
    mask_ref, q_gain_ref, k_gain_ref, q_ref, k_ref, small_sems, q_sems, k_sems, v_sems = refs[n_outs:]
    packs, asks = outs[:members], outs[members:]
    count = q_hbm.shape[0]
    width = own_heads * depth
    position = ring_place(members)
    small = [
        pltpu.make_async_copy(source, target, small_sems.at[n])
        for n, (source, target) in enumerate(
            [(mask_hbm, mask_ref), (q_gain_hbm, q_gain_ref), (k_gain_hbm, k_gain_ref)]
        )
    ]
    for copy in small:
        copy.start()
    order = [b for b in range(1, members)] + [0]
    loads = {}
    for b in order:
        columns = pl.ds(pl.multiple_of(lax.rem(position + b, members) * width, depth), width)
        values = packs[b].at[pl.ds(live_count + count, count), :]
        loads[b] = (
            pltpu.make_async_copy(q_hbm.at[:, columns], q_ref.at[b], q_sems.at[b]),
            pltpu.make_async_copy(k_hbm.at[:, columns], k_ref.at[b], k_sems.at[b]),
            pltpu.make_async_copy(v_hbm.at[:, columns], values, v_sems.at[b]),
        )
    for b in order:
        loads[b][0].start()
        loads[b][1].start()
    for b in order:
        loads[b][2].start()
    for copy in small:
        copy.wait()
    picks = pick_matrix(mask_ref, live_count)

    def normed(lifted, gain_ref):
        lifted = lifted.astype(jnp.float32)
        mean_square = jnp.mean(lifted * lifted, axis=-1, keepdims=True)
        return (lifted * lax.rsqrt(mean_square + 1e-06) * gain_ref[...]).astype(jnp.bfloat16)

    for b in order:
        loads[b][0].wait()
        loads[b][1].wait()
        for h in range(own_heads):
            columns = pl.ds(h * depth, depth)
            picked = dot_f32(picks, normed(q_ref[b, :, columns], q_gain_ref)).astype(jnp.bfloat16)
            packs[b][pl.ds(0, live_count), columns] = picked
            if asks:
                asks[b][:, columns] = picked
            packs[b][pl.ds(live_count, count), columns] = normed(k_ref[b, :, columns], k_gain_ref)
    for b in order:
        loads[b][2].wait()


def fetch_kernel(count, *refs):
    sources, targets, sems = refs[:count], refs[count + 1 : 2 * count + 1], refs[2 * count + 1]
    copies = [pltpu.make_async_copy(s, t, sems.at[n]) for n, (s, t) in enumerate(zip(sources, targets))]
    for copy in copies:
        copy.start()
    for copy in copies:
        copy.wait()


def attend_kernel(dims, *refs):
    members, partial, own_heads, depth, live_count, count, stat_rows, n_asks = dims
    refs = refs[1:]
    packs = refs[:members]
    asks = refs[members : members + n_asks] if n_asks else packs
    sources = len(asks)
    outs = refs[members + n_asks : members + n_asks + sources]
    stats = refs[members + n_asks + sources]
    factor = depth ** (-0.5)
    power = factor * math.log2(math.e)
    lanes = lax.broadcasted_iota(jnp.int32, (live_count, stats.shape[2]), 1)
    if partial:
        stats[...] = jnp.zeros_like(stats)
    batch = 2 if sources % 2 == 0 else 1

    def one_head(h, carry):
        columns = pl.ds(pl.multiple_of(h * depth, depth), depth)
        keys = [ref[pl.ds(live_count, count), columns] for ref in packs]
        values = [ref[pl.ds(live_count + count, count), columns] for ref in packs]
        for first in range(0, sources, batch):
            chosen = range(first, first + batch)
            parts = [asks[s][pl.ds(0, live_count), columns] for s in chosen]
            queries = jnp.concatenate(parts, axis=0) if batch > 1 else parts[0]
            scores = [dot_nt(queries, k) for k in keys]
            biggest = functools.reduce(jnp.maximum, scores)
            biggest = jnp.max(biggest, axis=-1, keepdims=True)
            weights = [jnp.exp2((s - biggest) * power) for s in scores]
            totals = jnp.sum(functools.reduce(jnp.add, weights), axis=-1, keepdims=True)
            summed = functools.reduce(jnp.add, [dot_f32(w.astype(jnp.bfloat16), v) for w, v in zip(weights, values)])
            attended = (summed / totals).astype(jnp.bfloat16)
            logged = biggest * factor + jnp.log(totals)
            for n, s in enumerate(chosen):
                rows = slice(n * live_count, (n + 1) * live_count)
                outs[s][pl.ds(pl.multiple_of(h * live_count, live_count), live_count), :] = attended[rows]
                if partial:
                    rest = logged[rows]
                    for piece in range(3):
                        rounded = rest.astype(jnp.bfloat16).astype(jnp.float32)
                        stats[s] = jnp.where(lanes == piece * own_heads + h, rounded, stats[s])
                        rest = rest - rounded
        return carry

    lax.fori_loop(0, own_heads, one_head, 0)
    if partial:
        for s in range(sources):
            turned = jnp.transpose(stats[s])[:stat_rows]
            outs[s][pl.ds(own_heads * live_count, stat_rows), :] = turned.astype(jnp.bfloat16)


def merge_kernel(dims, mask_ref, weight_ref, *refs):
    members, groups, own_heads, depth, live_count, stat_rows, parts = dims
    sources = members * groups
    parcels = refs[:sources]
    sends = refs[sources : sources + parts - 1]
    own_ref, attended_ref = refs[sources + parts - 1 :]
    share = own_ref.shape[0]
    width = own_heads * depth
    position, mine = ring_place(members), lax.axis_index("tp")
    for b in range(members):
        logged = []
        if groups > 1:
            for a in range(groups):
                stat = parcels[a * members + b][pl.ds(own_heads * live_count, stat_rows), :].astype(jnp.float32)
                full = jnp.concatenate([stat, jnp.zeros((depth - stat_rows, live_count), jnp.float32)], axis=0)
                turned = jnp.transpose(full)
                pieces = [turned[:, n : n + 1] for n in range(3 * own_heads)]
                logged.append(
                    [pieces[h] + pieces[own_heads + h] + pieces[2 * own_heads + h] for h in range(own_heads)]
                )
        for h in range(own_heads):
            rows = pl.ds(h * live_count, live_count)
            held = [parcels[a * members + b][rows, :] for a in range(groups)]
            if groups > 1:
                biggest = functools.reduce(jnp.maximum, [l[h] for l in logged])
                shares = [jnp.exp(l[h] - biggest) for l in logged]
                total = functools.reduce(jnp.add, shares)
                mixed = functools.reduce(jnp.add, [w * o.astype(jnp.float32) for w, o in zip(shares, held)])
                value = (mixed / total).astype(jnp.bfloat16)
            else:
                value = held[0]
            base = lax.rem(position + b, members) * width + h * depth
            attended_ref[:, pl.ds(pl.multiple_of(base, depth), depth)] = value
    attended = attended_ref[...]
    for s in list(range(1, parts)) + [0]:
        first = lax.rem(mine + s, parts) * share
        placed = dot_f32(place_matrix(mask_ref, live_count, first, share), attended).astype(jnp.bfloat16)
        if s == 0:
            own_ref[...] = placed
        else:
            project(placed, weight_ref, sends[s - 1])


def project(rows, weight_ref, out_ref):
    features = weight_ref.shape[1]
    tile = 512 if features % 512 == 0 else features
    for first in range(0, features, tile):
        columns = pl.ds(first, tile)
        out_ref[:, columns] = dot_f32(rows, weight_ref[:, columns]).astype(out_ref.dtype)


def project_kernel(rows_ref, weight_ref, out_ref):
    project(rows_ref[...], weight_ref, out_ref)


def tail_kernel(parts, mask_ref, own_ref, *refs):
    arrived = refs[: parts - 1]
    input_ref, cached_ref, gate_ref, shift_ref, scale_ref, patch_ref, block_ref, kept_ref, given_ref = refs[
        parts - 1 :
    ]
    projected = own_ref[...]
    for ref in arrived:
        projected = projected + ref[...].astype(jnp.float32)
    share = projected.shape[0]
    count = mask_ref.shape[1]
    first = lax.axis_index("tp") * share
    rows = lax.broadcasted_iota(jnp.int32, (share, count), 0) + first
    cols = lax.broadcasted_iota(jnp.int32, (share, count), 1)
    replayed = jnp.where((cols == rows) & (jnp.broadcast_to(mask_ref[...], rows.shape) == 1), 1.0, 0.0)
    replayed = jnp.sum(replayed, axis=-1, keepdims=True) > 0.5
    mixed = input_ref[...].astype(jnp.float32) + gate_ref[...] * projected
    block = jnp.where(replayed, cached_ref[...].astype(jnp.float32), mixed).astype(jnp.bfloat16)
    block_ref[...] = block
    lifted = block.astype(jnp.float32)
    centred = lifted - jnp.mean(lifted, axis=-1, keepdims=True)
    spread = jnp.mean(centred * centred, axis=-1, keepdims=True)
    normed = centred * lax.rsqrt(spread + 1e-06) * (1.0 + scale_ref[...]) + shift_ref[...]
    branch = dot_nt(patch_ref[...], normed.astype(jnp.bfloat16))
    half = branch.shape[0] // 2
    first_side = lax.axis_index("cfg") == 0
    kept_ref[...] = jnp.where(first_side, branch[:half], branch[half:])
    given_ref[...] = jnp.where(first_side, branch[half:], branch[:half])


def guide_kernel(kept_ref, partner_ref, out_ref):
    first_side = lax.axis_index("cfg") == 0
    cond = jnp.where(first_side, kept_ref[...], partner_ref[...])
    uncond = jnp.where(first_side, partner_ref[...], kept_ref[...])
    out_ref[...] = uncond + guidance_scale * (cond - uncond)


def shards(
    query_proj,
    key_proj,
    value_proj,
    query_gain,
    key_gain,
    block_input,
    cached_out,
    replay_mask,
    branch_gate,
    attn_weight,
    final_shift,
    final_scale,
    patch_weight,
):
    _, count, width = query_proj.shape
    depth = query_gain.shape[0]
    heads = width // depth
    features = attn_weight.shape[1]
    channels = patch_weight.shape[1]
    live_count = count // 2
    ring = lax.axis_size("ctx")
    parts = lax.axis_size("tp")
    share = count // parts
    members = math.gcd(heads, ring)
    groups = ring // members
    own_heads = heads // members
    own_width = own_heads * depth
    partial = groups > 1
    stat_rows = -(-3 * own_heads // 16) * 16

    def route(a, b, back):
        pairs = []
        for g in range(groups):
            for p in range(members):
                other = ((g + a) % groups) * members + (p + b) % members
                pairs.append((other, g * members + p) if back else (g * members + p, other))
        return pairs

    def call(kernel, name, inputs, outs, in_specs=None, out_specs=None, scratch=(), limit=24, cost=None):
        return pl.pallas_call(
            kernel,
            out_shape=outs,
            in_specs=in_specs or [VMEM] * len(inputs),
            out_specs=out_specs or [VMEM] * len(outs),
            scratch_shapes=scratch,
            compiler_params=pltpu.CompilerParams(vmem_limit_bytes=limit << 20),
            cost_estimate=cost,
            name=name,
        )(*inputs)

    bf16, f32 = jnp.bfloat16, jnp.float32
    shaped = jax.ShapeDtypeStruct
    pack_shape = shaped((live_count + 2 * count, own_width), bf16)
    ask_shape = shaped((live_count, own_width), bf16)
    prep_outs = [pack_shape] * members + ([ask_shape] * members if partial else [])
    prep_inputs = (replay_mask, query_gain[None], key_gain[None], query_proj[0], key_proj[0], value_proj[0])
    prepared = call(
        functools.partial(prep_kernel, (members, own_heads, depth, live_count, len(prep_outs))),
        "prep",
        tuple(map(in_hbm, prep_inputs)),
        prep_outs,
        in_specs=[HBM] * len(prep_inputs),
        scratch=[
            pltpu.VMEM((1, count), jnp.int32),
            pltpu.VMEM((1, depth), f32),
            pltpu.VMEM((1, depth), f32),
            pltpu.VMEM((members, count, own_width), bf16),
            pltpu.VMEM((members, count, own_width), bf16),
            pltpu.SemaphoreType.DMA((3,)),
            pltpu.SemaphoreType.DMA((members,)),
            pltpu.SemaphoreType.DMA((members,)),
            pltpu.SemaphoreType.DMA((members,)),
        ],
        limit=16,
    )
    packs, asks = list(prepared[:members]), list(prepared[members:])
    for b in range(1, members):
        packs[b] = lax.ppermute(packs[b], "ctx", route(0, b, False))
    asked = [lax.ppermute(asks[b], "ctx", route(a, b, False)) for a in range(1, groups) for b in range(members)]

    wanted = (
        attn_weight,
        block_input[0],
        cached_out[0],
        branch_gate,
        final_shift,
        final_scale,
        patch_weight.T,
        replay_mask,
    )
    fetched = call(
        functools.partial(fetch_kernel, len(wanted)),
        "fetch",
        (*map(in_hbm, wanted), packs[0]),
        [shaped(w.shape, w.dtype) for w in wanted],
        in_specs=[HBM] * len(wanted) + [VMEM],
        scratch=[pltpu.SemaphoreType.DMA((len(wanted),))],
        limit=16,
        cost=pl.CostEstimate(flops=0, transcendentals=0, bytes_accessed=2 * sum(w.size * w.dtype.itemsize for w in wanted)),
    )
    weight, inputs_here, cached_here, gate, shift, scale, patch, mask = fetched

    parcel_rows = own_heads * live_count + (stat_rows if partial else 0)
    parcel_shape = shaped((parcel_rows, depth), bf16)

    def attend(name, after, packs, asks, sources):
        pairs = sources * live_count * members * count * own_heads
        return call(
            functools.partial(
                attend_kernel,
                (members, partial, own_heads, depth, live_count, count, stat_rows, len(asks)),
            ),
            name,
            (after, *packs, *asks),
            [parcel_shape] * sources,
            scratch=[pltpu.VMEM((sources, live_count, live_count), f32)],
            cost=pl.CostEstimate(flops=4 * pairs * depth, transcendentals=pairs, bytes_accessed=1 << 20),
        )

    near = attend("near", mask, packs, [], members)
    parcels = [near[0]] + [lax.ppermute(near[b], "ctx", route(0, b, True)) for b in range(1, members)]
    if partial:
        far = attend("far", near[0], packs, asked, members * (groups - 1))
        parcels += [
            lax.ppermute(far[(a - 1) * members + b], "ctx", route(a, b, True))
            for a in range(1, groups)
            for b in range(members)
        ]

    merged = call(
        functools.partial(merge_kernel, (members, groups, own_heads, depth, live_count, stat_rows, parts)),
        "merge",
        (mask, weight, *parcels),
        [shaped((share, features), bf16)] * (parts - 1) + [shaped((share, width), bf16)],
        scratch=[pltpu.VMEM((live_count, width), bf16)],
    )
    arrived = [
        lax.ppermute(merged[s - 1], "tp", [(i, (i + s) % parts) for i in range(parts)]) for s in range(1, parts)
    ]
    (own,) = call(
        project_kernel,
        "own",
        (merged[-1], weight),
        [shaped((share, features), f32)],
        cost=pl.CostEstimate(flops=2 * share * width * features, transcendentals=0, bytes_accessed=1 << 20),
    )

    half = channels // 2
    block_out, kept, given = call(
        functools.partial(tail_kernel, parts),
        "tail",
        (mask, own, *arrived, inputs_here, cached_here, gate, shift, scale, patch),
        [shaped((share, features), bf16), shaped((half, share), f32), shaped((half, share), f32)],
    )
    partner = lax.ppermute(given, "cfg", [(0, 1), (1, 0)])
    (velocity,) = call(guide_kernel, "guide", (kept, partner), [shaped((half, share), f32)], limit=4)
    return (block_out[None], velocity.T)


def solution(mesh):
    in_specs = (
        P("cfg", "ctx", "tp"),
        P("cfg", "ctx", "tp"),
        P("cfg", "ctx", "tp"),
        P(),
        P(),
        P("cfg", ("ctx", "tp"), None),
        P("cfg", ("ctx", "tp"), None),
        P("cfg", "ctx"),
        P("cfg", None),
        P("tp", None),
        P("cfg", None),
        P("cfg", None),
        P(),
    )
    out_specs = (P("cfg", ("ctx", "tp"), None), P(("ctx", "tp"), "cfg"))
    return jax.shard_map(shards, mesh=mesh, in_specs=in_specs, out_specs=out_specs, check_vma=False)
```

```python
import functools
import math

import jax
import jax.numpy as jnp
from jax import lax
from jax.experimental import pallas as pl
from jax.experimental.pallas import tpu as pltpu
from jax.sharding import PartitionSpec as P


guidance_scale = 3.0
VMEM = pl.BlockSpec(memory_space=pltpu.VMEM)
HBM = pl.BlockSpec(memory_space=pltpu.HBM)
NT = (((1,), (1,)), ((), ()))


def in_hbm(value):
    return pltpu.with_memory_space_constraint(value, pltpu.HBM)


def dot_f32(a, b):
    return jnp.dot(a, b, preferred_element_type=jnp.float32)


def dot_nt(a, b):
    return lax.dot_general(a, b, NT, preferred_element_type=jnp.float32)


def live_lanes(mask_ref):
    return jnp.where(mask_ref[...] == 1, 0.0, 1.0)


def pick_matrix(mask_ref, live_count):
    live = live_lanes(mask_ref)
    count = live.shape[1]
    rows = lax.broadcasted_iota(jnp.int32, (count, count), 0)
    cols = lax.broadcasted_iota(jnp.int32, (count, count), 1)
    upto = jnp.where(rows <= cols, 1.0, 0.0).astype(jnp.bfloat16)
    wide = jnp.broadcast_to(live, (8, count)).astype(jnp.bfloat16)
    rank = dot_f32(wide, upto)[0:1]
    slot = lax.broadcasted_iota(jnp.int32, (live_count, count), 0).astype(jnp.float32)
    hit = (jnp.broadcast_to(rank, slot.shape) == slot + 1.0) & (jnp.broadcast_to(live, slot.shape) > 0.5)
    return jnp.where(hit, 1.0, 0.0).astype(jnp.bfloat16)


def place_matrix(mask_ref, live_count, first, share):
    live = live_lanes(mask_ref)
    count = live.shape[1]
    wide = jnp.broadcast_to(live, (live_count, count)).astype(jnp.bfloat16)
    rows = lax.broadcasted_iota(jnp.int32, (share, count), 0) + first
    cols = lax.broadcasted_iota(jnp.int32, (share, count), 1)
    rank = dot_nt(jnp.where(cols <= rows, 1.0, 0.0).astype(jnp.bfloat16), wide)
    alive = dot_nt(jnp.where(cols == rows, 1.0, 0.0).astype(jnp.bfloat16), wide)
    slot = lax.broadcasted_iota(jnp.int32, (share, live_count), 1).astype(jnp.float32)
    hit = (rank == slot + 1.0) & (alive > 0.5)
    return jnp.where(hit, 1.0, 0.0).astype(jnp.bfloat16)


def ring_place(members):
    return lax.rem(lax.axis_index("ctx"), members)


def unit_rows(raw, gain):
    lifted = raw.astype(jnp.float32)
    mean_square = jnp.mean(lifted * lifted, axis=-1, keepdims=True)
    return (lifted * lax.rsqrt(mean_square + 1e-06) * gain).astype(jnp.bfloat16)


def split_kernel(dims, k_hbm, v_hbm, *refs):
    members, width, depth = dims
    outs, sems = refs[:members], refs[members]
    count = k_hbm.shape[0]
    position = ring_place(members)
    copies = []
    for b in [b for b in range(1, members)] + [0]:
        columns = pl.ds(pl.multiple_of(lax.rem(position + b, members) * width, depth), width)
        for n, source in enumerate((k_hbm, v_hbm)):
            target = outs[b].at[pl.ds(n * count, count), :]
            copies.append(pltpu.make_async_copy(source.at[:, columns], target, sems.at[n, b]))
    for copy in copies:
        copy.start()
    for copy in copies:
        copy.wait()


def ask_kernel(dims, mask_hbm, gain_hbm, q_hbm, *refs):
    members, own_heads, depth, live_count = dims
    asks = refs[1 : members + 1]
    mask_ref, gain_ref, q_ref, small_sems, q_sems = refs[members + 1 :]
    width = own_heads * depth
    position = ring_place(members)
    small = [
        pltpu.make_async_copy(mask_hbm, mask_ref, small_sems.at[0]),
        pltpu.make_async_copy(gain_hbm, gain_ref, small_sems.at[1]),
    ]
    for copy in small:
        copy.start()
    order = [b for b in range(1, members)] + [0]
    loads = {}
    for b in order:
        columns = pl.ds(pl.multiple_of(lax.rem(position + b, members) * width, depth), width)
        loads[b] = pltpu.make_async_copy(q_hbm.at[:, columns], q_ref.at[b], q_sems.at[b])
        loads[b].start()
    for copy in small:
        copy.wait()
    picks = pick_matrix(mask_ref, live_count)
    gain = gain_ref[...]
    for b in order:
        loads[b].wait()
        picked = dot_f32(picks, q_ref[b])
        for h in range(own_heads):
            columns = slice(h * depth, (h + 1) * depth)
            asks[b][:, columns] = unit_rows(picked[:, columns], gain)


def unit_kernel(depth, gain_ref, *refs):
    pairs, out_ref = refs[:-1], refs[-1]
    count = out_ref.shape[0] // len(pairs)
    gain = gain_ref[...]
    for b, ref in enumerate(pairs):
        for first in range(0, out_ref.shape[1], depth):
            columns = slice(first, first + depth)
            out_ref[pl.ds(b * count, count), columns] = unit_rows(ref[pl.ds(0, count), columns], gain)


def fetch_kernel(dims, *refs):
    n, live_count, parts = dims
    sources, targets, places_ref, sems = refs[:n], refs[n + 1 : 2 * n + 1], refs[2 * n + 1], refs[2 * n + 2]
    copies = [pltpu.make_async_copy(s, t, sems.at[i]) for i, (s, t) in enumerate(zip(sources, targets))]
    for copy in copies:
        copy.start()
    mask_ref = targets[0]
    copies[0].wait()
    share = places_ref.shape[1]
    for s in range(parts):
        first = lax.rem(lax.axis_index("tp") + s, parts) * share
        places_ref[s] = place_matrix(mask_ref, live_count, first, share)
    for copy in copies[1:]:
        copy.wait()


def attend_kernel(dims, *refs):
    members, partial, own_heads, depth, live_count, count, stat_rows, sources = dims
    pairs, units_ref = refs[1 : members + 1], refs[members + 1]
    asks = refs[members + 2 : members + 2 + sources]
    outs, stats = refs[members + 2 + sources : -1], refs[-1]
    factor = depth ** (-0.5)
    power = factor * math.log2(math.e)
    lanes = lax.broadcasted_iota(jnp.int32, (live_count, stats.shape[2]), 1)
    if partial:
        stats[...] = jnp.zeros_like(stats)
    batch = 2 if sources % 2 == 0 else 1

    def one_head(h, carry):
        columns = pl.ds(pl.multiple_of(h * depth, depth), depth)
        keys = [units_ref[pl.ds(b * count, count), columns] for b in range(members)]
        values = [ref[pl.ds(count, count), columns] for ref in pairs]
        for first in range(0, sources, batch):
            chosen = range(first, first + batch)
            parts = [asks[s][:, columns] for s in chosen]
            queries = jnp.concatenate(parts, axis=0) if batch > 1 else parts[0]
            scores = [dot_nt(queries, k) for k in keys]
            biggest = functools.reduce(jnp.maximum, scores)
            biggest = jnp.max(biggest, axis=-1, keepdims=True)
            weights = [jnp.exp2((s - biggest) * power) for s in scores]
            totals = jnp.sum(functools.reduce(jnp.add, weights), axis=-1, keepdims=True)
            summed = functools.reduce(jnp.add, [dot_f32(w.astype(jnp.bfloat16), v) for w, v in zip(weights, values)])
            attended = (summed / totals).astype(jnp.bfloat16)
            logged = biggest * factor + jnp.log(totals)
            for n, s in enumerate(chosen):
                rows = slice(n * live_count, (n + 1) * live_count)
                outs[s][pl.ds(pl.multiple_of(h * live_count, live_count), live_count), :] = attended[rows]
                if partial:
                    rest = logged[rows]
                    for piece in range(3):
                        rounded = rest.astype(jnp.bfloat16).astype(jnp.float32)
                        stats[s] = jnp.where(lanes == piece * own_heads + h, rounded, stats[s])
                        rest = rest - rounded
        return carry

    lax.fori_loop(0, own_heads, one_head, 0)
    if partial:
        for s in range(sources):
            turned = jnp.transpose(stats[s])[:stat_rows]
            outs[s][pl.ds(own_heads * live_count, stat_rows), :] = turned.astype(jnp.bfloat16)


def merge_kernel(dims, places_ref, weight_ref, *refs):
    members, groups, own_heads, depth, live_count, stat_rows, parts = dims
    sources = members * groups
    parcels = refs[:sources]
    sends = refs[sources : sources + parts - 1]
    own_ref, attended_ref = refs[sources + parts - 1 :]
    width = own_heads * depth
    position = ring_place(members)
    for b in range(members):
        logged = []
        if groups > 1:
            for a in range(groups):
                stat = parcels[a * members + b][pl.ds(own_heads * live_count, stat_rows), :].astype(jnp.float32)
                full = jnp.concatenate([stat, jnp.zeros((depth - stat_rows, live_count), jnp.float32)], axis=0)
                turned = jnp.transpose(full)
                pieces = [turned[:, n : n + 1] for n in range(3 * own_heads)]
                logged.append(
                    [pieces[h] + pieces[own_heads + h] + pieces[2 * own_heads + h] for h in range(own_heads)]
                )
        for h in range(own_heads):
            rows = pl.ds(h * live_count, live_count)
            held = [parcels[a * members + b][rows, :] for a in range(groups)]
            if groups > 1:
                biggest = functools.reduce(jnp.maximum, [l[h] for l in logged])
                shares = [jnp.exp(l[h] - biggest) for l in logged]
                total = functools.reduce(jnp.add, shares)
                mixed = functools.reduce(jnp.add, [w * o.astype(jnp.float32) for w, o in zip(shares, held)])
                value = (mixed / total).astype(jnp.bfloat16)
            else:
                value = held[0]
            base = lax.rem(position + b, members) * width + h * depth
            attended_ref[:, pl.ds(pl.multiple_of(base, depth), depth)] = value
    attended = attended_ref[...]
    for s in list(range(1, parts)) + [0]:
        placed = dot_f32(places_ref[s], attended).astype(jnp.bfloat16)
        if s == 0:
            own_ref[...] = placed
        else:
            project(placed, weight_ref, sends[s - 1])


def project(rows, weight_ref, out_ref):
    features = weight_ref.shape[1]
    tile = 512 if features % 512 == 0 else features
    for first in range(0, features, tile):
        columns = pl.ds(first, tile)
        out_ref[:, columns] = dot_f32(rows, weight_ref[:, columns]).astype(out_ref.dtype)


def project_kernel(rows_ref, weight_ref, out_ref):
    project(rows_ref[...], weight_ref, out_ref)


def tail_kernel(parts, mask_ref, own_ref, *refs):
    arrived = refs[: parts - 1]
    input_ref, cached_ref, gate_ref, shift_ref, scale_ref, patch_ref, block_ref, kept_ref, given_ref = refs[
        parts - 1 :
    ]
    projected = own_ref[...]
    for ref in arrived:
        projected = projected + ref[...].astype(jnp.float32)
    share = projected.shape[0]
    count = mask_ref.shape[1]
    first = lax.axis_index("tp") * share
    rows = lax.broadcasted_iota(jnp.int32, (share, count), 0) + first
    cols = lax.broadcasted_iota(jnp.int32, (share, count), 1)
    replayed = jnp.where((cols == rows) & (jnp.broadcast_to(mask_ref[...], rows.shape) == 1), 1.0, 0.0)
    replayed = jnp.sum(replayed, axis=-1, keepdims=True) > 0.5
    mixed = input_ref[...].astype(jnp.float32) + gate_ref[...] * projected
    block = jnp.where(replayed, cached_ref[...].astype(jnp.float32), mixed).astype(jnp.bfloat16)
    block_ref[...] = block
    lifted = block.astype(jnp.float32)
    centred = lifted - jnp.mean(lifted, axis=-1, keepdims=True)
    spread = jnp.mean(centred * centred, axis=-1, keepdims=True)
    normed = centred * lax.rsqrt(spread + 1e-06) * (1.0 + scale_ref[...]) + shift_ref[...]
    branch = dot_nt(patch_ref[...], normed.astype(jnp.bfloat16))
    half = branch.shape[0] // 2
    first_side = lax.axis_index("cfg") == 0
    kept_ref[...] = jnp.where(first_side, branch[:half], branch[half:])
    given_ref[...] = jnp.where(first_side, branch[half:], branch[:half])


def guide_kernel(kept_ref, partner_ref, out_ref):
    first_side = lax.axis_index("cfg") == 0
    cond = jnp.where(first_side, kept_ref[...], partner_ref[...])
    uncond = jnp.where(first_side, partner_ref[...], kept_ref[...])
    out_ref[...] = uncond + guidance_scale * (cond - uncond)


def shards(
    query_proj,
    key_proj,
    value_proj,
    query_gain,
    key_gain,
    block_input,
    cached_out,
    replay_mask,
    branch_gate,
    attn_weight,
    final_shift,
    final_scale,
    patch_weight,
):
    _, count, width = query_proj.shape
    depth = query_gain.shape[0]
    heads = width // depth
    features = attn_weight.shape[1]
    channels = patch_weight.shape[1]
    live_count = count // 2
    ring = lax.axis_size("ctx")
    parts = lax.axis_size("tp")
    share = count // parts
    members = math.gcd(heads, ring)
    groups = ring // members
    own_heads = heads // members
    own_width = own_heads * depth
    partial = groups > 1
    stat_rows = -(-3 * own_heads // 16) * 16

    def route(a, b, back):
        pairs = []
        for g in range(groups):
            for p in range(members):
                other = ((g + a) % groups) * members + (p + b) % members
                pairs.append((other, g * members + p) if back else (g * members + p, other))
        return pairs

    def call(kernel, inputs, outs, in_specs=None, out_specs=None, scratch=(), limit=24, cost=None):
        return pl.pallas_call(
            kernel,
            out_shape=outs,
            in_specs=in_specs or [VMEM] * len(inputs),
            out_specs=out_specs or [VMEM] * len(outs),
            scratch_shapes=scratch,
            compiler_params=pltpu.CompilerParams(vmem_limit_bytes=limit << 20),
            cost_estimate=cost,
        )(*inputs)

    bf16, f32 = jnp.bfloat16, jnp.float32
    shaped = jax.ShapeDtypeStruct
    pair_shape = shaped((2 * count, own_width), bf16)
    pairs = call(
        functools.partial(split_kernel, (members, own_width, depth)),
        (in_hbm(key_proj[0]), in_hbm(value_proj[0])),
        [pair_shape] * members,
        in_specs=[HBM] * 2,
        scratch=[pltpu.SemaphoreType.DMA((2, members))],
        limit=8,
    )
    pairs = [pairs[0]] + [lax.ppermute(pairs[b], "ctx", route(0, b, False)) for b in range(1, members)]
    asks = call(
        functools.partial(ask_kernel, (members, own_heads, depth, live_count)),
        (*map(in_hbm, (replay_mask, query_gain[None], query_proj[0])), pairs[0]),
        [shaped((live_count, own_width), bf16)] * members,
        in_specs=[HBM] * 3 + [VMEM],
        scratch=[
            pltpu.VMEM((1, count), jnp.int32),
            pltpu.VMEM((1, depth), f32),
            pltpu.VMEM((members, count, own_width), bf16),
            pltpu.SemaphoreType.DMA((2,)),
            pltpu.SemaphoreType.DMA((members,)),
        ],
        limit=16,
    )
    far_asks = [lax.ppermute(asks[b], "ctx", route(a, b, False)) for a in range(1, groups) for b in range(members)]
    near_asks = [asks[0]] + [lax.ppermute(asks[b], "ctx", route(0, b, False)) for b in range(1, members)]

    wanted = (
        replay_mask,
        key_gain[None],
        attn_weight,
        block_input[0],
        cached_out[0],
        branch_gate,
        final_shift,
        final_scale,
        patch_weight.T,
    )
    fetched = call(
        functools.partial(fetch_kernel, (len(wanted), live_count, parts)),
        (*map(in_hbm, wanted), asks[0]),
        [shaped(w.shape, w.dtype) for w in wanted] + [shaped((parts, share, live_count), bf16)],
        in_specs=[HBM] * len(wanted) + [VMEM],
        scratch=[pltpu.SemaphoreType.DMA((len(wanted),))],
        limit=16,
        cost=pl.CostEstimate(flops=0, transcendentals=0, bytes_accessed=2 * sum(w.size * w.dtype.itemsize for w in wanted)),
    )
    mask, key_gain_here, weight, inputs_here, cached_here, gate, shift, scale, patch, places = fetched

    parcel_rows = own_heads * live_count + (stat_rows if partial else 0)
    parcel_shape = shaped((parcel_rows, depth), bf16)

    (units,) = call(
        functools.partial(unit_kernel, depth),
        (key_gain_here, *pairs),
        [shaped((members * count, own_width), bf16)],
        cost=pl.CostEstimate(flops=0, transcendentals=0, bytes_accessed=1 << 20),
    )

    def attend(after, asks):
        scores = len(asks) * live_count * members * count * own_heads
        return call(
            functools.partial(
                attend_kernel,
                (members, partial, own_heads, depth, live_count, count, stat_rows, len(asks)),
            ),
            (after, *pairs, units, *asks),
            [parcel_shape] * len(asks),
            scratch=[pltpu.VMEM((len(asks), live_count, live_count), f32)],
            cost=pl.CostEstimate(flops=4 * scores * depth, transcendentals=scores, bytes_accessed=1 << 20),
        )

    after, distant = mask, []
    pieces = 2
    for piece in range(pieces):
        low, high = (piece * len(far_asks) // pieces, (piece + 1) * len(far_asks) // pieces)
        if low == high:
            continue
        far = attend(after, far_asks[low:high])
        after = far[0]
        distant += [
            lax.ppermute(far[n - low], "ctx", route(1 + n // members, n % members, True))
            for n in range(low, high)
        ]
    near = attend(after, near_asks)
    parcels = [near[0]] + [lax.ppermute(near[b], "ctx", route(0, b, True)) for b in range(1, members)] + distant

    merged = call(
        functools.partial(merge_kernel, (members, groups, own_heads, depth, live_count, stat_rows, parts)),
        (places, weight, *parcels),
        [shaped((share, features), bf16)] * (parts - 1) + [shaped((share, width), bf16)],
        scratch=[pltpu.VMEM((live_count, width), bf16)],
    )
    arrived = [
        lax.ppermute(merged[s - 1], "tp", [(i, (i + s) % parts) for i in range(parts)]) for s in range(1, parts)
    ]
    (own,) = call(
        project_kernel,
        (merged[-1], weight),
        [shaped((share, features), f32)],
        cost=pl.CostEstimate(flops=2 * share * width * features, transcendentals=0, bytes_accessed=1 << 20),
    )

    half = channels // 2
    block_out, kept, given = call(
        functools.partial(tail_kernel, parts),
        (mask, own, *arrived, inputs_here, cached_here, gate, shift, scale, patch),
        [shaped((share, features), bf16), shaped((half, share), f32), shaped((half, share), f32)],
    )
    partner = lax.ppermute(given, "cfg", [(0, 1), (1, 0)])
    (velocity,) = call(guide_kernel, (kept, partner), [shaped((half, share), f32)], limit=4)
    return (block_out[None], velocity.T)


def solution(mesh):
    in_specs = (
        P("cfg", "ctx", "tp"),
        P("cfg", "ctx", "tp"),
        P("cfg", "ctx", "tp"),
        P(),
        P(),
        P("cfg", ("ctx", "tp"), None),
        P("cfg", ("ctx", "tp"), None),
        P("cfg", "ctx"),
        P("cfg", None),
        P("tp", None),
        P("cfg", None),
        P("cfg", None),
        P(),
    )
    out_specs = (P("cfg", ("ctx", "tp"), None), P(("ctx", "tp"), "cfg"))
    return jax.shard_map(shards, mesh=mesh, in_specs=in_specs, out_specs=out_specs, check_vma=False)
```

```python
import functools
import math

import jax
import jax.numpy as jnp
from jax import lax
from jax.experimental import pallas as pl
from jax.experimental.pallas import tpu as pltpu
from jax.sharding import PartitionSpec as P


guidance_scale = 3.0
VMEM = pl.BlockSpec(memory_space=pltpu.VMEM)
HBM = pl.BlockSpec(memory_space=pltpu.HBM)
NT = (((1,), (1,)), ((), ()))


def in_hbm(value):
    return pltpu.with_memory_space_constraint(value, pltpu.HBM)


def dot_f32(a, b):
    return jnp.dot(a, b, preferred_element_type=jnp.float32)


def dot_nt(a, b):
    return lax.dot_general(a, b, NT, preferred_element_type=jnp.float32)


def live_lanes(mask_ref):
    return jnp.where(mask_ref[...] == 1, 0.0, 1.0)


def pick_matrix(mask_ref, live_count):
    live = live_lanes(mask_ref)
    count = live.shape[1]
    rows = lax.broadcasted_iota(jnp.int32, (count, count), 0)
    cols = lax.broadcasted_iota(jnp.int32, (count, count), 1)
    upto = jnp.where(rows <= cols, 1.0, 0.0).astype(jnp.bfloat16)
    wide = jnp.broadcast_to(live, (8, count)).astype(jnp.bfloat16)
    rank = dot_f32(wide, upto)[0:1]
    slot = lax.broadcasted_iota(jnp.int32, (live_count, count), 0).astype(jnp.float32)
    hit = (jnp.broadcast_to(rank, slot.shape) == slot + 1.0) & (jnp.broadcast_to(live, slot.shape) > 0.5)
    return jnp.where(hit, 1.0, 0.0).astype(jnp.bfloat16)


def place_matrix(mask_ref, live_count, first, share):
    live = live_lanes(mask_ref)
    count = live.shape[1]
    wide = jnp.broadcast_to(live, (live_count, count)).astype(jnp.bfloat16)
    rows = lax.broadcasted_iota(jnp.int32, (share, count), 0) + first
    cols = lax.broadcasted_iota(jnp.int32, (share, count), 1)
    rank = dot_nt(jnp.where(cols <= rows, 1.0, 0.0).astype(jnp.bfloat16), wide)
    alive = dot_nt(jnp.where(cols == rows, 1.0, 0.0).astype(jnp.bfloat16), wide)
    slot = lax.broadcasted_iota(jnp.int32, (share, live_count), 1).astype(jnp.float32)
    hit = (rank == slot + 1.0) & (alive > 0.5)
    return jnp.where(hit, 1.0, 0.0).astype(jnp.bfloat16)


def ring_place(members):
    return lax.rem(lax.axis_index("ctx"), members)


def unit_rows(raw, gain):
    lifted = raw.astype(jnp.float32)
    mean_square = jnp.mean(lifted * lifted, axis=-1, keepdims=True)
    return (lifted * lax.rsqrt(mean_square + 1e-06) * gain).astype(jnp.bfloat16)


def split_kernel(dims, k_hbm, v_hbm, *refs):
    members, width, depth = dims
    outs, sems = refs[:members], refs[members]
    count = k_hbm.shape[0]
    position = ring_place(members)
    copies = []
    for b in [b for b in range(1, members)] + [0]:
        columns = pl.ds(pl.multiple_of(lax.rem(position + b, members) * width, depth), width)
        for n, source in enumerate((k_hbm, v_hbm)):
            target = outs[b].at[pl.ds(n * count, count), :]
            copies.append(pltpu.make_async_copy(source.at[:, columns], target, sems.at[n, b]))
    for copy in copies:
        copy.start()
    for copy in copies:
        copy.wait()


def ask_kernel(dims, mask_hbm, gain_hbm, q_hbm, *refs):
    members, own_heads, depth, live_count = dims
    asks = refs[1 : members + 1]
    mask_ref, gain_ref, q_ref, small_sems, q_sems = refs[members + 1 :]
    width = own_heads * depth
    position = ring_place(members)
    small = [
        pltpu.make_async_copy(mask_hbm, mask_ref, small_sems.at[0]),
        pltpu.make_async_copy(gain_hbm, gain_ref, small_sems.at[1]),
    ]
    for copy in small:
        copy.start()
    order = [b for b in range(1, members)] + [0]
    loads = {}
    for b in order:
        columns = pl.ds(pl.multiple_of(lax.rem(position + b, members) * width, depth), width)
        loads[b] = pltpu.make_async_copy(q_hbm.at[:, columns], q_ref.at[b], q_sems.at[b])
        loads[b].start()
    for copy in small:
        copy.wait()
    picks = pick_matrix(mask_ref, live_count)
    gain = gain_ref[...]
    for b in order:
        loads[b].wait()
        picked = dot_f32(picks, q_ref[b])
        for h in range(own_heads):
            columns = slice(h * depth, (h + 1) * depth)
            asks[b][:, columns] = unit_rows(picked[:, columns], gain)


def unit_kernel(depth, gain_ref, *refs):
    pairs, out_ref = refs[:-1], refs[-1]
    count = out_ref.shape[0] // len(pairs)
    gain = gain_ref[...]
    for b, ref in enumerate(pairs):
        for first in range(0, out_ref.shape[1], depth):
            columns = slice(first, first + depth)
            out_ref[pl.ds(b * count, count), columns] = unit_rows(ref[pl.ds(0, count), columns], gain)


def fetch_kernel(dims, *refs):
    n, live_count, parts = dims
    sources, targets, places_ref, sems = refs[:n], refs[n + 1 : 2 * n + 1], refs[2 * n + 1], refs[2 * n + 2]
    copies = [pltpu.make_async_copy(s, t, sems.at[i]) for i, (s, t) in enumerate(zip(sources, targets))]
    for copy in copies:
        copy.start()
    mask_ref = targets[0]
    copies[0].wait()
    share = places_ref.shape[1]
    for s in range(parts):
        first = lax.rem(lax.axis_index("tp") + s, parts) * share
        places_ref[s] = place_matrix(mask_ref, live_count, first, share)
    for copy in copies[1:]:
        copy.wait()


def attend_kernel(dims, *refs):
    members, partial, own_heads, depth, live_count, count, stat_rows, sources = dims
    pairs, units_ref = refs[1 : members + 1], refs[members + 1]
    asks = refs[members + 2 : members + 2 + sources]
    outs, stats = refs[members + 2 + sources : -1], refs[-1]
    factor = depth ** (-0.5)
    power = factor * math.log2(math.e)
    lanes = lax.broadcasted_iota(jnp.int32, (live_count, stats.shape[2]), 1)
    if partial:
        stats[...] = jnp.zeros_like(stats)
    ones = jnp.ones((count, depth), jnp.bfloat16)
    for h in range(own_heads):
        columns = slice(h * depth, (h + 1) * depth)
        for s in range(sources):
            queries = asks[s][:, columns]
            scores = [dot_nt(queries, units_ref[pl.ds(b * count, count), columns]) for b in range(members)]
            biggest = jnp.max(functools.reduce(jnp.maximum, scores), axis=-1, keepdims=True)
            weights = [jnp.exp2((score - biggest) * power).astype(jnp.bfloat16) for score in scores]
            summed = functools.reduce(
                jnp.add,
                [
                    dot_f32(w, jnp.concatenate([ref[pl.ds(count, count), columns], ones], axis=1))
                    for w, ref in zip(weights, pairs)
                ],
            )
            totals = summed[:, depth : depth + 1]
            outs[s][pl.ds(h * live_count, live_count), :] = (summed[:, :depth] / totals).astype(jnp.bfloat16)
            if partial:
                rest = biggest * factor + jnp.log(totals)
                for piece in range(3):
                    rounded = rest.astype(jnp.bfloat16).astype(jnp.float32)
                    stats[s] = jnp.where(lanes == piece * own_heads + h, rounded, stats[s])
                    rest = rest - rounded
    if partial:
        for s in range(sources):
            turned = jnp.transpose(stats[s])[:stat_rows]
            outs[s][pl.ds(own_heads * live_count, stat_rows), :] = turned.astype(jnp.bfloat16)


def merge_kernel(dims, places_ref, weight_ref, *refs):
    members, groups, own_heads, depth, live_count, stat_rows, parts = dims
    sources = members * groups
    parcels = refs[:sources]
    sends = refs[sources : sources + parts - 1]
    own_ref, attended_ref = refs[sources + parts - 1 :]
    width = own_heads * depth
    position = ring_place(members)
    for b in range(members):
        logged = []
        if groups > 1:
            for a in range(groups):
                stat = parcels[a * members + b][pl.ds(own_heads * live_count, stat_rows), :].astype(jnp.float32)
                full = jnp.concatenate([stat, jnp.zeros((depth - stat_rows, live_count), jnp.float32)], axis=0)
                turned = jnp.transpose(full)
                pieces = [turned[:, n : n + 1] for n in range(3 * own_heads)]
                logged.append(
                    [pieces[h] + pieces[own_heads + h] + pieces[2 * own_heads + h] for h in range(own_heads)]
                )
        for h in range(own_heads):
            rows = pl.ds(h * live_count, live_count)
            held = [parcels[a * members + b][rows, :] for a in range(groups)]
            if groups > 1:
                biggest = functools.reduce(jnp.maximum, [l[h] for l in logged])
                shares = [jnp.exp(l[h] - biggest) for l in logged]
                total = functools.reduce(jnp.add, shares)
                mixed = functools.reduce(jnp.add, [w * o.astype(jnp.float32) for w, o in zip(shares, held)])
                value = (mixed / total).astype(jnp.bfloat16)
            else:
                value = held[0]
            base = lax.rem(position + b, members) * width + h * depth
            attended_ref[:, pl.ds(pl.multiple_of(base, depth), depth)] = value
    attended = attended_ref[...]
    for s in list(range(1, parts)) + [0]:
        placed = dot_f32(places_ref[s], attended).astype(jnp.bfloat16)
        if s == 0:
            own_ref[...] = placed
        else:
            project(placed, weight_ref, sends[s - 1])


def project(rows, weight_ref, out_ref):
    features = weight_ref.shape[1]
    tile = 512 if features % 512 == 0 else features
    for first in range(0, features, tile):
        columns = pl.ds(first, tile)
        out_ref[:, columns] = dot_f32(rows, weight_ref[:, columns]).astype(out_ref.dtype)


def project_kernel(rows_ref, weight_ref, out_ref):
    project(rows_ref[...], weight_ref, out_ref)


def tail_kernel(parts, mask_ref, own_ref, *refs):
    arrived = refs[: parts - 1]
    input_ref, cached_ref, gate_ref, shift_ref, scale_ref, patch_ref, block_ref, kept_ref, given_ref = refs[
        parts - 1 :
    ]
    projected = own_ref[...]
    for ref in arrived:
        projected = projected + ref[...].astype(jnp.float32)
    share = projected.shape[0]
    count = mask_ref.shape[1]
    first = lax.axis_index("tp") * share
    rows = lax.broadcasted_iota(jnp.int32, (share, count), 0) + first
    cols = lax.broadcasted_iota(jnp.int32, (share, count), 1)
    replayed = jnp.where((cols == rows) & (jnp.broadcast_to(mask_ref[...], rows.shape) == 1), 1.0, 0.0)
    replayed = jnp.sum(replayed, axis=-1, keepdims=True) > 0.5
    mixed = input_ref[...].astype(jnp.float32) + gate_ref[...] * projected
    block = jnp.where(replayed, cached_ref[...].astype(jnp.float32), mixed).astype(jnp.bfloat16)
    block_ref[...] = block
    lifted = block.astype(jnp.float32)
    centred = lifted - jnp.mean(lifted, axis=-1, keepdims=True)
    spread = jnp.mean(centred * centred, axis=-1, keepdims=True)
    normed = centred * lax.rsqrt(spread + 1e-06) * (1.0 + scale_ref[...]) + shift_ref[...]
    branch = dot_nt(patch_ref[...], normed.astype(jnp.bfloat16))
    half = branch.shape[0] // 2
    first_side = lax.axis_index("cfg") == 0
    kept_ref[...] = jnp.where(first_side, branch[:half], branch[half:])
    given_ref[...] = jnp.where(first_side, branch[half:], branch[:half])


def store_kernel(block_ref, out_hbm, sem):
    copy = pltpu.make_async_copy(block_ref, out_hbm, sem)
    copy.start()
    copy.wait()


def guide_kernel(kept_ref, partner_ref, out_ref):
    first_side = lax.axis_index("cfg") == 0
    cond = jnp.where(first_side, kept_ref[...], partner_ref[...])
    uncond = jnp.where(first_side, partner_ref[...], kept_ref[...])
    out_ref[...] = uncond + guidance_scale * (cond - uncond)


def shards(
    query_proj,
    key_proj,
    value_proj,
    query_gain,
    key_gain,
    block_input,
    cached_out,
    replay_mask,
    branch_gate,
    attn_weight,
    final_shift,
    final_scale,
    patch_weight,
):
    _, count, width = query_proj.shape
    depth = query_gain.shape[0]
    heads = width // depth
    features = attn_weight.shape[1]
    channels = patch_weight.shape[1]
    live_count = count // 2
    ring = lax.axis_size("ctx")
    parts = lax.axis_size("tp")
    share = count // parts
    members = math.gcd(heads, ring)
    groups = ring // members
    own_heads = heads // members
    own_width = own_heads * depth
    partial = groups > 1
    stat_rows = -(-3 * own_heads // 16) * 16

    def route(a, b, back):
        pairs = []
        for g in range(groups):
            for p in range(members):
                other = ((g + a) % groups) * members + (p + b) % members
                pairs.append((other, g * members + p) if back else (g * members + p, other))
        return pairs

    def call(kernel, inputs, outs, in_specs=None, out_specs=None, scratch=(), limit=24, cost=None):
        return pl.pallas_call(
            kernel,
            out_shape=outs,
            in_specs=in_specs or [VMEM] * len(inputs),
            out_specs=out_specs or [VMEM] * len(outs),
            scratch_shapes=scratch,
            compiler_params=pltpu.CompilerParams(vmem_limit_bytes=limit << 20),
            cost_estimate=cost,
        )(*inputs)

    bf16, f32 = jnp.bfloat16, jnp.float32
    shaped = jax.ShapeDtypeStruct
    pair_shape = shaped((2 * count, own_width), bf16)
    pairs = call(
        functools.partial(split_kernel, (members, own_width, depth)),
        (in_hbm(key_proj[0]), in_hbm(value_proj[0])),
        [pair_shape] * members,
        in_specs=[HBM] * 2,
        scratch=[pltpu.SemaphoreType.DMA((2, members))],
        limit=8,
    )
    pairs = [pairs[0]] + [lax.ppermute(pairs[b], "ctx", route(0, b, False)) for b in range(1, members)]
    asks = call(
        functools.partial(ask_kernel, (members, own_heads, depth, live_count)),
        (*map(in_hbm, (replay_mask, query_gain[None], query_proj[0])), pairs[0]),
        [shaped((live_count, own_width), bf16)] * members,
        in_specs=[HBM] * 3 + [VMEM],
        scratch=[
            pltpu.VMEM((1, count), jnp.int32),
            pltpu.VMEM((1, depth), f32),
            pltpu.VMEM((members, count, own_width), bf16),
            pltpu.SemaphoreType.DMA((2,)),
            pltpu.SemaphoreType.DMA((members,)),
        ],
        limit=16,
    )
    far_asks = [lax.ppermute(asks[b], "ctx", route(a, b, False)) for a in range(1, groups) for b in range(members)]
    near_asks = [asks[0]] + [lax.ppermute(asks[b], "ctx", route(0, b, False)) for b in range(1, members)]

    wanted = (
        replay_mask,
        key_gain[None],
        attn_weight,
        block_input[0],
        cached_out[0],
        branch_gate,
        final_shift,
        final_scale,
        patch_weight.T,
    )
    fetched = call(
        functools.partial(fetch_kernel, (len(wanted), live_count, parts)),
        (*map(in_hbm, wanted), asks[0]),
        [shaped(w.shape, w.dtype) for w in wanted] + [shaped((parts, share, live_count), bf16)],
        in_specs=[HBM] * len(wanted) + [VMEM],
        scratch=[pltpu.SemaphoreType.DMA((len(wanted),))],
        limit=16,
        cost=pl.CostEstimate(flops=0, transcendentals=0, bytes_accessed=2 * sum(w.size * w.dtype.itemsize for w in wanted)),
    )
    mask, key_gain_here, weight, inputs_here, cached_here, gate, shift, scale, patch, places = fetched

    parcel_rows = own_heads * live_count + (stat_rows if partial else 0)
    parcel_shape = shaped((parcel_rows, depth), bf16)

    (units,) = call(
        functools.partial(unit_kernel, depth),
        (key_gain_here, *pairs),
        [shaped((members * count, own_width), bf16)],
        cost=pl.CostEstimate(flops=0, transcendentals=0, bytes_accessed=1 << 20),
    )

    def attend(after, asks):
        scores = len(asks) * live_count * members * count * own_heads
        return call(
            functools.partial(
                attend_kernel,
                (members, partial, own_heads, depth, live_count, count, stat_rows, len(asks)),
            ),
            (after, *pairs, units, *asks),
            [parcel_shape] * len(asks),
            scratch=[pltpu.VMEM((len(asks), live_count, live_count), f32)],
            cost=pl.CostEstimate(flops=4 * scores * depth, transcendentals=scores, bytes_accessed=1 << 20),
        )

    after, distant = mask, []
    pieces = 2
    for piece in range(pieces):
        low, high = (piece * len(far_asks) // pieces, (piece + 1) * len(far_asks) // pieces)
        if low == high:
            continue
        far = attend(after, far_asks[low:high])
        after = far[0]
        distant += [
            lax.ppermute(far[n - low], "ctx", route(1 + n // members, n % members, True))
            for n in range(low, high)
        ]
    near = attend(after, near_asks)
    parcels = [near[0]] + [lax.ppermute(near[b], "ctx", route(0, b, True)) for b in range(1, members)] + distant

    merged = call(
        functools.partial(merge_kernel, (members, groups, own_heads, depth, live_count, stat_rows, parts)),
        (places, weight, *parcels),
        [shaped((share, features), bf16)] * (parts - 1) + [shaped((share, width), bf16)],
        scratch=[pltpu.VMEM((live_count, width), bf16)],
    )
    arrived = [
        lax.ppermute(merged[s - 1], "tp", [(i, (i + s) % parts) for i in range(parts)]) for s in range(1, parts)
    ]
    (own,) = call(
        project_kernel,
        (merged[-1], weight),
        [shaped((share, features), f32)],
        cost=pl.CostEstimate(flops=2 * share * width * features, transcendentals=0, bytes_accessed=1 << 20),
    )

    half = channels // 2
    block_out, kept, given = call(
        functools.partial(tail_kernel, parts),
        (mask, own, *arrived, inputs_here, cached_here, gate, shift, scale, patch),
        [shaped((share, features), bf16), shaped((half, share), f32), shaped((half, share), f32)],
    )
    partner = lax.ppermute(given, "cfg", [(0, 1), (1, 0)])
    (block_out,) = call(
        store_kernel,
        (block_out,),
        [shaped((share, features), bf16)],
        out_specs=[HBM],
        scratch=[pltpu.SemaphoreType.DMA(())],
        limit=4,
    )
    (velocity,) = call(guide_kernel, (kept, partner), [shaped((half, share), f32)], limit=4)
    return (block_out[None], velocity.T)


def solution(mesh):
    in_specs = (
        P("cfg", "ctx", "tp"),
        P("cfg", "ctx", "tp"),
        P("cfg", "ctx", "tp"),
        P(),
        P(),
        P("cfg", ("ctx", "tp"), None),
        P("cfg", ("ctx", "tp"), None),
        P("cfg", "ctx"),
        P("cfg", None),
        P("tp", None),
        P("cfg", None),
        P("cfg", None),
        P(),
    )
    out_specs = (P("cfg", ("ctx", "tp"), None), P(("ctx", "tp"), "cfg"))
    return jax.shard_map(shards, mesh=mesh, in_specs=in_specs, out_specs=out_specs, check_vma=False)
```

```python
import functools
import math

import jax
import jax.numpy as jnp
from jax import lax
from jax.experimental import pallas as pl
from jax.experimental.pallas import tpu as pltpu
from jax.sharding import PartitionSpec as P


guidance_scale = 3.0
VMEM = pl.BlockSpec(memory_space=pltpu.VMEM)
HBM = pl.BlockSpec(memory_space=pltpu.HBM)
NT = (((1,), (1,)), ((), ()))


def in_hbm(value):
    return pltpu.with_memory_space_constraint(value, pltpu.HBM)


def dot_f32(a, b):
    return jnp.dot(a, b, preferred_element_type=jnp.float32)


def dot_nt(a, b):
    return lax.dot_general(a, b, NT, preferred_element_type=jnp.float32)


def live_lanes(mask_ref):
    return jnp.where(mask_ref[...] == 1, 0.0, 1.0)


def pick_matrix(mask_ref, live_count):
    live = live_lanes(mask_ref)
    count = live.shape[1]
    rows = lax.broadcasted_iota(jnp.int32, (count, count), 0)
    cols = lax.broadcasted_iota(jnp.int32, (count, count), 1)
    upto = jnp.where(rows <= cols, 1.0, 0.0).astype(jnp.bfloat16)
    wide = jnp.broadcast_to(live, (8, count)).astype(jnp.bfloat16)
    rank = dot_f32(wide, upto)[0:1]
    slot = lax.broadcasted_iota(jnp.int32, (live_count, count), 0).astype(jnp.float32)
    hit = (jnp.broadcast_to(rank, slot.shape) == slot + 1.0) & (jnp.broadcast_to(live, slot.shape) > 0.5)
    return jnp.where(hit, 1.0, 0.0).astype(jnp.bfloat16)


def place_matrix(mask_ref, live_count, first, share):
    live = live_lanes(mask_ref)
    count = live.shape[1]
    wide = jnp.broadcast_to(live, (live_count, count)).astype(jnp.bfloat16)
    rows = lax.broadcasted_iota(jnp.int32, (share, count), 0) + first
    cols = lax.broadcasted_iota(jnp.int32, (share, count), 1)
    rank = dot_nt(jnp.where(cols <= rows, 1.0, 0.0).astype(jnp.bfloat16), wide)
    alive = dot_nt(jnp.where(cols == rows, 1.0, 0.0).astype(jnp.bfloat16), wide)
    slot = lax.broadcasted_iota(jnp.int32, (share, live_count), 1).astype(jnp.float32)
    hit = (rank == slot + 1.0) & (alive > 0.5)
    return jnp.where(hit, 1.0, 0.0).astype(jnp.bfloat16)


def ring_place(members):
    return lax.rem(lax.axis_index("ctx"), members)


def unit_rows(raw, gain):
    lifted = raw.astype(jnp.float32)
    mean_square = jnp.mean(lifted * lifted, axis=-1, keepdims=True)
    return (lifted * lax.rsqrt(mean_square + 1e-06) * gain).astype(jnp.bfloat16)


def split_kernel(dims, k_hbm, v_hbm, *refs):
    members, width, depth = dims
    outs, sems = refs[:members], refs[members]
    count = k_hbm.shape[0]
    position = ring_place(members)
    copies = []
    for b in [b for b in range(1, members)] + [0]:
        columns = pl.ds(pl.multiple_of(lax.rem(position + b, members) * width, depth), width)
        for n, source in enumerate((k_hbm, v_hbm)):
            target = outs[b].at[pl.ds(n * count, count), :]
            copies.append(pltpu.make_async_copy(source.at[:, columns], target, sems.at[n, b]))
    for copy in copies:
        copy.start()
    for copy in copies:
        copy.wait()


def ask_kernel(dims, mask_hbm, gain_hbm, q_hbm, *refs):
    members, own_heads, depth, live_count = dims
    asks = refs[1 : members + 1]
    mask_ref, gain_ref, q_ref, small_sems, q_sems = refs[members + 1 :]
    width = own_heads * depth
    position = ring_place(members)
    small = [
        pltpu.make_async_copy(mask_hbm, mask_ref, small_sems.at[0]),
        pltpu.make_async_copy(gain_hbm, gain_ref, small_sems.at[1]),
    ]
    for copy in small:
        copy.start()
    order = [b for b in range(1, members)] + [0]
    loads = {}
    for b in order:
        columns = pl.ds(pl.multiple_of(lax.rem(position + b, members) * width, depth), width)
        loads[b] = pltpu.make_async_copy(q_hbm.at[:, columns], q_ref.at[b], q_sems.at[b])
        loads[b].start()
    for copy in small:
        copy.wait()
    picks = pick_matrix(mask_ref, live_count)
    gain = gain_ref[...]
    for b in order:
        loads[b].wait()
        picked = dot_f32(picks, q_ref[b])
        for h in range(own_heads):
            columns = slice(h * depth, (h + 1) * depth)
            asks[b][:, columns] = unit_rows(picked[:, columns], gain)


def unit_kernel(depth, gain_ref, *refs):
    pairs, out_ref = refs[:-1], refs[-1]
    count = out_ref.shape[0] // len(pairs)
    gain = gain_ref[...]
    for b, ref in enumerate(pairs):
        for first in range(0, out_ref.shape[1], depth):
            columns = slice(first, first + depth)
            out_ref[pl.ds(b * count, count), columns] = unit_rows(ref[pl.ds(0, count), columns], gain)


def fetch_kernel(dims, *refs):
    n, live_count, parts = dims
    sources, targets, places_ref, sems = refs[:n], refs[n + 1 : 2 * n + 1], refs[2 * n + 1], refs[2 * n + 2]
    copies = [pltpu.make_async_copy(s, t, sems.at[i]) for i, (s, t) in enumerate(zip(sources, targets))]
    for copy in copies:
        copy.start()
    mask_ref = targets[0]
    copies[0].wait()
    share = places_ref.shape[1]
    for s in range(parts):
        first = lax.rem(lax.axis_index("tp") + s, parts) * share
        places_ref[s] = place_matrix(mask_ref, live_count, first, share)
    for copy in copies[1:]:
        copy.wait()


def attend_kernel(dims, *refs):
    members, partial, own_heads, depth, live_count, count, stat_rows, sources = dims
    pairs, units_ref = refs[1 : members + 1], refs[members + 1]
    asks = refs[members + 2 : members + 2 + sources]
    outs, stats = refs[members + 2 + sources : -1], refs[-1]
    factor = depth ** (-0.5)
    power = factor * math.log2(math.e)
    lanes = lax.broadcasted_iota(jnp.int32, (live_count, stats.shape[2]), 1)
    if partial:
        stats[...] = jnp.zeros_like(stats)
    ones = jnp.ones((count, depth), jnp.bfloat16)
    for h in range(own_heads):
        columns = slice(h * depth, (h + 1) * depth)
        for s in range(sources):
            queries = asks[s][:, columns]
            scores = [dot_nt(queries, units_ref[pl.ds(b * count, count), columns]) for b in range(members)]
            biggest = jnp.max(functools.reduce(jnp.maximum, scores), axis=-1, keepdims=True)
            weights = [jnp.exp2((score - biggest) * power).astype(jnp.bfloat16) for score in scores]
            summed = functools.reduce(
                jnp.add,
                [
                    dot_f32(w, jnp.concatenate([ref[pl.ds(count, count), columns], ones], axis=1))
                    for w, ref in zip(weights, pairs)
                ],
            )
            totals = summed[:, depth : depth + 1]
            outs[s][pl.ds(h * live_count, live_count), :] = (summed[:, :depth] / totals).astype(jnp.bfloat16)
            if partial:
                rest = biggest * factor + jnp.log(totals)
                for piece in range(3):
                    rounded = rest.astype(jnp.bfloat16).astype(jnp.float32)
                    stats[s] = jnp.where(lanes == piece * own_heads + h, rounded, stats[s])
                    rest = rest - rounded
    if partial:
        for s in range(sources):
            turned = jnp.transpose(stats[s])[:stat_rows]
            outs[s][pl.ds(own_heads * live_count, stat_rows), :] = turned.astype(jnp.bfloat16)


def merge_kernel(dims, places_ref, weight_ref, *refs):
    members, groups, own_heads, depth, live_count, stat_rows, parts = dims
    sources = members * groups
    parcels = refs[:sources]
    sends = refs[sources : sources + parts - 1]
    own_ref, spread_ref = refs[sources + parts - 1 :]
    share = own_ref.shape[0]
    width = own_heads * depth
    position = ring_place(members)
    places = jnp.concatenate([places_ref[s] for s in range(parts)], axis=0)
    for b in range(members):
        held = [parcels[a * members + b] for a in range(groups)]
        if groups > 1:
            stats = [ref[pl.ds(own_heads * live_count, stat_rows), :].astype(jnp.float32) for ref in held]
        for h in range(own_heads):
            values = [ref[pl.ds(h * live_count, live_count), :] for ref in held]
            if groups > 1:
                logged = [
                    t[h : h + 1] + t[own_heads + h : own_heads + h + 1] + t[2 * own_heads + h : 2 * own_heads + h + 1]
                    for t in stats
                ]
                biggest = functools.reduce(jnp.maximum, logged)
                shares = [jnp.exp(l - biggest) for l in logged]
                total = functools.reduce(jnp.add, shares)
                spots = [places * (w / total).astype(jnp.bfloat16) for w in shares]
                placed = dot_f32(jnp.concatenate(spots, axis=1), jnp.concatenate(values, axis=0))
            else:
                placed = dot_f32(places, values[0])
            base = lax.rem(position + b, members) * width + h * depth
            spread_ref[:, pl.ds(pl.multiple_of(base, depth), depth)] = placed.astype(jnp.bfloat16)
    own_ref[...] = spread_ref[pl.ds(0, share), :]
    for s in range(1, parts):
        project(spread_ref[pl.ds(s * share, share), :], weight_ref, sends[s - 1])


def project(rows, weight_ref, out_ref):
    features = weight_ref.shape[1]
    tile = 512 if features % 512 == 0 else features
    for first in range(0, features, tile):
        columns = pl.ds(first, tile)
        out_ref[:, columns] = dot_f32(rows, weight_ref[:, columns]).astype(out_ref.dtype)


def project_kernel(rows_ref, weight_ref, out_ref):
    project(rows_ref[...], weight_ref, out_ref)


def tail_kernel(parts, mask_ref, own_ref, *refs):
    arrived = refs[: parts - 1]
    input_ref, cached_ref, gate_ref, shift_ref, scale_ref, patch_ref, block_ref, kept_ref, given_ref = refs[
        parts - 1 :
    ]
    projected = own_ref[...]
    for ref in arrived:
        projected = projected + ref[...].astype(jnp.float32)
    share = projected.shape[0]
    count = mask_ref.shape[1]
    first = lax.axis_index("tp") * share
    rows = lax.broadcasted_iota(jnp.int32, (share, count), 0) + first
    cols = lax.broadcasted_iota(jnp.int32, (share, count), 1)
    replayed = jnp.where((cols == rows) & (jnp.broadcast_to(mask_ref[...], rows.shape) == 1), 1.0, 0.0)
    replayed = jnp.sum(replayed, axis=-1, keepdims=True) > 0.5
    mixed = input_ref[...].astype(jnp.float32) + gate_ref[...] * projected
    block = jnp.where(replayed, cached_ref[...].astype(jnp.float32), mixed).astype(jnp.bfloat16)
    block_ref[...] = block
    lifted = block.astype(jnp.float32)
    centred = lifted - jnp.mean(lifted, axis=-1, keepdims=True)
    spread = jnp.mean(centred * centred, axis=-1, keepdims=True)
    normed = centred * lax.rsqrt(spread + 1e-06) * (1.0 + scale_ref[...]) + shift_ref[...]
    branch = dot_nt(patch_ref[...], normed.astype(jnp.bfloat16))
    half = branch.shape[0] // 2
    first_side = lax.axis_index("cfg") == 0
    kept_ref[...] = jnp.where(first_side, branch[:half], branch[half:])
    given_ref[...] = jnp.where(first_side, branch[half:], branch[:half])


def store_kernel(block_ref, out_hbm, sem):
    copy = pltpu.make_async_copy(block_ref, out_hbm, sem)
    copy.start()
    copy.wait()


def guide_kernel(kept_ref, partner_ref, out_ref):
    first_side = lax.axis_index("cfg") == 0
    cond = jnp.where(first_side, kept_ref[...], partner_ref[...])
    uncond = jnp.where(first_side, partner_ref[...], kept_ref[...])
    out_ref[...] = uncond + guidance_scale * (cond - uncond)


def shards(
    query_proj,
    key_proj,
    value_proj,
    query_gain,
    key_gain,
    block_input,
    cached_out,
    replay_mask,
    branch_gate,
    attn_weight,
    final_shift,
    final_scale,
    patch_weight,
):
    _, count, width = query_proj.shape
    depth = query_gain.shape[0]
    heads = width // depth
    features = attn_weight.shape[1]
    channels = patch_weight.shape[1]
    live_count = count // 2
    ring = lax.axis_size("ctx")
    parts = lax.axis_size("tp")
    share = count // parts
    members = math.gcd(heads, ring)
    groups = ring // members
    own_heads = heads // members
    own_width = own_heads * depth
    partial = groups > 1
    stat_rows = -(-3 * own_heads // 16) * 16

    def route(a, b, back):
        pairs = []
        for g in range(groups):
            for p in range(members):
                other = ((g + a) % groups) * members + (p + b) % members
                pairs.append((other, g * members + p) if back else (g * members + p, other))
        return pairs

    def call(kernel, inputs, outs, in_specs=None, out_specs=None, scratch=(), limit=24, cost=None):
        return pl.pallas_call(
            kernel,
            out_shape=outs,
            in_specs=in_specs or [VMEM] * len(inputs),
            out_specs=out_specs or [VMEM] * len(outs),
            scratch_shapes=scratch,
            compiler_params=pltpu.CompilerParams(vmem_limit_bytes=limit << 20),
            cost_estimate=cost,
        )(*inputs)

    bf16, f32 = jnp.bfloat16, jnp.float32
    shaped = jax.ShapeDtypeStruct
    pair_shape = shaped((2 * count, own_width), bf16)
    pairs = call(
        functools.partial(split_kernel, (members, own_width, depth)),
        (in_hbm(key_proj[0]), in_hbm(value_proj[0])),
        [pair_shape] * members,
        in_specs=[HBM] * 2,
        scratch=[pltpu.SemaphoreType.DMA((2, members))],
        limit=8,
    )
    pairs = [pairs[0]] + [lax.ppermute(pairs[b], "ctx", route(0, b, False)) for b in range(1, members)]
    asks = call(
        functools.partial(ask_kernel, (members, own_heads, depth, live_count)),
        (*map(in_hbm, (replay_mask, query_gain[None], query_proj[0])), pairs[0]),
        [shaped((live_count, own_width), bf16)] * members,
        in_specs=[HBM] * 3 + [VMEM],
        scratch=[
            pltpu.VMEM((1, count), jnp.int32),
            pltpu.VMEM((1, depth), f32),
            pltpu.VMEM((members, count, own_width), bf16),
            pltpu.SemaphoreType.DMA((2,)),
            pltpu.SemaphoreType.DMA((members,)),
        ],
        limit=16,
    )
    far_asks = [lax.ppermute(asks[b], "ctx", route(a, b, False)) for a in range(1, groups) for b in range(members)]
    near_asks = [asks[0]] + [lax.ppermute(asks[b], "ctx", route(0, b, False)) for b in range(1, members)]

    wanted = (
        replay_mask,
        key_gain[None],
        attn_weight,
        block_input[0],
        cached_out[0],
        branch_gate,
        final_shift,
        final_scale,
        patch_weight.T,
    )
    fetched = call(
        functools.partial(fetch_kernel, (len(wanted), live_count, parts)),
        (*map(in_hbm, wanted), asks[0]),
        [shaped(w.shape, w.dtype) for w in wanted] + [shaped((parts, share, live_count), bf16)],
        in_specs=[HBM] * len(wanted) + [VMEM],
        scratch=[pltpu.SemaphoreType.DMA((len(wanted),))],
        limit=16,
        cost=pl.CostEstimate(flops=0, transcendentals=0, bytes_accessed=2 * sum(w.size * w.dtype.itemsize for w in wanted)),
    )
    mask, key_gain_here, weight, inputs_here, cached_here, gate, shift, scale, patch, places = fetched

    parcel_rows = own_heads * live_count + (stat_rows if partial else 0)
    parcel_shape = shaped((parcel_rows, depth), bf16)

    (units,) = call(
        functools.partial(unit_kernel, depth),
        (key_gain_here, *pairs),
        [shaped((members * count, own_width), bf16)],
        cost=pl.CostEstimate(flops=0, transcendentals=0, bytes_accessed=1 << 20),
    )

    def attend(after, asks):
        scores = len(asks) * live_count * members * count * own_heads
        return call(
            functools.partial(
                attend_kernel,
                (members, partial, own_heads, depth, live_count, count, stat_rows, len(asks)),
            ),
            (after, *pairs, units, *asks),
            [parcel_shape] * len(asks),
            scratch=[pltpu.VMEM((len(asks), live_count, live_count), f32)],
            cost=pl.CostEstimate(flops=4 * scores * depth, transcendentals=scores, bytes_accessed=1 << 20),
        )

    after, distant = mask, []
    pieces = 2
    for piece in range(pieces):
        low, high = (piece * len(far_asks) // pieces, (piece + 1) * len(far_asks) // pieces)
        if low == high:
            continue
        far = attend(after, far_asks[low:high])
        after = far[0]
        distant += [
            lax.ppermute(far[n - low], "ctx", route(1 + n // members, n % members, True))
            for n in range(low, high)
        ]
    near = attend(after, near_asks)
    parcels = [near[0]] + [lax.ppermute(near[b], "ctx", route(0, b, True)) for b in range(1, members)] + distant

    merged = call(
        functools.partial(merge_kernel, (members, groups, own_heads, depth, live_count, stat_rows, parts)),
        (places, weight, *parcels),
        [shaped((share, features), bf16)] * (parts - 1) + [shaped((share, width), bf16)],
        scratch=[pltpu.VMEM((count, width), bf16)],
    )
    arrived = [
        lax.ppermute(merged[s - 1], "tp", [(i, (i + s) % parts) for i in range(parts)]) for s in range(1, parts)
    ]
    (own,) = call(
        project_kernel,
        (merged[-1], weight),
        [shaped((share, features), f32)],
        cost=pl.CostEstimate(flops=2 * share * width * features, transcendentals=0, bytes_accessed=1 << 20),
    )

    half = channels // 2
    block_out, kept, given = call(
        functools.partial(tail_kernel, parts),
        (mask, own, *arrived, inputs_here, cached_here, gate, shift, scale, patch),
        [shaped((share, features), bf16), shaped((half, share), f32), shaped((half, share), f32)],
    )
    partner = lax.ppermute(given, "cfg", [(0, 1), (1, 0)])
    (block_out,) = call(
        store_kernel,
        (block_out,),
        [shaped((share, features), bf16)],
        out_specs=[HBM],
        scratch=[pltpu.SemaphoreType.DMA(())],
        limit=4,
    )
    (velocity,) = call(guide_kernel, (kept, partner), [shaped((half, share), f32)], limit=4)
    return (block_out[None], velocity.T)


def solution(mesh):
    in_specs = (
        P("cfg", "ctx", "tp"),
        P("cfg", "ctx", "tp"),
        P("cfg", "ctx", "tp"),
        P(),
        P(),
        P("cfg", ("ctx", "tp"), None),
        P("cfg", ("ctx", "tp"), None),
        P("cfg", "ctx"),
        P("cfg", None),
        P("tp", None),
        P("cfg", None),
        P("cfg", None),
        P(),
    )
    out_specs = (P("cfg", ("ctx", "tp"), None), P(("ctx", "tp"), "cfg"))
    return jax.shard_map(shards, mesh=mesh, in_specs=in_specs, out_specs=out_specs, check_vma=False)
```

```python
import functools
import math

import jax
import jax.numpy as jnp
from jax import lax
from jax.experimental import pallas as pl
from jax.experimental.pallas import tpu as pltpu
from jax.sharding import PartitionSpec as P


guidance_scale = 3.0
VMEM = pl.BlockSpec(memory_space=pltpu.VMEM)
HBM = pl.BlockSpec(memory_space=pltpu.HBM)
NT = (((1,), (1,)), ((), ()))


def in_hbm(value):
    return pltpu.with_memory_space_constraint(value, pltpu.HBM)


def dot_f32(a, b):
    return jnp.dot(a, b, preferred_element_type=jnp.float32)


def dot_nt(a, b):
    return lax.dot_general(a, b, NT, preferred_element_type=jnp.float32)


def live_lanes(mask_ref):
    return jnp.where(mask_ref[...] == 1, 0.0, 1.0)


def pick_matrix(mask_ref, live_count):
    live = live_lanes(mask_ref)
    count = live.shape[1]
    rows = lax.broadcasted_iota(jnp.int32, (count, count), 0)
    cols = lax.broadcasted_iota(jnp.int32, (count, count), 1)
    upto = jnp.where(rows <= cols, 1.0, 0.0).astype(jnp.bfloat16)
    wide = jnp.broadcast_to(live, (8, count)).astype(jnp.bfloat16)
    rank = dot_f32(wide, upto)[0:1]
    slot = lax.broadcasted_iota(jnp.int32, (live_count, count), 0).astype(jnp.float32)
    hit = (jnp.broadcast_to(rank, slot.shape) == slot + 1.0) & (jnp.broadcast_to(live, slot.shape) > 0.5)
    return jnp.where(hit, 1.0, 0.0).astype(jnp.bfloat16)


def place_matrix(mask_ref, live_count, first, share):
    live = live_lanes(mask_ref)
    count = live.shape[1]
    wide = jnp.broadcast_to(live, (live_count, count)).astype(jnp.bfloat16)
    rows = lax.broadcasted_iota(jnp.int32, (share, count), 0) + first
    cols = lax.broadcasted_iota(jnp.int32, (share, count), 1)
    rank = dot_nt(jnp.where(cols <= rows, 1.0, 0.0).astype(jnp.bfloat16), wide)
    alive = dot_nt(jnp.where(cols == rows, 1.0, 0.0).astype(jnp.bfloat16), wide)
    slot = lax.broadcasted_iota(jnp.int32, (share, live_count), 1).astype(jnp.float32)
    hit = (rank == slot + 1.0) & (alive > 0.5)
    return jnp.where(hit, 1.0, 0.0).astype(jnp.bfloat16)


def hop(place, step, size):
    return place ^ step if size & (size - 1) == 0 else (place + step) % size


def ring_place(members):
    return lax.rem(lax.axis_index("ctx"), members)


def unit_rows(raw, gain):
    lifted = raw.astype(jnp.float32)
    mean_square = jnp.mean(lifted * lifted, axis=-1, keepdims=True)
    return (lifted * lax.rsqrt(mean_square + 1e-06) * gain).astype(jnp.bfloat16)


def split_kernel(dims, k_hbm, v_hbm, *refs):
    members, width, depth = dims
    outs, sems = refs[:members], refs[members]
    count = k_hbm.shape[0]
    position = ring_place(members)
    copies = []
    for b in [b for b in range(1, members)] + [0]:
        columns = pl.ds(pl.multiple_of(hop(position, b, members) * width, depth), width)
        for n, source in enumerate((k_hbm, v_hbm)):
            target = outs[b].at[pl.ds(n * count, count), :]
            copies.append(pltpu.make_async_copy(source.at[:, columns], target, sems.at[n, b]))
    for copy in copies:
        copy.start()
    for copy in copies:
        copy.wait()


def ask_kernel(dims, mask_hbm, gain_hbm, q_hbm, *refs):
    members, own_heads, depth, live_count = dims
    asks = refs[1 : members + 1]
    mask_ref, gain_ref, q_ref, small_sems, q_sems = refs[members + 1 :]
    width = own_heads * depth
    position = ring_place(members)
    small = [
        pltpu.make_async_copy(mask_hbm, mask_ref, small_sems.at[0]),
        pltpu.make_async_copy(gain_hbm, gain_ref, small_sems.at[1]),
    ]
    for copy in small:
        copy.start()
    order = [b for b in range(1, members)] + [0]
    loads = {}
    for b in order:
        columns = pl.ds(pl.multiple_of(hop(position, b, members) * width, depth), width)
        loads[b] = pltpu.make_async_copy(q_hbm.at[:, columns], q_ref.at[b], q_sems.at[b])
        loads[b].start()
    for copy in small:
        copy.wait()
    picks = pick_matrix(mask_ref, live_count)
    gain = gain_ref[...]
    for b in order:
        loads[b].wait()
        picked = dot_f32(picks, q_ref[b])
        for h in range(own_heads):
            columns = slice(h * depth, (h + 1) * depth)
            asks[b][:, columns] = unit_rows(picked[:, columns], gain)


def unit_kernel(depth, gain_ref, pair_ref, out_ref):
    count = out_ref.shape[0]
    for first in range(0, out_ref.shape[1], depth):
        columns = slice(first, first + depth)
        out_ref[:, columns] = unit_rows(pair_ref[pl.ds(0, count), columns], gain_ref[...])


def fetch_kernel(dims, *refs):
    n, live_count, parts = dims
    sources, targets, places_ref, sems = refs[:n], refs[n + 1 : 2 * n + 1], refs[2 * n + 1], refs[2 * n + 2]
    copies = [pltpu.make_async_copy(s, t, sems.at[i]) for i, (s, t) in enumerate(zip(sources, targets))]
    for copy in copies:
        copy.start()
    mask_ref = targets[0]
    copies[0].wait()
    share = places_ref.shape[1]
    for s in range(parts):
        first = lax.rem(lax.axis_index("tp") + s, parts) * share
        places_ref[s] = place_matrix(mask_ref, live_count, first, share)
    for copy in copies[1:]:
        copy.wait()


def attend_kernel(dims, *refs):
    members, partial, own_heads, depth, live_count, count, stat_rows, sources = dims
    pairs, units = refs[1 : members + 1], refs[members + 1 : 2 * members + 1]
    asks = refs[2 * members + 1 : 2 * members + 1 + sources]
    outs, stats = refs[2 * members + 1 + sources : -1], refs[-1]
    factor = depth ** (-0.5)
    power = factor * math.log2(math.e)
    lanes = lax.broadcasted_iota(jnp.int32, (live_count, stats.shape[2]), 1)
    if partial:
        stats[...] = jnp.zeros_like(stats)
    ones = jnp.ones((count, depth), jnp.bfloat16)
    for h in range(own_heads):
        columns = slice(h * depth, (h + 1) * depth)
        for s in range(sources):
            queries = asks[s][:, columns]
            scores = [dot_nt(queries, unit[:, columns]) for unit in units]
            biggest = jnp.max(functools.reduce(jnp.maximum, scores), axis=-1, keepdims=True)
            weights = [jnp.exp2((score - biggest) * power).astype(jnp.bfloat16) for score in scores]
            summed = functools.reduce(
                jnp.add,
                [
                    dot_f32(w, jnp.concatenate([ref[pl.ds(count, count), columns], ones], axis=1))
                    for w, ref in zip(weights, pairs)
                ],
            )
            totals = summed[:, depth : depth + 1]
            outs[s][pl.ds(h * live_count, live_count), :] = (summed[:, :depth] / totals).astype(jnp.bfloat16)
            if partial:
                rest = biggest * factor + jnp.log(totals)
                for piece in range(3):
                    rounded = rest.astype(jnp.bfloat16).astype(jnp.float32)
                    stats[s] = jnp.where(lanes == piece * own_heads + h, rounded, stats[s])
                    rest = rest - rounded
    if partial:
        for s in range(sources):
            turned = jnp.transpose(stats[s])[:stat_rows]
            outs[s][pl.ds(own_heads * live_count, stat_rows), :] = turned.astype(jnp.bfloat16)


def merge_kernel(dims, places_ref, weight_ref, *refs):
    members, groups, own_heads, depth, live_count, stat_rows, parts = dims
    sources = members * groups
    parcels = refs[:sources]
    sends = refs[sources : sources + parts - 1]
    own_ref, spread_ref = refs[sources + parts - 1 :]
    share = own_ref.shape[0]
    width = own_heads * depth
    position = ring_place(members)
    places = jnp.concatenate([places_ref[s] for s in range(parts)], axis=0)
    for b in range(members):
        held = [parcels[a * members + b] for a in range(groups)]
        if groups > 1:
            stats = [ref[pl.ds(own_heads * live_count, stat_rows), :].astype(jnp.float32) for ref in held]
        for h in range(own_heads):
            values = [ref[pl.ds(h * live_count, live_count), :] for ref in held]
            if groups > 1:
                logged = [
                    t[h : h + 1] + t[own_heads + h : own_heads + h + 1] + t[2 * own_heads + h : 2 * own_heads + h + 1]
                    for t in stats
                ]
                biggest = functools.reduce(jnp.maximum, logged)
                shares = [jnp.exp(l - biggest) for l in logged]
                total = functools.reduce(jnp.add, shares)
                spots = [places * (w / total).astype(jnp.bfloat16) for w in shares]
                placed = dot_f32(jnp.concatenate(spots, axis=1), jnp.concatenate(values, axis=0))
            else:
                placed = dot_f32(places, values[0])
            base = hop(position, b, members) * width + h * depth
            spread_ref[:, pl.ds(pl.multiple_of(base, depth), depth)] = placed.astype(jnp.bfloat16)
    own_ref[...] = spread_ref[pl.ds(0, share), :]
    for s in range(1, parts):
        project(spread_ref[pl.ds(s * share, share), :], weight_ref, sends[s - 1])


def project(rows, weight_ref, out_ref):
    features = weight_ref.shape[1]
    tile = 512 if features % 512 == 0 else features
    for first in range(0, features, tile):
        columns = pl.ds(first, tile)
        out_ref[:, columns] = dot_f32(rows, weight_ref[:, columns]).astype(out_ref.dtype)


def project_kernel(rows_ref, weight_ref, out_ref):
    project(rows_ref[...], weight_ref, out_ref)


def tail_kernel(parts, mask_ref, own_ref, *refs):
    arrived = refs[: parts - 1]
    input_ref, cached_ref, gate_ref, shift_ref, scale_ref, patch_ref, block_ref, kept_ref, given_ref = refs[
        parts - 1 :
    ]
    projected = own_ref[...]
    for ref in arrived:
        projected = projected + ref[...].astype(jnp.float32)
    share = projected.shape[0]
    count = mask_ref.shape[1]
    first = lax.axis_index("tp") * share
    rows = lax.broadcasted_iota(jnp.int32, (share, count), 0) + first
    cols = lax.broadcasted_iota(jnp.int32, (share, count), 1)
    replayed = jnp.where((cols == rows) & (jnp.broadcast_to(mask_ref[...], rows.shape) == 1), 1.0, 0.0)
    replayed = jnp.sum(replayed, axis=-1, keepdims=True) > 0.5
    mixed = input_ref[...].astype(jnp.float32) + gate_ref[...] * projected
    block = jnp.where(replayed, cached_ref[...].astype(jnp.float32), mixed).astype(jnp.bfloat16)
    block_ref[...] = block
    lifted = block.astype(jnp.float32)
    centred = lifted - jnp.mean(lifted, axis=-1, keepdims=True)
    spread = jnp.mean(centred * centred, axis=-1, keepdims=True)
    normed = centred * lax.rsqrt(spread + 1e-06) * (1.0 + scale_ref[...]) + shift_ref[...]
    branch = dot_nt(patch_ref[...], normed.astype(jnp.bfloat16))
    half = branch.shape[0] // 2
    first_side = lax.axis_index("cfg") == 0
    kept_ref[...] = jnp.where(first_side, branch[:half], branch[half:])
    given_ref[...] = jnp.where(first_side, branch[half:], branch[:half])


def store_kernel(block_ref, out_hbm, sem):
    copy = pltpu.make_async_copy(block_ref, out_hbm, sem)
    copy.start()
    copy.wait()


def guide_kernel(kept_ref, partner_ref, out_ref):
    first_side = lax.axis_index("cfg") == 0
    cond = jnp.where(first_side, kept_ref[...], partner_ref[...])
    uncond = jnp.where(first_side, partner_ref[...], kept_ref[...])
    out_ref[...] = uncond + guidance_scale * (cond - uncond)


def shards(
    query_proj,
    key_proj,
    value_proj,
    query_gain,
    key_gain,
    block_input,
    cached_out,
    replay_mask,
    branch_gate,
    attn_weight,
    final_shift,
    final_scale,
    patch_weight,
):
    _, count, width = query_proj.shape
    depth = query_gain.shape[0]
    heads = width // depth
    features = attn_weight.shape[1]
    channels = patch_weight.shape[1]
    live_count = count // 2
    ring = lax.axis_size("ctx")
    parts = lax.axis_size("tp")
    share = count // parts
    members = math.gcd(heads, ring)
    groups = ring // members
    own_heads = heads // members
    own_width = own_heads * depth
    partial = groups > 1
    stat_rows = -(-3 * own_heads // 16) * 16

    def route(a, b, back):
        pairs = []
        for g in range(groups):
            for p in range(members):
                other = hop(g, a, groups) * members + hop(p, b, members)
                pairs.append((other, g * members + p) if back else (g * members + p, other))
        return pairs

    def call(kernel, inputs, outs, in_specs=None, out_specs=None, scratch=(), limit=24, cost=None):
        return pl.pallas_call(
            kernel,
            out_shape=outs,
            in_specs=in_specs or [VMEM] * len(inputs),
            out_specs=out_specs or [VMEM] * len(outs),
            scratch_shapes=scratch,
            compiler_params=pltpu.CompilerParams(vmem_limit_bytes=limit << 20),
            cost_estimate=cost,
        )(*inputs)

    bf16, f32 = jnp.bfloat16, jnp.float32
    shaped = jax.ShapeDtypeStruct
    pair_shape = shaped((2 * count, own_width), bf16)
    pairs = call(
        functools.partial(split_kernel, (members, own_width, depth)),
        (in_hbm(key_proj[0]), in_hbm(value_proj[0])),
        [pair_shape] * members,
        in_specs=[HBM] * 2,
        scratch=[pltpu.SemaphoreType.DMA((2, members))],
        limit=8,
    )
    pairs = list(pairs)
    pair_order = sorted(range(1, members), key=lambda b: (b < members // 2, b))
    for b in pair_order:
        pairs[b] = lax.ppermute(pairs[b], "ctx", route(0, b, False))
    asks = call(
        functools.partial(ask_kernel, (members, own_heads, depth, live_count)),
        (*map(in_hbm, (replay_mask, query_gain[None], query_proj[0])), pairs[0]),
        [shaped((live_count, own_width), bf16)] * members,
        in_specs=[HBM] * 3 + [VMEM],
        scratch=[
            pltpu.VMEM((1, count), jnp.int32),
            pltpu.VMEM((1, depth), f32),
            pltpu.VMEM((members, count, own_width), bf16),
            pltpu.SemaphoreType.DMA((2,)),
            pltpu.SemaphoreType.DMA((members,)),
        ],
        limit=16,
    )
    pieces = 2
    far_routes = sorted(((a, b) for a in range(1, groups) for b in range(members)), key=lambda r: (r[1] % 2, r))
    cuts = [piece * len(far_routes) // pieces for piece in range(pieces + 1)]
    far_asks = []
    for a, b in far_routes:
        far_asks.append(lax.ppermute(asks[b], "ctx", route(a, b, False)))
    near_asks = [asks[0]] + [lax.ppermute(asks[b], "ctx", route(0, b, False)) for b in range(1, members)]

    wanted = (
        replay_mask,
        key_gain[None],
        attn_weight,
        block_input[0],
        cached_out[0],
        branch_gate,
        final_shift,
        final_scale,
        patch_weight.T,
    )
    fetched = call(
        functools.partial(fetch_kernel, (len(wanted), live_count, parts)),
        (*map(in_hbm, wanted), asks[0]),
        [shaped(w.shape, w.dtype) for w in wanted] + [shaped((parts, share, live_count), bf16)],
        in_specs=[HBM] * len(wanted) + [VMEM],
        scratch=[pltpu.SemaphoreType.DMA((len(wanted),))],
        limit=16,
        cost=pl.CostEstimate(flops=0, transcendentals=0, bytes_accessed=2 * sum(w.size * w.dtype.itemsize for w in wanted)),
    )
    mask, key_gain_here, weight, inputs_here, cached_here, gate, shift, scale, patch, places = fetched

    parcel_rows = own_heads * live_count + (stat_rows if partial else 0)
    parcel_shape = shaped((parcel_rows, depth), bf16)

    units = [
        call(
            functools.partial(unit_kernel, depth),
            (key_gain_here, pair),
            [shaped((count, own_width), bf16)],
            cost=pl.CostEstimate(flops=0, transcendentals=0, bytes_accessed=1 << 18),
        )[0]
        for pair in pairs
    ]

    def attend(after, asks):
        scores = len(asks) * live_count * members * count * own_heads
        return call(
            functools.partial(
                attend_kernel,
                (members, partial, own_heads, depth, live_count, count, stat_rows, len(asks)),
            ),
            (after, *pairs, *units, *asks),
            [parcel_shape] * len(asks),
            scratch=[pltpu.VMEM((len(asks), live_count, live_count), f32)],
            cost=pl.CostEstimate(flops=4 * scores * depth, transcendentals=scores, bytes_accessed=1 << 20),
        )

    after = mask
    parcels = {}
    for piece in range(pieces):
        low, high = cuts[piece], cuts[piece + 1]
        if low == high:
            continue
        far = attend(after, far_asks[low:high])
        after = far[0]
        for n in range(low, high):
            parcels[far_routes[n]] = lax.ppermute(far[n - low], "ctx", route(*far_routes[n], True))
    near = attend(after, near_asks)
    parcels[0, 0] = near[0]
    for b in range(1, members):
        parcels[0, b] = lax.ppermute(near[b], "ctx", route(0, b, True))
    parcels = [parcels[a, b] for a in range(groups) for b in range(members)]

    merged = call(
        functools.partial(merge_kernel, (members, groups, own_heads, depth, live_count, stat_rows, parts)),
        (places, weight, *parcels),
        [shaped((share, features), bf16)] * (parts - 1) + [shaped((share, width), bf16)],
        scratch=[pltpu.VMEM((count, width), bf16)],
    )
    arrived = [
        lax.ppermute(merged[s - 1], "tp", [(i, (i + s) % parts) for i in range(parts)]) for s in range(1, parts)
    ]
    (own,) = call(
        project_kernel,
        (merged[-1], weight),
        [shaped((share, features), f32)],
        cost=pl.CostEstimate(flops=2 * share * width * features, transcendentals=0, bytes_accessed=1 << 20),
    )

    half = channels // 2
    block_out, kept, given = call(
        functools.partial(tail_kernel, parts),
        (mask, own, *arrived, inputs_here, cached_here, gate, shift, scale, patch),
        [shaped((share, features), bf16), shaped((half, share), f32), shaped((half, share), f32)],
    )
    partner = lax.ppermute(given, "cfg", [(0, 1), (1, 0)])
    (block_out,) = call(
        store_kernel,
        (block_out,),
        [shaped((share, features), bf16)],
        out_specs=[HBM],
        scratch=[pltpu.SemaphoreType.DMA(())],
        limit=4,
    )
    (velocity,) = call(guide_kernel, (kept, partner), [shaped((half, share), f32)], limit=4)
    return (block_out[None], velocity.T)


def solution(mesh):
    in_specs = (
        P("cfg", "ctx", "tp"),
        P("cfg", "ctx", "tp"),
        P("cfg", "ctx", "tp"),
        P(),
        P(),
        P("cfg", ("ctx", "tp"), None),
        P("cfg", ("ctx", "tp"), None),
        P("cfg", "ctx"),
        P("cfg", None),
        P("tp", None),
        P("cfg", None),
        P("cfg", None),
        P(),
    )
    out_specs = (P("cfg", ("ctx", "tp"), None), P(("ctx", "tp"), "cfg"))
    return jax.shard_map(shards, mesh=mesh, in_specs=in_specs, out_specs=out_specs, check_vma=False)
```

```python
import functools
import math

import jax
import jax.numpy as jnp
from jax import lax
from jax.experimental import pallas as pl
from jax.experimental.pallas import tpu as pltpu
from jax.sharding import PartitionSpec as P


guidance_scale = 3.0
VMEM = pl.BlockSpec(memory_space=pltpu.VMEM)
HBM = pl.BlockSpec(memory_space=pltpu.HBM)
NT = (((1,), (1,)), ((), ()))


def in_hbm(value):
    return pltpu.with_memory_space_constraint(value, pltpu.HBM)


def dot_f32(a, b):
    return jnp.dot(a, b, preferred_element_type=jnp.float32)


def dot_nt(a, b):
    return lax.dot_general(a, b, NT, preferred_element_type=jnp.float32)


def live_lanes(mask_ref):
    return jnp.where(mask_ref[...] == 1, 0.0, 1.0)


def pick_matrix(mask_ref, live_count):
    live = live_lanes(mask_ref)
    count = live.shape[1]
    rows = lax.broadcasted_iota(jnp.int32, (count, count), 0)
    cols = lax.broadcasted_iota(jnp.int32, (count, count), 1)
    upto = jnp.where(rows <= cols, 1.0, 0.0).astype(jnp.bfloat16)
    wide = jnp.broadcast_to(live, (8, count)).astype(jnp.bfloat16)
    rank = dot_f32(wide, upto)[0:1]
    slot = lax.broadcasted_iota(jnp.int32, (live_count, count), 0).astype(jnp.float32)
    hit = (jnp.broadcast_to(rank, slot.shape) == slot + 1.0) & (jnp.broadcast_to(live, slot.shape) > 0.5)
    return jnp.where(hit, 1.0, 0.0).astype(jnp.bfloat16)


def place_matrix(mask_ref, live_count, first, share):
    live = live_lanes(mask_ref)
    count = live.shape[1]
    wide = jnp.broadcast_to(live, (live_count, count)).astype(jnp.bfloat16)
    rows = lax.broadcasted_iota(jnp.int32, (share, count), 0) + first
    cols = lax.broadcasted_iota(jnp.int32, (share, count), 1)
    rank = dot_nt(jnp.where(cols <= rows, 1.0, 0.0).astype(jnp.bfloat16), wide)
    alive = dot_nt(jnp.where(cols == rows, 1.0, 0.0).astype(jnp.bfloat16), wide)
    slot = lax.broadcasted_iota(jnp.int32, (share, live_count), 1).astype(jnp.float32)
    hit = (rank == slot + 1.0) & (alive > 0.5)
    return jnp.where(hit, 1.0, 0.0).astype(jnp.bfloat16)


def hop(place, step, size):
    return place ^ step if size & (size - 1) == 0 else (place + step) % size


def ring_place(members):
    return lax.rem(lax.axis_index("ctx"), members)


def unit_rows(raw, gain):
    lifted = raw.astype(jnp.float32)
    mean_square = jnp.mean(lifted * lifted, axis=-1, keepdims=True)
    return (lifted * lax.rsqrt(mean_square + 1e-06) * gain).astype(jnp.bfloat16)


def split_kernel(dims, k_hbm, v_hbm, *refs):
    members, width, depth = dims
    outs, sems = refs[:members], refs[members]
    count = k_hbm.shape[0]
    position = ring_place(members)
    copies = []
    for b in [b for b in range(1, members)] + [0]:
        columns = pl.ds(pl.multiple_of(hop(position, b, members) * width, depth), width)
        for n, source in enumerate((k_hbm, v_hbm)):
            target = outs[b].at[pl.ds(n * count, count), :]
            copies.append(pltpu.make_async_copy(source.at[:, columns], target, sems.at[n, b]))
    for copy in copies:
        copy.start()
    for copy in copies:
        copy.wait()


def ask_kernel(dims, mask_hbm, gain_hbm, q_hbm, *refs):
    members, own_heads, depth, live_count = dims
    asks = refs[1 : members + 1]
    mask_ref, gain_ref, q_ref, small_sems, q_sems = refs[members + 1 :]
    width = own_heads * depth
    position = ring_place(members)
    small = [
        pltpu.make_async_copy(mask_hbm, mask_ref, small_sems.at[0]),
        pltpu.make_async_copy(gain_hbm, gain_ref, small_sems.at[1]),
    ]
    for copy in small:
        copy.start()
    order = [b for b in range(1, members)] + [0]
    loads = {}
    for b in order:
        columns = pl.ds(pl.multiple_of(hop(position, b, members) * width, depth), width)
        loads[b] = pltpu.make_async_copy(q_hbm.at[:, columns], q_ref.at[b], q_sems.at[b])
        loads[b].start()
    for copy in small:
        copy.wait()
    picks = pick_matrix(mask_ref, live_count)
    gain = gain_ref[...]
    for b in order:
        loads[b].wait()
        picked = dot_f32(picks, q_ref[b])
        for h in range(own_heads):
            columns = slice(h * depth, (h + 1) * depth)
            asks[b][:, columns] = unit_rows(picked[:, columns], gain)


def unit_kernel(depth, gain_ref, pair_ref, out_ref):
    count = out_ref.shape[0]
    for first in range(0, out_ref.shape[1], depth):
        columns = slice(first, first + depth)
        out_ref[:, columns] = unit_rows(pair_ref[pl.ds(0, count), columns], gain_ref[...])


def fetch_kernel(dims, *refs):
    n, live_count, parts = dims
    sources, targets, places_ref, sems = refs[:n], refs[n + 1 : 2 * n + 1], refs[2 * n + 1], refs[2 * n + 2]
    copies = [pltpu.make_async_copy(s, t, sems.at[i]) for i, (s, t) in enumerate(zip(sources, targets))]
    for copy in copies:
        copy.start()
    mask_ref = targets[0]
    copies[0].wait()
    share = places_ref.shape[1]
    for s in range(parts):
        first = lax.rem(lax.axis_index("tp") + s, parts) * share
        places_ref[s] = place_matrix(mask_ref, live_count, first, share)
    for copy in copies[1:]:
        copy.wait()


def attend_kernel(dims, *refs):
    members, partial, own_heads, depth, live_count, count, stat_rows, sources = dims
    pairs, units = refs[1 : members + 1], refs[members + 1 : 2 * members + 1]
    asks = refs[2 * members + 1 : 2 * members + 1 + sources]
    outs, stats = refs[2 * members + 1 + sources : -1], refs[-1]
    factor = depth ** (-0.5)
    power = factor * math.log2(math.e)
    lanes = lax.broadcasted_iota(jnp.int32, (live_count, stats.shape[2]), 1)
    if partial:
        stats[...] = jnp.zeros_like(stats)
    ones = jnp.ones((count, depth), jnp.bfloat16)
    for h in range(own_heads):
        columns = slice(h * depth, (h + 1) * depth)
        for s in range(sources):
            queries = asks[s][:, columns]
            scores = [dot_nt(queries, unit[:, columns]) for unit in units]
            biggest = jnp.max(functools.reduce(jnp.maximum, scores), axis=-1, keepdims=True)
            weights = [jnp.exp2((score - biggest) * power).astype(jnp.bfloat16) for score in scores]
            summed = functools.reduce(
                jnp.add,
                [
                    dot_f32(w, jnp.concatenate([ref[pl.ds(count, count), columns], ones], axis=1))
                    for w, ref in zip(weights, pairs)
                ],
            )
            totals = summed[:, depth : depth + 1]
            outs[s][pl.ds(h * live_count, live_count), :] = (summed[:, :depth] / totals).astype(jnp.bfloat16)
            if partial:
                rest = biggest * factor + jnp.log(totals)
                for piece in range(3):
                    rounded = rest.astype(jnp.bfloat16).astype(jnp.float32)
                    stats[s] = jnp.where(lanes == piece * own_heads + h, rounded, stats[s])
                    rest = rest - rounded
    if partial:
        for s in range(sources):
            turned = jnp.transpose(stats[s])[:stat_rows]
            outs[s][pl.ds(own_heads * live_count, stat_rows), :] = turned.astype(jnp.bfloat16)


def merge_kernel(dims, places_ref, weight_ref, *refs):
    members, groups, own_heads, depth, live_count, stat_rows, parts = dims
    sources = members * groups
    parcels = refs[:sources]
    sends = refs[sources : sources + parts - 1]
    own_ref, spread_ref = refs[sources + parts - 1 :]
    share = own_ref.shape[0]
    width = own_heads * depth
    position = ring_place(members)
    places = jnp.concatenate([places_ref[s] for s in range(parts)], axis=0)
    for b in range(members):
        held = [parcels[a * members + b] for a in range(groups)]
        if groups > 1:
            stats = [ref[pl.ds(own_heads * live_count, stat_rows), :].astype(jnp.float32) for ref in held]
        for h in range(own_heads):
            values = [ref[pl.ds(h * live_count, live_count), :] for ref in held]
            if groups > 1:
                logged = [
                    t[h : h + 1] + t[own_heads + h : own_heads + h + 1] + t[2 * own_heads + h : 2 * own_heads + h + 1]
                    for t in stats
                ]
                biggest = functools.reduce(jnp.maximum, logged)
                shares = [jnp.exp(l - biggest) for l in logged]
                total = functools.reduce(jnp.add, shares)
                spots = [places * (w / total).astype(jnp.bfloat16) for w in shares]
                placed = dot_f32(jnp.concatenate(spots, axis=1), jnp.concatenate(values, axis=0))
            else:
                placed = dot_f32(places, values[0])
            base = hop(position, b, members) * width + h * depth
            spread_ref[:, pl.ds(pl.multiple_of(base, depth), depth)] = placed.astype(jnp.bfloat16)
    own_ref[...] = spread_ref[pl.ds(0, share), :]
    for s in range(1, parts):
        project(spread_ref[pl.ds(s * share, share), :], weight_ref, sends[s - 1])


def project(rows, weight_ref, out_ref):
    features = weight_ref.shape[1]
    tile = 512 if features % 512 == 0 else features
    for first in range(0, features, tile):
        columns = pl.ds(first, tile)
        out_ref[:, columns] = dot_f32(rows, weight_ref[:, columns]).astype(out_ref.dtype)


def project_kernel(rows_ref, weight_ref, out_ref):
    project(rows_ref[...], weight_ref, out_ref)


def tail_kernel(parts, mask_ref, own_ref, *refs):
    arrived = refs[: parts - 1]
    input_ref, cached_ref, gate_ref, shift_ref, scale_ref, patch_ref, block_ref, kept_ref, given_ref = refs[
        parts - 1 :
    ]
    projected = own_ref[...]
    for ref in arrived:
        projected = projected + ref[...].astype(jnp.float32)
    share = projected.shape[0]
    count = mask_ref.shape[1]
    first = lax.axis_index("tp") * share
    rows = lax.broadcasted_iota(jnp.int32, (share, count), 0) + first
    cols = lax.broadcasted_iota(jnp.int32, (share, count), 1)
    replayed = jnp.where((cols == rows) & (jnp.broadcast_to(mask_ref[...], rows.shape) == 1), 1.0, 0.0)
    replayed = jnp.sum(replayed, axis=-1, keepdims=True) > 0.5
    mixed = input_ref[...].astype(jnp.float32) + gate_ref[...] * projected
    block = jnp.where(replayed, cached_ref[...].astype(jnp.float32), mixed).astype(jnp.bfloat16)
    block_ref[...] = block
    lifted = block.astype(jnp.float32)
    centred = lifted - jnp.mean(lifted, axis=-1, keepdims=True)
    spread = jnp.mean(centred * centred, axis=-1, keepdims=True)
    normed = centred * lax.rsqrt(spread + 1e-06) * (1.0 + scale_ref[...]) + shift_ref[...]
    branch = dot_nt(patch_ref[...], normed.astype(jnp.bfloat16))
    half = branch.shape[0] // 2
    first_side = lax.axis_index("cfg") == 0
    kept_ref[...] = jnp.where(first_side, branch[:half], branch[half:])
    given_ref[...] = jnp.where(first_side, branch[half:], branch[:half])


def store_kernel(block_ref, out_hbm, sem):
    copy = pltpu.make_async_copy(block_ref, out_hbm, sem)
    copy.start()
    copy.wait()


def guide_kernel(kept_ref, partner_ref, out_ref):
    first_side = lax.axis_index("cfg") == 0
    cond = jnp.where(first_side, kept_ref[...], partner_ref[...])
    uncond = jnp.where(first_side, partner_ref[...], kept_ref[...])
    out_ref[...] = uncond + guidance_scale * (cond - uncond)


def shards(
    query_proj,
    key_proj,
    value_proj,
    query_gain,
    key_gain,
    block_input,
    cached_out,
    replay_mask,
    branch_gate,
    attn_weight,
    final_shift,
    final_scale,
    patch_weight,
):
    _, count, width = query_proj.shape
    depth = query_gain.shape[0]
    heads = width // depth
    features = attn_weight.shape[1]
    channels = patch_weight.shape[1]
    live_count = count // 2
    ring = lax.axis_size("ctx")
    parts = lax.axis_size("tp")
    share = count // parts
    members = math.gcd(heads, ring)
    groups = ring // members
    own_heads = heads // members
    own_width = own_heads * depth
    partial = groups > 1
    stat_rows = -(-3 * own_heads // 16) * 16

    def route(a, b, back):
        pairs = []
        for g in range(groups):
            for p in range(members):
                other = hop(g, a, groups) * members + hop(p, b, members)
                pairs.append((other, g * members + p) if back else (g * members + p, other))
        return pairs

    def call(kernel, inputs, outs, in_specs=None, out_specs=None, scratch=(), limit=24, cost=None):
        return pl.pallas_call(
            kernel,
            out_shape=outs,
            in_specs=in_specs or [VMEM] * len(inputs),
            out_specs=out_specs or [VMEM] * len(outs),
            scratch_shapes=scratch,
            compiler_params=pltpu.CompilerParams(vmem_limit_bytes=limit << 20),
            cost_estimate=cost,
        )(*inputs)

    bf16, f32 = jnp.bfloat16, jnp.float32
    shaped = jax.ShapeDtypeStruct
    pair_shape = shaped((2 * count, own_width), bf16)
    pairs = call(
        functools.partial(split_kernel, (members, own_width, depth)),
        (in_hbm(key_proj[0]), in_hbm(value_proj[0])),
        [pair_shape] * members,
        in_specs=[HBM] * 2,
        scratch=[pltpu.SemaphoreType.DMA((2, members))],
        limit=8,
    )
    pairs = list(pairs)
    pair_order = sorted(range(1, members), key=lambda b: (b < members // 2, b))
    for b in pair_order:
        pairs[b] = lax.ppermute(pairs[b], "ctx", route(0, b, False))
    asks = call(
        functools.partial(ask_kernel, (members, own_heads, depth, live_count)),
        (*map(in_hbm, (replay_mask, query_gain[None], query_proj[0])), pairs[0]),
        [shaped((live_count, own_width), bf16)] * members,
        in_specs=[HBM] * 3 + [VMEM],
        scratch=[
            pltpu.VMEM((1, count), jnp.int32),
            pltpu.VMEM((1, depth), f32),
            pltpu.VMEM((members, count, own_width), bf16),
            pltpu.SemaphoreType.DMA((2,)),
            pltpu.SemaphoreType.DMA((members,)),
        ],
        limit=16,
    )
    far_routes = [(a, b) for a in range(1, groups) for b in range(members)]
    far_asks = []
    for a, b in far_routes:
        far_asks.append(lax.ppermute(asks[b], "ctx", route(a, b, False)))
    near_asks = [asks[0]] + [lax.ppermute(asks[b], "ctx", route(0, b, False)) for b in range(1, members)]

    wanted = (
        replay_mask,
        key_gain[None],
        attn_weight,
        block_input[0],
        cached_out[0],
        branch_gate,
        final_shift,
        final_scale,
        patch_weight.T,
    )
    fetched = call(
        functools.partial(fetch_kernel, (len(wanted), live_count, parts)),
        (*map(in_hbm, wanted), asks[0]),
        [shaped(w.shape, w.dtype) for w in wanted] + [shaped((parts, share, live_count), bf16)],
        in_specs=[HBM] * len(wanted) + [VMEM],
        scratch=[pltpu.SemaphoreType.DMA((len(wanted),))],
        limit=16,
        cost=pl.CostEstimate(flops=0, transcendentals=0, bytes_accessed=2 * sum(w.size * w.dtype.itemsize for w in wanted)),
    )
    mask, key_gain_here, weight, inputs_here, cached_here, gate, shift, scale, patch, places = fetched

    parcel_rows = own_heads * live_count + (stat_rows if partial else 0)
    parcel_shape = shaped((parcel_rows, depth), bf16)

    units = [
        call(
            functools.partial(unit_kernel, depth),
            (key_gain_here, pair),
            [shaped((count, own_width), bf16)],
            cost=pl.CostEstimate(flops=0, transcendentals=0, bytes_accessed=1 << 18),
        )[0]
        for pair in pairs
    ]

    def attend(after, asks):
        scores = len(asks) * live_count * members * count * own_heads
        return call(
            functools.partial(
                attend_kernel,
                (members, partial, own_heads, depth, live_count, count, stat_rows, len(asks)),
            ),
            (after, *pairs, *units, *asks),
            [parcel_shape] * len(asks),
            scratch=[pltpu.VMEM((len(asks), live_count, live_count), f32)],
            cost=pl.CostEstimate(flops=4 * scores * depth, transcendentals=scores, bytes_accessed=1 << 20),
        )

    after, parcels = mask, {}
    for n, ask in enumerate(far_asks):
        (far,) = attend(after, [ask])
        after = far
        parcels[far_routes[n]] = lax.ppermute(far, "ctx", route(*far_routes[n], True))
    if members > 1:
        near = attend(after, near_asks[1:])
        after = near[0]
        for b in range(1, members):
            parcels[0, b] = lax.ppermute(near[b - 1], "ctx", route(0, b, True))
    (parcels[0, 0],) = attend(after, near_asks[:1])
    parcels = [parcels[a, b] for a in range(groups) for b in range(members)]

    merged = call(
        functools.partial(merge_kernel, (members, groups, own_heads, depth, live_count, stat_rows, parts)),
        (places, weight, *parcels),
        [shaped((share, features), bf16)] * (parts - 1) + [shaped((share, width), bf16)],
        scratch=[pltpu.VMEM((count, width), bf16)],
    )
    arrived = [
        lax.ppermute(merged[s - 1], "tp", [(i, (i + s) % parts) for i in range(parts)]) for s in range(1, parts)
    ]
    (own,) = call(
        project_kernel,
        (merged[-1], weight),
        [shaped((share, features), f32)],
        cost=pl.CostEstimate(flops=2 * share * width * features, transcendentals=0, bytes_accessed=1 << 20),
    )

    half = channels // 2
    block_out, kept, given = call(
        functools.partial(tail_kernel, parts),
        (mask, own, *arrived, inputs_here, cached_here, gate, shift, scale, patch),
        [shaped((share, features), bf16), shaped((half, share), f32), shaped((half, share), f32)],
    )
    partner = lax.ppermute(given, "cfg", [(0, 1), (1, 0)])
    (block_out,) = call(
        store_kernel,
        (block_out,),
        [shaped((share, features), bf16)],
        out_specs=[HBM],
        scratch=[pltpu.SemaphoreType.DMA(())],
        limit=4,
    )
    (velocity,) = call(guide_kernel, (kept, partner), [shaped((half, share), f32)], limit=4)
    return (block_out[None], velocity.T)


def solution(mesh):
    in_specs = (
        P("cfg", "ctx", "tp"),
        P("cfg", "ctx", "tp"),
        P("cfg", "ctx", "tp"),
        P(),
        P(),
        P("cfg", ("ctx", "tp"), None),
        P("cfg", ("ctx", "tp"), None),
        P("cfg", "ctx"),
        P("cfg", None),
        P("tp", None),
        P("cfg", None),
        P("cfg", None),
        P(),
    )
    out_specs = (P("cfg", ("ctx", "tp"), None), P(("ctx", "tp"), "cfg"))
    return jax.shard_map(shards, mesh=mesh, in_specs=in_specs, out_specs=out_specs, check_vma=False)
```

```python
import functools
import math

import jax
import jax.numpy as jnp
from jax import lax
from jax.experimental import pallas as pl
from jax.experimental.pallas import tpu as pltpu
from jax.sharding import PartitionSpec as P


guidance_scale = 3.0
VMEM = pl.BlockSpec(memory_space=pltpu.VMEM)
HBM = pl.BlockSpec(memory_space=pltpu.HBM)
NT = (((1,), (1,)), ((), ()))


def in_hbm(value):
    return pltpu.with_memory_space_constraint(value, pltpu.HBM)


def dot_f32(a, b):
    return jnp.dot(a, b, preferred_element_type=jnp.float32)


def dot_nt(a, b):
    return lax.dot_general(a, b, NT, preferred_element_type=jnp.float32)


def live_lanes(mask_ref):
    return jnp.where(mask_ref[...] == 1, 0.0, 1.0)


def pick_matrix(mask_ref, live_count):
    live = live_lanes(mask_ref)
    count = live.shape[1]
    rows = lax.broadcasted_iota(jnp.int32, (count, count), 0)
    cols = lax.broadcasted_iota(jnp.int32, (count, count), 1)
    upto = jnp.where(rows <= cols, 1.0, 0.0).astype(jnp.bfloat16)
    wide = jnp.broadcast_to(live, (8, count)).astype(jnp.bfloat16)
    rank = dot_f32(wide, upto)[0:1]
    slot = lax.broadcasted_iota(jnp.int32, (live_count, count), 0).astype(jnp.float32)
    hit = (jnp.broadcast_to(rank, slot.shape) == slot + 1.0) & (jnp.broadcast_to(live, slot.shape) > 0.5)
    return jnp.where(hit, 1.0, 0.0).astype(jnp.bfloat16)


def place_matrix(mask_ref, live_count, first, share):
    live = live_lanes(mask_ref)
    count = live.shape[1]
    wide = jnp.broadcast_to(live, (live_count, count)).astype(jnp.bfloat16)
    rows = lax.broadcasted_iota(jnp.int32, (share, count), 0) + first
    cols = lax.broadcasted_iota(jnp.int32, (share, count), 1)
    rank = dot_nt(jnp.where(cols <= rows, 1.0, 0.0).astype(jnp.bfloat16), wide)
    alive = dot_nt(jnp.where(cols == rows, 1.0, 0.0).astype(jnp.bfloat16), wide)
    slot = lax.broadcasted_iota(jnp.int32, (share, live_count), 1).astype(jnp.float32)
    hit = (rank == slot + 1.0) & (alive > 0.5)
    return jnp.where(hit, 1.0, 0.0).astype(jnp.bfloat16)


def hop(place, step, size):
    return place ^ step if size & (size - 1) == 0 else (place + step) % size


def ring_place(members):
    return lax.rem(lax.axis_index("ctx"), members)


def unit_rows(raw, gain):
    lifted = raw.astype(jnp.float32)
    mean_square = jnp.mean(lifted * lifted, axis=-1, keepdims=True)
    return (lifted * lax.rsqrt(mean_square + 1e-06) * gain).astype(jnp.bfloat16)


def split_kernel(dims, k_hbm, v_hbm, *refs):
    members, width, depth = dims
    outs, sems = refs[:members], refs[members]
    count = k_hbm.shape[0]
    position = ring_place(members)
    copies = []
    for b in [b for b in range(1, members)] + [0]:
        columns = pl.ds(pl.multiple_of(hop(position, b, members) * width, depth), width)
        for n, source in enumerate((k_hbm, v_hbm)):
            target = outs[b].at[pl.ds(n * count, count), :]
            copies.append(pltpu.make_async_copy(source.at[:, columns], target, sems.at[n, b]))
    for copy in copies:
        copy.start()
    for copy in copies:
        copy.wait()


def ask_kernel(dims, mask_hbm, gain_hbm, q_hbm, *refs):
    members, own_heads, depth, live_count = dims
    asks = refs[1 : members + 1]
    mask_ref, gain_ref, q_ref, small_sems, q_sems = refs[members + 1 :]
    width = own_heads * depth
    position = ring_place(members)
    small = [
        pltpu.make_async_copy(mask_hbm, mask_ref, small_sems.at[0]),
        pltpu.make_async_copy(gain_hbm, gain_ref, small_sems.at[1]),
    ]
    for copy in small:
        copy.start()
    order = [b for b in range(1, members)] + [0]
    loads = {}
    for b in order:
        columns = pl.ds(pl.multiple_of(hop(position, b, members) * width, depth), width)
        loads[b] = pltpu.make_async_copy(q_hbm.at[:, columns], q_ref.at[b], q_sems.at[b])
        loads[b].start()
    for copy in small:
        copy.wait()
    picks = pick_matrix(mask_ref, live_count)
    gain = gain_ref[...]
    for b in order:
        loads[b].wait()
        picked = dot_f32(picks, q_ref[b])
        for h in range(own_heads):
            columns = slice(h * depth, (h + 1) * depth)
            asks[b][:, columns] = unit_rows(picked[:, columns], gain)


def unit_kernel(depth, gain_ref, pair_ref, out_ref):
    count = out_ref.shape[0]
    for first in range(0, out_ref.shape[1], depth):
        columns = slice(first, first + depth)
        out_ref[:, columns] = unit_rows(pair_ref[pl.ds(0, count), columns], gain_ref[...])


def fetch_kernel(dims, *refs):
    n, live_count, parts = dims
    sources, targets, places_ref, sems = refs[:n], refs[n + 1 : 2 * n + 1], refs[2 * n + 1], refs[2 * n + 2]
    copies = [pltpu.make_async_copy(s, t, sems.at[i]) for i, (s, t) in enumerate(zip(sources, targets))]
    for copy in copies:
        copy.start()
    mask_ref = targets[0]
    copies[0].wait()
    share = places_ref.shape[1]
    for s in range(parts):
        first = lax.rem(lax.axis_index("tp") + s, parts) * share
        places_ref[s] = place_matrix(mask_ref, live_count, first, share)
    for copy in copies[1:]:
        copy.wait()


def attend_kernel(dims, *refs):
    members, partial, own_heads, depth, live_count, count, stat_rows, sources = dims
    pairs, units = refs[1 : members + 1], refs[members + 1 : 2 * members + 1]
    asks = refs[2 * members + 1 : 2 * members + 1 + sources]
    outs = refs[2 * members + 1 + sources :]
    factor = depth ** (-0.5)
    power = factor * math.log2(math.e)
    lanes = lax.broadcasted_iota(jnp.int32, (live_count, depth), 1)
    padded = -(-own_heads // 8) * 8
    stats = [jnp.zeros((live_count, depth), jnp.float32)] * sources
    ones = jnp.ones((count, depth), jnp.bfloat16)
    for h in range(own_heads):
        columns = slice(h * depth, (h + 1) * depth)
        for s in range(sources):
            queries = asks[s][:, columns]
            scores = [dot_nt(queries, unit[:, columns]) for unit in units]
            biggest = jnp.max(functools.reduce(jnp.maximum, scores), axis=-1, keepdims=True)
            weights = [jnp.exp2((score - biggest) * power).astype(jnp.bfloat16) for score in scores]
            summed = functools.reduce(
                jnp.add,
                [
                    dot_f32(w, jnp.concatenate([ref[pl.ds(count, count), columns], ones], axis=1))
                    for w, ref in zip(weights, pairs)
                ],
            )
            totals = summed[:, depth:]
            outs[s][pl.ds(h * live_count, live_count), :] = (summed[:, :depth] / totals).astype(jnp.bfloat16)
            stats[s] = jnp.where(lanes == h, biggest, jnp.where(lanes == padded + h, totals, stats[s]))
    if partial:
        blank = jnp.zeros((stat_rows - 3 * own_heads, live_count), jnp.float32)
        for s in range(sources):
            turned = jnp.transpose(stats[s])
            rest = turned[:own_heads] * factor + jnp.log(turned[padded : padded + own_heads])
            pieces = []
            for _ in range(3):
                pieces.append(rest.astype(jnp.bfloat16).astype(jnp.float32))
                rest = rest - pieces[-1]
            stat = jnp.concatenate([*pieces, blank], axis=0)
            outs[s][pl.ds(own_heads * live_count, stat_rows), :] = stat.astype(jnp.bfloat16)


def merge_kernel(dims, places_ref, weight_ref, *refs):
    members, groups, own_heads, depth, live_count, stat_rows, parts = dims
    sources = members * groups
    parcels = refs[:sources]
    sends = refs[sources : sources + parts - 1]
    own_ref, spread_ref = refs[sources + parts - 1 :]
    share = own_ref.shape[0]
    width = own_heads * depth
    position = ring_place(members)
    places = jnp.concatenate([places_ref[s] for s in range(parts)], axis=0)
    for b in range(members):
        held = [parcels[a * members + b] for a in range(groups)]
        if groups > 1:
            stats = [ref[pl.ds(own_heads * live_count, stat_rows), :].astype(jnp.float32) for ref in held]
        for h in range(own_heads):
            values = [ref[pl.ds(h * live_count, live_count), :] for ref in held]
            if groups > 1:
                logged = [
                    t[h : h + 1] + t[own_heads + h : own_heads + h + 1] + t[2 * own_heads + h : 2 * own_heads + h + 1]
                    for t in stats
                ]
                biggest = functools.reduce(jnp.maximum, logged)
                shares = [jnp.exp(l - biggest) for l in logged]
                total = functools.reduce(jnp.add, shares)
                spots = [places * (w / total).astype(jnp.bfloat16) for w in shares]
                placed = dot_f32(jnp.concatenate(spots, axis=1), jnp.concatenate(values, axis=0))
            else:
                placed = dot_f32(places, values[0])
            base = hop(position, b, members) * width + h * depth
            spread_ref[:, pl.ds(pl.multiple_of(base, depth), depth)] = placed.astype(jnp.bfloat16)
    own_ref[...] = spread_ref[pl.ds(0, share), :]
    for s in range(1, parts):
        project(spread_ref[pl.ds(s * share, share), :], weight_ref, sends[s - 1])


def project(rows, weight_ref, out_ref):
    features = weight_ref.shape[1]
    tile = 512 if features % 512 == 0 else features
    for first in range(0, features, tile):
        columns = pl.ds(first, tile)
        out_ref[:, columns] = dot_f32(rows, weight_ref[:, columns]).astype(out_ref.dtype)


def project_kernel(rows_ref, weight_ref, input_ref, gate_ref, out_ref):
    features = weight_ref.shape[1]
    tile = 512 if features % 512 == 0 else features
    for first in range(0, features, tile):
        columns = pl.ds(first, tile)
        product = dot_f32(rows_ref[...], weight_ref[:, columns])
        out_ref[:, columns] = input_ref[:, columns].astype(jnp.float32) + gate_ref[:, columns] * product


def tail_kernel(parts, mask_ref, own_ref, *refs):
    arrived = refs[: parts - 1]
    cached_ref, gate_ref, shift_ref, scale_ref, patch_ref, block_ref, kept_ref, given_ref = refs[parts - 1 :]
    others = functools.reduce(jnp.add, [ref[...].astype(jnp.float32) for ref in arrived])
    mixed = own_ref[...] + gate_ref[...] * others
    share = mixed.shape[0]
    count = mask_ref.shape[1]
    first = lax.axis_index("tp") * share
    rows = lax.broadcasted_iota(jnp.int32, (share, count), 0) + first
    cols = lax.broadcasted_iota(jnp.int32, (share, count), 1)
    replayed = jnp.where((cols == rows) & (jnp.broadcast_to(mask_ref[...], rows.shape) == 1), 1.0, 0.0)
    replayed = jnp.sum(replayed, axis=-1, keepdims=True) > 0.5
    block = jnp.where(replayed, cached_ref[...].astype(jnp.float32), mixed).astype(jnp.bfloat16)
    block_ref[...] = block
    lifted = block.astype(jnp.float32)
    centred = lifted - jnp.mean(lifted, axis=-1, keepdims=True)
    spread = jnp.mean(centred * centred, axis=-1, keepdims=True)
    normed = centred * lax.rsqrt(spread + 1e-06) * (1.0 + scale_ref[...]) + shift_ref[...]
    branch = dot_nt(patch_ref[...], normed.astype(jnp.bfloat16))
    half = branch.shape[0] // 2
    first_side = lax.axis_index("cfg") == 0
    kept_ref[...] = jnp.where(first_side, branch[:half], branch[half:])
    given_ref[...] = jnp.where(first_side, branch[half:], branch[:half])


def store_kernel(block_ref, out_hbm, sem):
    copy = pltpu.make_async_copy(block_ref, out_hbm, sem)
    copy.start()
    copy.wait()


def guide_kernel(kept_ref, partner_ref, out_ref):
    first_side = lax.axis_index("cfg") == 0
    cond = jnp.where(first_side, kept_ref[...], partner_ref[...])
    uncond = jnp.where(first_side, partner_ref[...], kept_ref[...])
    out_ref[...] = uncond + guidance_scale * (cond - uncond)


def shards(
    query_proj,
    key_proj,
    value_proj,
    query_gain,
    key_gain,
    block_input,
    cached_out,
    replay_mask,
    branch_gate,
    attn_weight,
    final_shift,
    final_scale,
    patch_weight,
):
    _, count, width = query_proj.shape
    depth = query_gain.shape[0]
    heads = width // depth
    features = attn_weight.shape[1]
    channels = patch_weight.shape[1]
    live_count = count // 2
    ring = lax.axis_size("ctx")
    parts = lax.axis_size("tp")
    share = count // parts
    members = math.gcd(heads, ring)
    groups = ring // members
    own_heads = heads // members
    own_width = own_heads * depth
    partial = groups > 1
    stat_rows = -(-3 * own_heads // 16) * 16

    def route(a, b, back):
        pairs = []
        for g in range(groups):
            for p in range(members):
                other = hop(g, a, groups) * members + hop(p, b, members)
                pairs.append((other, g * members + p) if back else (g * members + p, other))
        return pairs

    def call(kernel, inputs, outs, in_specs=None, out_specs=None, scratch=(), limit=24, cost=None):
        return pl.pallas_call(
            kernel,
            out_shape=outs,
            in_specs=in_specs or [VMEM] * len(inputs),
            out_specs=out_specs or [VMEM] * len(outs),
            scratch_shapes=scratch,
            compiler_params=pltpu.CompilerParams(vmem_limit_bytes=limit << 20),
            cost_estimate=cost,
        )(*inputs)

    bf16, f32 = jnp.bfloat16, jnp.float32
    shaped = jax.ShapeDtypeStruct
    pair_shape = shaped((2 * count, own_width), bf16)
    pairs = call(
        functools.partial(split_kernel, (members, own_width, depth)),
        (in_hbm(key_proj[0]), in_hbm(value_proj[0])),
        [pair_shape] * members,
        in_specs=[HBM] * 2,
        scratch=[pltpu.SemaphoreType.DMA((2, members))],
        limit=8,
    )
    pairs = list(pairs)
    pair_order = sorted(range(1, members), key=lambda b: (b < members // 2, b))
    for b in pair_order:
        pairs[b] = lax.ppermute(pairs[b], "ctx", route(0, b, False))
    asks = call(
        functools.partial(ask_kernel, (members, own_heads, depth, live_count)),
        (*map(in_hbm, (replay_mask, query_gain[None], query_proj[0])), pairs[0]),
        [shaped((live_count, own_width), bf16)] * members,
        in_specs=[HBM] * 3 + [VMEM],
        scratch=[
            pltpu.VMEM((1, count), jnp.int32),
            pltpu.VMEM((1, depth), f32),
            pltpu.VMEM((members, count, own_width), bf16),
            pltpu.SemaphoreType.DMA((2,)),
            pltpu.SemaphoreType.DMA((members,)),
        ],
        limit=16,
    )
    far_routes = [(a, b) for a in range(1, groups) for b in range(members)]
    far_asks = []
    for a, b in far_routes:
        far_asks.append(lax.ppermute(asks[b], "ctx", route(a, b, False)))
    near_asks = [asks[0]] + [lax.ppermute(asks[b], "ctx", route(0, b, False)) for b in range(1, members)]

    wanted = (
        replay_mask,
        key_gain[None],
        attn_weight,
        block_input[0],
        cached_out[0],
        branch_gate,
        final_shift,
        final_scale,
        patch_weight.T,
    )
    fetched = call(
        functools.partial(fetch_kernel, (len(wanted), live_count, parts)),
        (*map(in_hbm, wanted), asks[0]),
        [shaped(w.shape, w.dtype) for w in wanted] + [shaped((parts, share, live_count), bf16)],
        in_specs=[HBM] * len(wanted) + [VMEM],
        scratch=[pltpu.SemaphoreType.DMA((len(wanted),))],
        limit=16,
        cost=pl.CostEstimate(flops=0, transcendentals=0, bytes_accessed=2 * sum(w.size * w.dtype.itemsize for w in wanted)),
    )
    mask, key_gain_here, weight, inputs_here, cached_here, gate, shift, scale, patch, places = fetched

    parcel_rows = own_heads * live_count + (stat_rows if partial else 0)
    parcel_shape = shaped((parcel_rows, depth), bf16)

    units = [
        call(
            functools.partial(unit_kernel, depth),
            (key_gain_here, pair),
            [shaped((count, own_width), bf16)],
            cost=pl.CostEstimate(flops=0, transcendentals=0, bytes_accessed=1 << 18),
        )[0]
        for pair in pairs
    ]

    def attend(after, asks):
        scores = len(asks) * live_count * members * count * own_heads
        return call(
            functools.partial(
                attend_kernel,
                (members, partial, own_heads, depth, live_count, count, stat_rows, len(asks)),
            ),
            (after, *pairs, *units, *asks),
            [parcel_shape] * len(asks),
            cost=pl.CostEstimate(flops=4 * scores * depth, transcendentals=scores, bytes_accessed=1 << 20),
        )

    after, parcels = mask, {}
    for n, ask in enumerate(far_asks):
        (far,) = attend(after, [ask])
        after = far
        parcels[far_routes[n]] = lax.ppermute(far, "ctx", route(*far_routes[n], True))
    if members > 1:
        near = attend(after, near_asks[1:])
        after = near[0]
        for b in range(1, members):
            parcels[0, b] = lax.ppermute(near[b - 1], "ctx", route(0, b, True))
    (parcels[0, 0],) = attend(after, near_asks[:1])
    parcels = [parcels[a, b] for a in range(groups) for b in range(members)]

    merged = call(
        functools.partial(merge_kernel, (members, groups, own_heads, depth, live_count, stat_rows, parts)),
        (places, weight, *parcels),
        [shaped((share, features), bf16)] * (parts - 1) + [shaped((share, width), bf16)],
        scratch=[pltpu.VMEM((count, width), bf16)],
    )
    arrived = [
        lax.ppermute(merged[s - 1], "tp", [(i, (i + s) % parts) for i in range(parts)]) for s in range(1, parts)
    ]
    (own,) = call(
        project_kernel,
        (merged[-1], weight, inputs_here, gate),
        [shaped((share, features), f32)],
        cost=pl.CostEstimate(flops=2 * share * width * features, transcendentals=0, bytes_accessed=1 << 20),
    )

    half = channels // 2
    block_out, kept, given = call(
        functools.partial(tail_kernel, parts),
        (mask, own, *arrived, cached_here, gate, shift, scale, patch),
        [shaped((share, features), bf16), shaped((half, share), f32), shaped((half, share), f32)],
    )
    partner = lax.ppermute(given, "cfg", [(0, 1), (1, 0)])
    (block_out,) = call(
        store_kernel,
        (block_out,),
        [shaped((share, features), bf16)],
        out_specs=[HBM],
        scratch=[pltpu.SemaphoreType.DMA(())],
        limit=4,
    )
    (velocity,) = call(guide_kernel, (kept, partner), [shaped((half, share), f32)], limit=4)
    return (block_out[None], velocity.T)


def solution(mesh):
    in_specs = (
        P("cfg", "ctx", "tp"),
        P("cfg", "ctx", "tp"),
        P("cfg", "ctx", "tp"),
        P(),
        P(),
        P("cfg", ("ctx", "tp"), None),
        P("cfg", ("ctx", "tp"), None),
        P("cfg", "ctx"),
        P("cfg", None),
        P("tp", None),
        P("cfg", None),
        P("cfg", None),
        P(),
    )
    out_specs = (P("cfg", ("ctx", "tp"), None), P(("ctx", "tp"), "cfg"))
    return jax.shard_map(shards, mesh=mesh, in_specs=in_specs, out_specs=out_specs, check_vma=False)
```

```python
import functools
import math

import jax
import jax.numpy as jnp
from jax import lax
from jax.experimental import pallas as pl
from jax.experimental.pallas import tpu as pltpu
from jax.sharding import PartitionSpec as P


guidance_scale = 3.0
VMEM = pl.BlockSpec(memory_space=pltpu.VMEM)
HBM = pl.BlockSpec(memory_space=pltpu.HBM)
NT = (((1,), (1,)), ((), ()))


def in_hbm(value):
    return pltpu.with_memory_space_constraint(value, pltpu.HBM)


def dot_f32(a, b):
    return jnp.dot(a, b, preferred_element_type=jnp.float32)


def dot_nt(a, b):
    return lax.dot_general(a, b, NT, preferred_element_type=jnp.float32)


def live_lanes(mask_ref):
    return jnp.where(mask_ref[...] == 1, 0.0, 1.0)


def pick_matrix(mask_ref, live_count):
    live = live_lanes(mask_ref)
    count = live.shape[1]
    rows = lax.broadcasted_iota(jnp.int32, (count, count), 0)
    cols = lax.broadcasted_iota(jnp.int32, (count, count), 1)
    upto = jnp.where(rows <= cols, 1.0, 0.0).astype(jnp.bfloat16)
    wide = jnp.broadcast_to(live, (8, count)).astype(jnp.bfloat16)
    rank = dot_f32(wide, upto)[0:1]
    slot = lax.broadcasted_iota(jnp.int32, (live_count, count), 0).astype(jnp.float32)
    hit = (jnp.broadcast_to(rank, slot.shape) == slot + 1.0) & (jnp.broadcast_to(live, slot.shape) > 0.5)
    return jnp.where(hit, 1.0, 0.0).astype(jnp.bfloat16)


def place_matrix(mask_ref, live_count, first, share):
    live = live_lanes(mask_ref)
    count = live.shape[1]
    wide = jnp.broadcast_to(live, (live_count, count)).astype(jnp.bfloat16)
    rows = lax.broadcasted_iota(jnp.int32, (share, count), 0) + first
    cols = lax.broadcasted_iota(jnp.int32, (share, count), 1)
    rank = dot_nt(jnp.where(cols <= rows, 1.0, 0.0).astype(jnp.bfloat16), wide)
    alive = dot_nt(jnp.where(cols == rows, 1.0, 0.0).astype(jnp.bfloat16), wide)
    slot = lax.broadcasted_iota(jnp.int32, (share, live_count), 1).astype(jnp.float32)
    hit = (rank == slot + 1.0) & (alive > 0.5)
    return jnp.where(hit, 1.0, 0.0).astype(jnp.bfloat16)


def hop(place, step, size):
    return place ^ step if size & (size - 1) == 0 else (place + step) % size


def ring_place(members):
    return lax.rem(lax.axis_index("ctx"), members)


def unit_rows(raw, gain):
    lifted = raw.astype(jnp.float32)
    mean_square = jnp.mean(lifted * lifted, axis=-1, keepdims=True)
    return (lifted * lax.rsqrt(mean_square + 1e-06) * gain).astype(jnp.bfloat16)


def split_kernel(dims, k_hbm, v_hbm, *refs):
    members, width, depth = dims
    outs, sems = refs[:members], refs[members]
    count = k_hbm.shape[0]
    position = ring_place(members)
    copies = []
    for b in [b for b in range(1, members)] + [0]:
        columns = pl.ds(pl.multiple_of(hop(position, b, members) * width, depth), width)
        for n, source in enumerate((k_hbm, v_hbm)):
            target = outs[b].at[pl.ds(n * count, count), :]
            copies.append(pltpu.make_async_copy(source.at[:, columns], target, sems.at[n, b]))
    for copy in copies:
        copy.start()
    for copy in copies:
        copy.wait()


def ask_kernel(dims, mask_hbm, gain_hbm, q_hbm, *refs):
    members, own_heads, depth, live_count = dims
    asks = refs[1 : members + 1]
    mask_ref, gain_ref, q_ref, small_sems, q_sems = refs[members + 1 :]
    width = own_heads * depth
    position = ring_place(members)
    small = [
        pltpu.make_async_copy(mask_hbm, mask_ref, small_sems.at[0]),
        pltpu.make_async_copy(gain_hbm, gain_ref, small_sems.at[1]),
    ]
    for copy in small:
        copy.start()
    order = [b for b in range(1, members)] + [0]
    loads = {}
    for b in order:
        columns = pl.ds(pl.multiple_of(hop(position, b, members) * width, depth), width)
        loads[b] = pltpu.make_async_copy(q_hbm.at[:, columns], q_ref.at[b], q_sems.at[b])
        loads[b].start()
    for copy in small:
        copy.wait()
    picks = pick_matrix(mask_ref, live_count)
    gain = gain_ref[...]
    for b in order:
        loads[b].wait()
        picked = dot_f32(picks, q_ref[b])
        for h in range(own_heads):
            columns = slice(h * depth, (h + 1) * depth)
            asks[b][:, columns] = unit_rows(picked[:, columns], gain)


def unit_kernel(depth, gain_ref, pair_ref, out_ref):
    count = out_ref.shape[0]
    for first in range(0, out_ref.shape[1], depth):
        columns = slice(first, first + depth)
        out_ref[:, columns] = unit_rows(pair_ref[pl.ds(0, count), columns], gain_ref[...])


def fetch_kernel(dims, *refs):
    n, live_count, parts = dims
    sources, targets, places_ref, sems = refs[:n], refs[n + 1 : 2 * n + 1], refs[2 * n + 1], refs[2 * n + 2]
    copies = [pltpu.make_async_copy(s, t, sems.at[i]) for i, (s, t) in enumerate(zip(sources, targets))]
    for copy in copies:
        copy.start()
    mask_ref = targets[0]
    copies[0].wait()
    share = places_ref.shape[1]
    for s in range(parts):
        first = lax.rem(lax.axis_index("tp") + s, parts) * share
        places_ref[s] = place_matrix(mask_ref, live_count, first, share)
    for copy in copies[1:]:
        copy.wait()


def attend_kernel(dims, *refs):
    members, partial, own_heads, depth, live_count, count, stat_rows, sources = dims
    pairs, units = refs[1 : members + 1], refs[members + 1 : 2 * members + 1]
    asks = refs[2 * members + 1 : 2 * members + 1 + sources]
    outs = refs[2 * members + 1 + sources :]
    factor = depth ** (-0.5)
    power = factor * math.log2(math.e)
    lanes = lax.broadcasted_iota(jnp.int32, (live_count, depth), 1)
    padded = -(-own_heads // 8) * 8
    stats = [jnp.zeros((live_count, depth), jnp.float32)] * sources
    ones = jnp.ones((count, depth), jnp.bfloat16)
    for h in range(own_heads):
        columns = slice(h * depth, (h + 1) * depth)
        for s in range(sources):
            queries = asks[s][:, columns]
            scores = [dot_nt(queries, unit[:, columns]) for unit in units]
            biggest = jnp.max(functools.reduce(jnp.maximum, scores), axis=-1, keepdims=True)
            weights = [jnp.exp2((score - biggest) * power).astype(jnp.bfloat16) for score in scores]
            summed = functools.reduce(
                jnp.add,
                [
                    dot_f32(w, jnp.concatenate([ref[pl.ds(count, count), columns], ones], axis=1))
                    for w, ref in zip(weights, pairs)
                ],
            )
            totals = summed[:, depth:]
            outs[s][pl.ds(h * live_count, live_count), :] = (summed[:, :depth] / totals).astype(jnp.bfloat16)
            stats[s] = jnp.where(lanes == h, biggest, jnp.where(lanes == padded + h, totals, stats[s]))
    if partial:
        blank = jnp.zeros((stat_rows - 3 * own_heads, live_count), jnp.float32)
        for s in range(sources):
            turned = jnp.transpose(stats[s])
            rest = turned[:own_heads] * factor + jnp.log(turned[padded : padded + own_heads])
            pieces = []
            for _ in range(3):
                pieces.append(rest.astype(jnp.bfloat16).astype(jnp.float32))
                rest = rest - pieces[-1]
            stat = jnp.concatenate([*pieces, blank], axis=0)
            outs[s][pl.ds(own_heads * live_count, stat_rows), :] = stat.astype(jnp.bfloat16)


def merge_rows(dims, places, parcels, spread_ref):
    members, groups, own_heads, depth, live_count, stat_rows, _ = dims
    width = own_heads * depth
    position = ring_place(members)
    for b in range(members):
        held = [parcels[a * members + b] for a in range(groups)]
        if groups > 1:
            stats = [ref[pl.ds(own_heads * live_count, stat_rows), :].astype(jnp.float32) for ref in held]
        for h in range(own_heads):
            values = [ref[pl.ds(h * live_count, live_count), :] for ref in held]
            if groups > 1:
                logged = [
                    t[h : h + 1] + t[own_heads + h : own_heads + h + 1] + t[2 * own_heads + h : 2 * own_heads + h + 1]
                    for t in stats
                ]
                biggest = functools.reduce(jnp.maximum, logged)
                shares = [jnp.exp(l - biggest) for l in logged]
                total = functools.reduce(jnp.add, shares)
                spots = [places * (w / total).astype(jnp.bfloat16) for w in shares]
                placed = dot_f32(jnp.concatenate(spots, axis=1), jnp.concatenate(values, axis=0))
            else:
                placed = dot_f32(places, values[0])
            base = hop(position, b, members) * width + h * depth
            spread_ref[:, pl.ds(pl.multiple_of(base, depth), depth)] = placed.astype(jnp.bfloat16)


def merge_kernel(dims, places_ref, weight_ref, *refs):
    members, groups, *_, parts = dims
    sources = members * groups
    parcels, sends, spread_ref = refs[:sources], refs[sources:-1], refs[-1]
    share = places_ref.shape[1]
    places = jnp.concatenate([places_ref[s] for s in range(1, parts)], axis=0)
    merge_rows(dims, places, parcels, spread_ref)
    for s, send in enumerate(sends):
        project(spread_ref[pl.ds(s * share, share), :], weight_ref, send)


def project(rows, weight_ref, out_ref):
    features = weight_ref.shape[1]
    tile = 512 if features % 512 == 0 else features
    for first in range(0, features, tile):
        columns = pl.ds(first, tile)
        out_ref[:, columns] = dot_f32(rows, weight_ref[:, columns]).astype(out_ref.dtype)


def own_kernel(dims, after_ref, places_ref, weight_ref, input_ref, gate_ref, *refs):
    parcels, out_ref, spread_ref = refs[:-2], refs[-2], refs[-1]
    merge_rows(dims, places_ref[0], parcels, spread_ref)
    features = weight_ref.shape[1]
    tile = 512 if features % 512 == 0 else features
    for first in range(0, features, tile):
        columns = pl.ds(first, tile)
        product = dot_f32(spread_ref[...], weight_ref[:, columns])
        out_ref[:, columns] = input_ref[:, columns].astype(jnp.float32) + gate_ref[:, columns] * product


def tail_kernel(parts, mask_ref, own_ref, *refs):
    arrived = refs[: parts - 1]
    cached_ref, gate_ref, shift_ref, scale_ref, patch_ref, block_ref, kept_ref, given_ref = refs[parts - 1 :]
    others = functools.reduce(jnp.add, [ref[...].astype(jnp.float32) for ref in arrived])
    mixed = own_ref[...] + gate_ref[...] * others
    share = mixed.shape[0]
    count = mask_ref.shape[1]
    first = lax.axis_index("tp") * share
    rows = lax.broadcasted_iota(jnp.int32, (share, count), 0) + first
    cols = lax.broadcasted_iota(jnp.int32, (share, count), 1)
    replayed = jnp.where((cols == rows) & (jnp.broadcast_to(mask_ref[...], rows.shape) == 1), 1.0, 0.0)
    replayed = jnp.sum(replayed, axis=-1, keepdims=True) > 0.5
    block = jnp.where(replayed, cached_ref[...].astype(jnp.float32), mixed).astype(jnp.bfloat16)
    block_ref[...] = block
    lifted = block.astype(jnp.float32)
    centred = lifted - jnp.mean(lifted, axis=-1, keepdims=True)
    spread = jnp.mean(centred * centred, axis=-1, keepdims=True)
    normed = centred * lax.rsqrt(spread + 1e-06) * (1.0 + scale_ref[...]) + shift_ref[...]
    branch = dot_nt(patch_ref[...], normed.astype(jnp.bfloat16))
    half = branch.shape[0] // 2
    first_side = lax.axis_index("cfg") == 0
    kept_ref[...] = jnp.where(first_side, branch[:half], branch[half:])
    given_ref[...] = jnp.where(first_side, branch[half:], branch[:half])


def store_kernel(block_ref, out_hbm, sem):
    copy = pltpu.make_async_copy(block_ref, out_hbm, sem)
    copy.start()
    copy.wait()


def guide_kernel(kept_ref, partner_ref, out_ref):
    first_side = lax.axis_index("cfg") == 0
    cond = jnp.where(first_side, kept_ref[...], partner_ref[...])
    uncond = jnp.where(first_side, partner_ref[...], kept_ref[...])
    out_ref[...] = uncond + guidance_scale * (cond - uncond)


def shards(
    query_proj,
    key_proj,
    value_proj,
    query_gain,
    key_gain,
    block_input,
    cached_out,
    replay_mask,
    branch_gate,
    attn_weight,
    final_shift,
    final_scale,
    patch_weight,
):
    _, count, width = query_proj.shape
    depth = query_gain.shape[0]
    heads = width // depth
    features = attn_weight.shape[1]
    channels = patch_weight.shape[1]
    live_count = count // 2
    ring = lax.axis_size("ctx")
    parts = lax.axis_size("tp")
    share = count // parts
    members = math.gcd(heads, ring)
    groups = ring // members
    own_heads = heads // members
    own_width = own_heads * depth
    partial = groups > 1
    stat_rows = -(-3 * own_heads // 16) * 16

    def route(a, b, back):
        pairs = []
        for g in range(groups):
            for p in range(members):
                other = hop(g, a, groups) * members + hop(p, b, members)
                pairs.append((other, g * members + p) if back else (g * members + p, other))
        return pairs

    def call(kernel, inputs, outs, in_specs=None, out_specs=None, scratch=(), limit=24, cost=None):
        return pl.pallas_call(
            kernel,
            out_shape=outs,
            in_specs=in_specs or [VMEM] * len(inputs),
            out_specs=out_specs or [VMEM] * len(outs),
            scratch_shapes=scratch,
            compiler_params=pltpu.CompilerParams(vmem_limit_bytes=limit << 20),
            cost_estimate=cost,
        )(*inputs)

    bf16, f32 = jnp.bfloat16, jnp.float32
    shaped = jax.ShapeDtypeStruct
    pair_shape = shaped((2 * count, own_width), bf16)
    pairs = call(
        functools.partial(split_kernel, (members, own_width, depth)),
        (in_hbm(key_proj[0]), in_hbm(value_proj[0])),
        [pair_shape] * members,
        in_specs=[HBM] * 2,
        scratch=[pltpu.SemaphoreType.DMA((2, members))],
        limit=8,
    )
    pairs = list(pairs)
    pair_order = sorted(range(1, members), key=lambda b: (b != members // 2, b))
    for b in pair_order:
        pairs[b] = lax.ppermute(pairs[b], "ctx", route(0, b, False))
    asks = call(
        functools.partial(ask_kernel, (members, own_heads, depth, live_count)),
        (*map(in_hbm, (replay_mask, query_gain[None], query_proj[0])), pairs[0]),
        [shaped((live_count, own_width), bf16)] * members,
        in_specs=[HBM] * 3 + [VMEM],
        scratch=[
            pltpu.VMEM((1, count), jnp.int32),
            pltpu.VMEM((1, depth), f32),
            pltpu.VMEM((members, count, own_width), bf16),
            pltpu.SemaphoreType.DMA((2,)),
            pltpu.SemaphoreType.DMA((members,)),
        ],
        limit=16,
    )
    far_routes = sorted(((a, b) for a in range(1, groups) for b in range(members)), key=lambda r: (r[0], (1 - r[1] if r[1] < 2 else r[1])))
    far_asks = []
    for a, b in far_routes:
        far_asks.append(lax.ppermute(asks[b], "ctx", route(a, b, False)))
    near_asks = [asks[0]] + [lax.ppermute(asks[b], "ctx", route(0, b, False)) for b in range(1, members)]

    wanted = (
        replay_mask,
        key_gain[None],
        attn_weight,
        block_input[0],
        cached_out[0],
        branch_gate,
        final_shift,
        final_scale,
        patch_weight.T,
    )
    fetched = call(
        functools.partial(fetch_kernel, (len(wanted), live_count, parts)),
        (*map(in_hbm, wanted), asks[0]),
        [shaped(w.shape, w.dtype) for w in wanted] + [shaped((parts, share, live_count), bf16)],
        in_specs=[HBM] * len(wanted) + [VMEM],
        scratch=[pltpu.SemaphoreType.DMA((len(wanted),))],
        limit=16,
        cost=pl.CostEstimate(flops=0, transcendentals=0, bytes_accessed=2 * sum(w.size * w.dtype.itemsize for w in wanted)),
    )
    mask, key_gain_here, weight, inputs_here, cached_here, gate, shift, scale, patch, places = fetched

    parcel_rows = own_heads * live_count + (stat_rows if partial else 0)
    parcel_shape = shaped((parcel_rows, depth), bf16)

    units = [
        call(
            functools.partial(unit_kernel, depth),
            (key_gain_here, pair),
            [shaped((count, own_width), bf16)],
            cost=pl.CostEstimate(flops=0, transcendentals=0, bytes_accessed=1 << 18),
        )[0]
        for pair in pairs
    ]

    def attend(after, asks):
        scores = len(asks) * live_count * members * count * own_heads
        return call(
            functools.partial(
                attend_kernel,
                (members, partial, own_heads, depth, live_count, count, stat_rows, len(asks)),
            ),
            (after, *pairs, *units, *asks),
            [parcel_shape] * len(asks),
            cost=pl.CostEstimate(flops=4 * scores * depth, transcendentals=scores, bytes_accessed=1 << 20),
        )

    after, parcels = mask, {}
    for n, ask in enumerate(far_asks):
        (far,) = attend(after, [ask])
        after = far
        parcels[far_routes[n]] = lax.ppermute(far, "ctx", route(*far_routes[n], True))
    if members > 1:
        near = attend(after, near_asks[1:])
        after = near[0]
        for b in range(1, members):
            parcels[0, b] = lax.ppermute(near[b - 1], "ctx", route(0, b, True))
    (parcels[0, 0],) = attend(after, near_asks[:1])
    parcels = [parcels[a, b] for a in range(groups) for b in range(members)]

    dims = (members, groups, own_heads, depth, live_count, stat_rows, parts)
    merged = call(
        functools.partial(merge_kernel, dims),
        (places, weight, *parcels),
        [shaped((share, features), bf16)] * (parts - 1),
        scratch=[pltpu.VMEM(((parts - 1) * share, width), bf16)],
    )
    arrived = [
        lax.ppermute(merged[s - 1], "tp", [(i, (i + s) % parts) for i in range(parts)]) for s in range(1, parts)
    ]
    (own,) = call(
        functools.partial(own_kernel, dims),
        (merged[0], places, weight, inputs_here, gate, *parcels),
        [shaped((share, features), f32)],
        scratch=[pltpu.VMEM((share, width), bf16)],
        cost=pl.CostEstimate(flops=2 * share * width * features, transcendentals=0, bytes_accessed=1 << 20),
    )

    half = channels // 2
    block_out, kept, given = call(
        functools.partial(tail_kernel, parts),
        (mask, own, *arrived, cached_here, gate, shift, scale, patch),
        [shaped((share, features), bf16), shaped((half, share), f32), shaped((half, share), f32)],
    )
    partner = lax.ppermute(given, "cfg", [(0, 1), (1, 0)])
    (block_out,) = call(
        store_kernel,
        (block_out,),
        [shaped((share, features), bf16)],
        out_specs=[HBM],
        scratch=[pltpu.SemaphoreType.DMA(())],
        limit=4,
    )
    (velocity,) = call(guide_kernel, (kept, partner), [shaped((half, share), f32)], limit=4)
    return (block_out[None], velocity.T)


def solution(mesh):
    in_specs = (
        P("cfg", "ctx", "tp"),
        P("cfg", "ctx", "tp"),
        P("cfg", "ctx", "tp"),
        P(),
        P(),
        P("cfg", ("ctx", "tp"), None),
        P("cfg", ("ctx", "tp"), None),
        P("cfg", "ctx"),
        P("cfg", None),
        P("tp", None),
        P("cfg", None),
        P("cfg", None),
        P(),
    )
    out_specs = (P("cfg", ("ctx", "tp"), None), P(("ctx", "tp"), "cfg"))
    return jax.shard_map(shards, mesh=mesh, in_specs=in_specs, out_specs=out_specs, check_vma=False)
```

```python
import functools
import math

import jax
import jax.numpy as jnp
from jax import lax
from jax.experimental import pallas as pl
from jax.experimental.pallas import tpu as pltpu
from jax.sharding import PartitionSpec as P


guidance_scale = 3.0
VMEM = pl.BlockSpec(memory_space=pltpu.VMEM)
HBM = pl.BlockSpec(memory_space=pltpu.HBM)
NT = (((1,), (1,)), ((), ()))


def in_hbm(value):
    return pltpu.with_memory_space_constraint(value, pltpu.HBM)


def dot_f32(a, b):
    return jnp.dot(a, b, preferred_element_type=jnp.float32)


def dot_nt(a, b):
    return lax.dot_general(a, b, NT, preferred_element_type=jnp.float32)


def live_lanes(mask_ref):
    return jnp.where(mask_ref[...] == 1, 0.0, 1.0)


def pick_matrix(mask_ref, live_count):
    live = live_lanes(mask_ref)
    count = live.shape[1]
    rows = lax.broadcasted_iota(jnp.int32, (count, count), 0)
    cols = lax.broadcasted_iota(jnp.int32, (count, count), 1)
    upto = jnp.where(rows <= cols, 1.0, 0.0).astype(jnp.bfloat16)
    wide = jnp.broadcast_to(live, (8, count)).astype(jnp.bfloat16)
    rank = dot_f32(wide, upto)[0:1]
    slot = lax.broadcasted_iota(jnp.int32, (live_count, count), 0).astype(jnp.float32)
    hit = (jnp.broadcast_to(rank, slot.shape) == slot + 1.0) & (jnp.broadcast_to(live, slot.shape) > 0.5)
    return jnp.where(hit, 1.0, 0.0).astype(jnp.bfloat16)


def place_matrix(mask_ref, live_count, first, share):
    live = live_lanes(mask_ref)
    count = live.shape[1]
    wide = jnp.broadcast_to(live, (live_count, count)).astype(jnp.bfloat16)
    rows = lax.broadcasted_iota(jnp.int32, (share, count), 0) + first
    cols = lax.broadcasted_iota(jnp.int32, (share, count), 1)
    rank = dot_nt(jnp.where(cols <= rows, 1.0, 0.0).astype(jnp.bfloat16), wide)
    alive = dot_nt(jnp.where(cols == rows, 1.0, 0.0).astype(jnp.bfloat16), wide)
    slot = lax.broadcasted_iota(jnp.int32, (share, live_count), 1).astype(jnp.float32)
    hit = (rank == slot + 1.0) & (alive > 0.5)
    return jnp.where(hit, 1.0, 0.0).astype(jnp.bfloat16)


def hop(place, step, size):
    return place ^ step if size & (size - 1) == 0 else (place + step) % size


def ring_place(members):
    return lax.rem(lax.axis_index("ctx"), members)


def unit_rows(raw, gain):
    lifted = raw.astype(jnp.float32)
    mean_square = jnp.mean(lifted * lifted, axis=-1, keepdims=True)
    return (lifted * lax.rsqrt(mean_square + 1e-06) * gain).astype(jnp.bfloat16)


def split_kernel(dims, k_hbm, v_hbm, *refs):
    members, width, depth = dims
    outs, sems = refs[:members], refs[members]
    count = k_hbm.shape[0]
    position = ring_place(members)
    copies = []
    for b in [b for b in range(1, members)] + [0]:
        columns = pl.ds(pl.multiple_of(hop(position, b, members) * width, depth), width)
        for n, source in enumerate((k_hbm, v_hbm)):
            target = outs[b].at[pl.ds(n * count, count), :]
            copies.append(pltpu.make_async_copy(source.at[:, columns], target, sems.at[n, b]))
    for copy in copies:
        copy.start()
    for copy in copies:
        copy.wait()


def ask_kernel(dims, mask_hbm, gain_hbm, q_hbm, *refs):
    members, own_heads, depth, live_count = dims
    asks = refs[1 : members + 1]
    mask_ref, gain_ref, q_ref, small_sems, q_sems = refs[members + 1 :]
    width = own_heads * depth
    position = ring_place(members)
    small = [
        pltpu.make_async_copy(mask_hbm, mask_ref, small_sems.at[0]),
        pltpu.make_async_copy(gain_hbm, gain_ref, small_sems.at[1]),
    ]
    for copy in small:
        copy.start()
    order = [b for b in range(1, members)] + [0]
    loads = {}
    for b in order:
        columns = pl.ds(pl.multiple_of(hop(position, b, members) * width, depth), width)
        loads[b] = pltpu.make_async_copy(q_hbm.at[:, columns], q_ref.at[b], q_sems.at[b])
        loads[b].start()
    for copy in small:
        copy.wait()
    picks = pick_matrix(mask_ref, live_count)
    gain = gain_ref[...]
    for b in order:
        loads[b].wait()
        picked = dot_f32(picks, q_ref[b])
        for h in range(own_heads):
            columns = slice(h * depth, (h + 1) * depth)
            asks[b][:, columns] = unit_rows(picked[:, columns], gain)


def unit_kernel(depth, gain_ref, pair_ref, out_ref):
    count = out_ref.shape[0]
    for first in range(0, out_ref.shape[1], depth):
        columns = slice(first, first + depth)
        out_ref[:, columns] = unit_rows(pair_ref[pl.ds(0, count), columns], gain_ref[...])


def fetch_kernel(dims, *refs):
    n, live_count, parts = dims
    sources, targets, places_ref, sems = refs[:n], refs[n + 1 : 2 * n + 1], refs[2 * n + 1], refs[2 * n + 2]
    copies = [pltpu.make_async_copy(s, t, sems.at[i]) for i, (s, t) in enumerate(zip(sources, targets))]
    for copy in copies:
        copy.start()
    mask_ref = targets[0]
    copies[0].wait()
    share = places_ref.shape[1]
    for s in range(parts):
        first = lax.rem(lax.axis_index("tp") + s, parts) * share
        places_ref[s] = place_matrix(mask_ref, live_count, first, share)
    for copy in copies[1:]:
        copy.wait()


def attend_kernel(dims, *refs):
    members, partial, own_heads, depth, live_count, count, stat_rows, sources = dims
    pairs, units = refs[1 : members + 1], refs[members + 1 : 2 * members + 1]
    asks = refs[2 * members + 1 : 2 * members + 1 + sources]
    outs = refs[2 * members + 1 + sources :]
    factor = depth ** (-0.5)
    power = factor * math.log2(math.e)
    lanes = lax.broadcasted_iota(jnp.int32, (live_count, depth), 1)
    padded = -(-own_heads // 8) * 8
    stats = [jnp.zeros((live_count, depth), jnp.float32)] * sources
    ones = jnp.ones((count, depth), jnp.bfloat16)
    for h in range(own_heads):
        columns = slice(h * depth, (h + 1) * depth)
        for s in range(sources):
            queries = asks[s][:, columns]
            scores = [dot_nt(queries, unit[:, columns]) for unit in units]
            biggest = jnp.max(functools.reduce(jnp.maximum, scores), axis=-1, keepdims=True)
            weights = [jnp.exp2((score - biggest) * power).astype(jnp.bfloat16) for score in scores]
            summed = functools.reduce(
                jnp.add,
                [
                    dot_f32(w, jnp.concatenate([ref[pl.ds(count, count), columns], ones], axis=1))
                    for w, ref in zip(weights, pairs)
                ],
            )
            totals = summed[:, depth:]
            outs[s][pl.ds(h * live_count, live_count), :] = (summed[:, :depth] / totals).astype(jnp.bfloat16)
            stats[s] = jnp.where(lanes == h, biggest, jnp.where(lanes == padded + h, totals, stats[s]))
    if partial:
        blank = jnp.zeros((stat_rows - 3 * own_heads, live_count), jnp.float32)
        for s in range(sources):
            turned = jnp.transpose(stats[s])
            rest = turned[:own_heads] * factor + jnp.log(turned[padded : padded + own_heads])
            pieces = []
            for _ in range(3):
                pieces.append(rest.astype(jnp.bfloat16).astype(jnp.float32))
                rest = rest - pieces[-1]
            stat = jnp.concatenate([*pieces, blank], axis=0)
            outs[s][pl.ds(own_heads * live_count, stat_rows), :] = stat.astype(jnp.bfloat16)


def merge_rows(dims, places, parcels, spread_ref):
    members, groups, own_heads, depth, live_count, stat_rows, _ = dims
    width = own_heads * depth
    position = ring_place(members)
    for b in range(members):
        held = [parcels[a * members + b] for a in range(groups)]
        if groups > 1:
            stats = [ref[pl.ds(own_heads * live_count, stat_rows), :].astype(jnp.float32) for ref in held]
        for h in range(own_heads):
            values = [ref[pl.ds(h * live_count, live_count), :] for ref in held]
            if groups > 1:
                logged = [
                    t[h : h + 1] + t[own_heads + h : own_heads + h + 1] + t[2 * own_heads + h : 2 * own_heads + h + 1]
                    for t in stats
                ]
                biggest = functools.reduce(jnp.maximum, logged)
                shares = [jnp.exp(l - biggest) for l in logged]
                total = functools.reduce(jnp.add, shares)
                spots = [places * (w / total).astype(jnp.bfloat16) for w in shares]
                placed = dot_f32(jnp.concatenate(spots, axis=1), jnp.concatenate(values, axis=0))
            else:
                placed = dot_f32(places, values[0])
            base = hop(position, b, members) * width + h * depth
            spread_ref[:, pl.ds(pl.multiple_of(base, depth), depth)] = placed.astype(jnp.bfloat16)


def merge_kernel(dims, places_ref, weight_ref, *refs):
    members, groups, *_, parts = dims
    sources = members * groups
    parcels, sends, spread_ref = refs[:sources], refs[sources:-1], refs[-1]
    share = places_ref.shape[1]
    places = jnp.concatenate([places_ref[s] for s in range(1, parts)], axis=0)
    merge_rows(dims, places, parcels, spread_ref)
    for s, send in enumerate(sends):
        project(spread_ref[pl.ds(s * share, share), :], weight_ref, send)


def project(rows, weight_ref, out_ref):
    features = weight_ref.shape[1]
    tile = 512 if features % 512 == 0 else features
    for first in range(0, features, tile):
        columns = pl.ds(first, tile)
        out_ref[:, columns] = dot_f32(rows, weight_ref[:, columns]).astype(out_ref.dtype)


def own_kernel(dims, after_ref, places_ref, weight_ref, input_ref, gate_ref, *refs):
    parcels, out_ref, spread_ref = refs[:-2], refs[-2], refs[-1]
    merge_rows(dims, places_ref[0], parcels, spread_ref)
    features = weight_ref.shape[1]
    tile = 512 if features % 512 == 0 else features
    for first in range(0, features, tile):
        columns = pl.ds(first, tile)
        product = dot_f32(spread_ref[...], weight_ref[:, columns])
        out_ref[:, columns] = input_ref[:, columns].astype(jnp.float32) + gate_ref[:, columns] * product


def tail_kernel(parts, mask_ref, own_ref, *refs):
    arrived = refs[: parts - 1]
    cached_ref, gate_ref, shift_ref, scale_ref, patch_ref, block_ref, kept_ref, given_ref = refs[parts - 1 :]
    others = functools.reduce(jnp.add, [ref[...].astype(jnp.float32) for ref in arrived])
    mixed = own_ref[...] + gate_ref[...] * others
    share = mixed.shape[0]
    count = mask_ref.shape[1]
    first = lax.axis_index("tp") * share
    rows = lax.broadcasted_iota(jnp.int32, (share, count), 0) + first
    cols = lax.broadcasted_iota(jnp.int32, (share, count), 1)
    replayed = jnp.where((cols == rows) & (jnp.broadcast_to(mask_ref[...], rows.shape) == 1), 1.0, 0.0)
    replayed = jnp.sum(replayed, axis=-1, keepdims=True) > 0.5
    block = jnp.where(replayed, cached_ref[...].astype(jnp.float32), mixed).astype(jnp.bfloat16)
    block_ref[...] = block
    lifted = block.astype(jnp.float32)
    centred = lifted - jnp.mean(lifted, axis=-1, keepdims=True)
    spread = jnp.mean(centred * centred, axis=-1, keepdims=True)
    normed = centred * lax.rsqrt(spread + 1e-06) * (1.0 + scale_ref[...]) + shift_ref[...]
    branch = dot_nt(patch_ref[...], normed.astype(jnp.bfloat16))
    half = branch.shape[0] // 2
    first_side = lax.axis_index("cfg") == 0
    kept_ref[...] = jnp.where(first_side, branch[:half], branch[half:])
    given_ref[...] = jnp.where(first_side, branch[half:], branch[:half])


def store_kernel(block_ref, out_hbm, sem):
    copy = pltpu.make_async_copy(block_ref, out_hbm, sem)
    copy.start()
    copy.wait()


def guide_kernel(kept_ref, partner_ref, out_ref):
    first_side = lax.axis_index("cfg") == 0
    cond = jnp.where(first_side, kept_ref[...], partner_ref[...])
    uncond = jnp.where(first_side, partner_ref[...], kept_ref[...])
    out_ref[...] = uncond + guidance_scale * (cond - uncond)


def shards(
    query_proj,
    key_proj,
    value_proj,
    query_gain,
    key_gain,
    block_input,
    cached_out,
    replay_mask,
    branch_gate,
    attn_weight,
    final_shift,
    final_scale,
    patch_weight,
):
    _, count, width = query_proj.shape
    depth = query_gain.shape[0]
    heads = width // depth
    features = attn_weight.shape[1]
    channels = patch_weight.shape[1]
    live_count = count // 2
    ring = lax.axis_size("ctx")
    parts = lax.axis_size("tp")
    share = count // parts
    members = math.gcd(heads, ring)
    groups = ring // members
    own_heads = heads // members
    own_width = own_heads * depth
    partial = groups > 1
    stat_rows = -(-3 * own_heads // 16) * 16

    def route(a, b, back):
        pairs = []
        for g in range(groups):
            for p in range(members):
                other = hop(g, a, groups) * members + hop(p, b, members)
                pairs.append((other, g * members + p) if back else (g * members + p, other))
        return pairs

    def call(kernel, inputs, outs, in_specs=None, out_specs=None, scratch=(), limit=24, cost=None):
        return pl.pallas_call(
            kernel,
            out_shape=outs,
            in_specs=in_specs or [VMEM] * len(inputs),
            out_specs=out_specs or [VMEM] * len(outs),
            scratch_shapes=scratch,
            compiler_params=pltpu.CompilerParams(vmem_limit_bytes=limit << 20),
            cost_estimate=cost,
        )(*inputs)

    bf16, f32 = jnp.bfloat16, jnp.float32
    shaped = jax.ShapeDtypeStruct
    pair_shape = shaped((2 * count, own_width), bf16)
    pairs = call(
        functools.partial(split_kernel, (members, own_width, depth)),
        (in_hbm(key_proj[0]), in_hbm(value_proj[0])),
        [pair_shape] * members,
        in_specs=[HBM] * 2,
        scratch=[pltpu.SemaphoreType.DMA((2, members))],
        limit=8,
    )
    pairs = list(pairs)
    pair_order = sorted(range(1, members), key=lambda b: (b != members // 2, b))
    for b in pair_order:
        pairs[b] = lax.ppermute(pairs[b], "ctx", route(0, b, False))
    asks = call(
        functools.partial(ask_kernel, (members, own_heads, depth, live_count)),
        (*map(in_hbm, (replay_mask, query_gain[None], query_proj[0])), pairs[0]),
        [shaped((live_count, own_width), bf16)] * members,
        in_specs=[HBM] * 3 + [VMEM],
        scratch=[
            pltpu.VMEM((1, count), jnp.int32),
            pltpu.VMEM((1, depth), f32),
            pltpu.VMEM((members, count, own_width), bf16),
            pltpu.SemaphoreType.DMA((2,)),
            pltpu.SemaphoreType.DMA((members,)),
        ],
        limit=16,
    )
    far_routes = sorted(((a, b) for a in range(1, groups) for b in range(members)), key=lambda r: (r[0], (1 - r[1] if r[1] < 2 else r[1])))
    far_asks = []
    for a, b in far_routes:
        far_asks.append(lax.ppermute(asks[b], "ctx", route(a, b, False)))
    near_asks = list(asks)
    for b in pair_order:
        near_asks[b] = lax.ppermute(asks[b], "ctx", route(0, b, False))

    wanted = (
        replay_mask,
        key_gain[None],
        attn_weight,
        block_input[0],
        cached_out[0],
        branch_gate,
        final_shift,
        final_scale,
        patch_weight.T,
    )
    fetched = call(
        functools.partial(fetch_kernel, (len(wanted), live_count, parts)),
        (*map(in_hbm, wanted), asks[0]),
        [shaped(w.shape, w.dtype) for w in wanted] + [shaped((parts, share, live_count), bf16)],
        in_specs=[HBM] * len(wanted) + [VMEM],
        scratch=[pltpu.SemaphoreType.DMA((len(wanted),))],
        limit=16,
        cost=pl.CostEstimate(flops=0, transcendentals=0, bytes_accessed=2 * sum(w.size * w.dtype.itemsize for w in wanted)),
    )
    mask, key_gain_here, weight, inputs_here, cached_here, gate, shift, scale, patch, places = fetched

    parcel_rows = own_heads * live_count + (stat_rows if partial else 0)
    parcel_shape = shaped((parcel_rows, depth), bf16)

    units = [
        call(
            functools.partial(unit_kernel, depth),
            (key_gain_here, pair),
            [shaped((count, own_width), bf16)],
            cost=pl.CostEstimate(flops=0, transcendentals=0, bytes_accessed=1 << 18),
        )[0]
        for pair in pairs
    ]

    def attend(after, asks):
        scores = len(asks) * live_count * members * count * own_heads
        return call(
            functools.partial(
                attend_kernel,
                (members, partial, own_heads, depth, live_count, count, stat_rows, len(asks)),
            ),
            (after, *pairs, *units, *asks),
            [parcel_shape] * len(asks),
            cost=pl.CostEstimate(flops=4 * scores * depth, transcendentals=scores, bytes_accessed=1 << 20),
        )

    after, parcels = mask, {}
    for n, ask in enumerate(far_asks):
        (far,) = attend(after, [ask])
        after = far
        parcels[far_routes[n]] = lax.ppermute(far, "ctx", route(*far_routes[n], True))
    if members > 1:
        near = attend(after, [near_asks[b] for b in pair_order])
        after = near[0]
        for n, b in enumerate(pair_order):
            parcels[0, b] = lax.ppermute(near[n], "ctx", route(0, b, True))
    (parcels[0, 0],) = attend(after, near_asks[:1])
    parcels = [parcels[a, b] for a in range(groups) for b in range(members)]

    dims = (members, groups, own_heads, depth, live_count, stat_rows, parts)
    merged = call(
        functools.partial(merge_kernel, dims),
        (places, weight, *parcels),
        [shaped((share, features), bf16)] * (parts - 1),
        scratch=[pltpu.VMEM(((parts - 1) * share, width), bf16)],
    )
    arrived = [
        lax.ppermute(merged[s - 1], "tp", [(i, (i + s) % parts) for i in range(parts)]) for s in range(1, parts)
    ]
    (own,) = call(
        functools.partial(own_kernel, dims),
        (merged[0], places, weight, inputs_here, gate, *parcels),
        [shaped((share, features), f32)],
        scratch=[pltpu.VMEM((share, width), bf16)],
        cost=pl.CostEstimate(flops=2 * share * width * features, transcendentals=0, bytes_accessed=1 << 20),
    )

    half = channels // 2
    block_out, kept, given = call(
        functools.partial(tail_kernel, parts),
        (mask, own, *arrived, cached_here, gate, shift, scale, patch),
        [shaped((share, features), bf16), shaped((half, share), f32), shaped((half, share), f32)],
    )
    partner = lax.ppermute(given, "cfg", [(0, 1), (1, 0)])
    (block_out,) = call(
        store_kernel,
        (block_out,),
        [shaped((share, features), bf16)],
        out_specs=[HBM],
        scratch=[pltpu.SemaphoreType.DMA(())],
        limit=4,
    )
    (velocity,) = call(guide_kernel, (kept, partner), [shaped((half, share), f32)], limit=4)
    return (block_out[None], velocity.T)


def solution(mesh):
    in_specs = (
        P("cfg", "ctx", "tp"),
        P("cfg", "ctx", "tp"),
        P("cfg", "ctx", "tp"),
        P(),
        P(),
        P("cfg", ("ctx", "tp"), None),
        P("cfg", ("ctx", "tp"), None),
        P("cfg", "ctx"),
        P("cfg", None),
        P("tp", None),
        P("cfg", None),
        P("cfg", None),
        P(),
    )
    out_specs = (P("cfg", ("ctx", "tp"), None), P(("ctx", "tp"), "cfg"))
    return jax.shard_map(shards, mesh=mesh, in_specs=in_specs, out_specs=out_specs, check_vma=False)
```
